128 devices in a mesh: gx: 16 (over z, y), gy: 8 (over x, core).
Axes of the slice: x: 4, y: 4, z: 4, core: 2. Of those that a mesh axis runs over, the one named last changes fastest.
Arguments:
- atm_state: float32 [2, 72, 1024, 1024], P(None, None, 'gx', 'gy'), may hold values from -6 to 6
- ocean_state: float32 [2, 60, 1024, 1024], P(None, None, 'gx', 'gy'), may hold values from -6 to 6
- land_mask: int32 [1024, 1024], P('gx', 'gy'), may hold values 0 or 1
- elem_op: float32 [16, 16], replicated, may hold values from -1.5 to 1.5
- column_mix: float32 [72, 72], replicated, may hold values from -0.75 to 0.75
- kappa: float32 [2, 60], replicated, may hold values from 0.03 to 0.2
- remap_weight: bfloat16 [1024, 8, 4, 128, 128], P('gx', 'gy'), may hold values from -0.5 to 0.5
- intersection: int32 [1024, 8, 4], replicated, may hold values from 0 to 8191, as said below
Outputs:
- atm_next: float32 [2, 72, 1024, 1024], P(None, None, 'gx', 'gy')
- ocean_next: float32 [2, 60, 1024, 1024], P(None, None, 'gx', 'gy')
- surface_on_atm: float32 [2, 1024, 1024], P(None, 'gx', 'gy')
The draws below stay inside these ranges and needn't reach their ends.
Inputs may be any that keep to these rules, and one draw needn't show every extreme that they name: `intersection`: among the 256 entries of the atmosphere points of one device (rows of one tile along the first dimension, one column block), at most 5 name blocks of any one ocean tile d = o // 64; in every draw some tile receives exactly 5 from every device.
All inputs are finite; a program needn't handle non-finite values. No bound on the sum of `land_mask` on one device may be relied on, other than what follows from the above.
Results may differ from the reference program's by a relative error of at most 0.0032.
Values may be sent and summed in bfloat16 or wider, within the bound.
No kernel may reach another device: no remote copies, remote signals or barrier semaphores. Data moves between devices by JAX's collectives and lax.ppermute only.
A program may use at most 192 MiB of HBM per device.

```python
import math
import jax
import jax.numpy as jnp
from jax import lax

LEV = 72
LO = 60
AX = 64
AY = 128
OX = 64
OY = 128
TOP = 4
OSUB = 2
TILES_X = 16
TILES_Y = 8
TILES = 128
CAP = 5
NAX = 1024
NAY = 1024
ONX = 1024
ONY = 1024


def draw_intersection(key, part):
    devices = TILES_X * TILES_Y
    entries = AX * TOP
    slot_count = devices * CAP
    favored = jax.random.randint(jax.random.fold_in(key, 11), (), 0, devices)
    slot_ids = jnp.arange(slot_count, dtype=jnp.int32)
    owners = slot_ids // CAP

    def one_source(source_key):
        subkeys = jax.random.split(source_key, 3)
        shuffled = jax.random.permutation(subkeys[0], slot_count)
        position = jnp.argsort(shuffled).astype(jnp.int32)
        ranking = jnp.where(owners == favored, slot_ids % CAP - CAP, position)
        sorted_slots = jnp.argsort(ranking, stable=True).astype(jnp.int32)
        chosen = sorted_slots[:entries]
        chosen = chosen[jax.random.permutation(subkeys[1], entries)]
        local_row = jax.random.randint(subkeys[2], (entries,), 0, OX)
        return chosen // CAP * OX + local_row
    source_keys = jax.random.split(jax.random.fold_in(key, 12), devices)
    flat_ids = jax.vmap(one_source)(source_keys)
    arranged = jnp.transpose(flat_ids.reshape(TILES_X, TILES_Y, AX, TOP), (0, 2, 1, 3))
    return arranged.reshape(TILES_X * AX, TILES_Y, TOP).astype(jnp.int32)


def set_ends(values, stream_key, smallest, largest):
    longest = values.shape.index(max(values.shape))
    spots = []
    for shift in (0, 1):
        where = [jax.random.randint(jax.random.fold_in(stream_key, axis), (), 0, length) for axis, length in enumerate(values.shape)]
        where[longest] = (where[longest] + shift) % values.shape[longest]
        spots.append(tuple(where))
    return values.at[spots[0]].set(smallest).at[spots[1]].set(largest)


def block_levels(stream_key, shape, pieces, low, top_value):
    factor_of, own = 1.0, jax.random.fold_in(stream_key, 6)
    for axis_at, blocks in pieces:
        steps = jnp.exp(jax.random.uniform(jax.random.fold_in(own, axis_at), (blocks,), jnp.float32, low / len(pieces), top_value / len(pieces)))
        factor_of = factor_of * jnp.repeat(steps, shape[axis_at] // blocks).reshape([-1 if axis == axis_at else 1 for axis in range(len(shape))])
    return factor_of


def gaussian(rng, dims, width, reach, cuts=(), held_as=jnp.bfloat16):
    array = width * jax.random.normal(rng, dims, jnp.float32)
    if cuts:
        array = array * block_levels(rng, dims, cuts, -0.22, 0.18)
    return jnp.clip(array, -reach, reach).astype(held_as)


def setup_inputs(seed: int = 0) -> dict:
    arg_keys = jax.random.split(jax.random.key(seed), 9)
    atm_state = gaussian(arg_keys[0], (2, LEV, NAX, NAY), 1.0, 6.0, ((2, 16), (3, 8)), jnp.float32)
    ocean_state = gaussian(arg_keys[1], (2, LO, ONX, ONY), 1.0, 6.0, ((2, 16), (3, 8)), jnp.float32)
    land_mask = set_ends((jax.random.randint(arg_keys[2], (ONX, ONY), 0, 4) < 3).astype(jnp.int32), jax.random.fold_in(arg_keys[2], 1), 0, 1)
    elem_op = gaussian(arg_keys[3], (16, 16), 16 ** -0.5, 1.5, (), jnp.float32)
    column_mix = gaussian(arg_keys[4], (LEV, LEV), LEV ** -0.5, 0.75, (), jnp.float32)
    kappa = jnp.clip(jnp.exp(jax.random.uniform(arg_keys[5], (2, LO), jnp.float32, math.log(0.03), math.log(0.2))), 0.03, 0.2)
    remap_weight = gaussian(arg_keys[6], (NAX, TILES_Y, TOP, OY, AY), AY ** -0.5, 0.5, ((0, 16), (1, 8)))
    intersection = draw_intersection(jax.random.fold_in(arg_keys[8], 71), 0)
    return dict(atm_state=atm_state, ocean_state=ocean_state, land_mask=land_mask, elem_op=elem_op, column_mix=column_mix, kappa=kappa, remap_weight=remap_weight, intersection=intersection)


ELEM_STEP = 0.5
MIX_STEP = 0.5
FLUX_GAIN = 0.25


def element_step(fields, elem_op, column_mix):
    variables, levels, row_count, col_count = fields.shape
    blocked = fields.reshape(variables, levels, row_count // 4, 4, col_count // 4, 4)
    kernel = elem_op.reshape(4, 4, 4, 4)
    applied = jnp.einsum("abij,vlxiyj->vlxayb", kernel, blocked, precision=lax.Precision.HIGHEST).reshape(fields.shape)
    stepped = fields + ELEM_STEP * applied
    column_term = jnp.einsum("lm,vmxy->vlxy", column_mix, stepped, precision=lax.Precision.HIGHEST)
    return stepped + MIX_STEP * column_term


def edge_average(padded, along):
    inner_count = padded.shape[along] - 2
    center = lax.slice_in_dim(padded, 1, inner_count + 1, axis=along)
    before = lax.slice_in_dim(padded, 0, inner_count, axis=along)
    after = lax.slice_in_dim(padded, 2, inner_count + 2, axis=along)
    place = (jnp.arange(inner_count) % 4).reshape((inner_count,) + (1,) * (padded.ndim - 1 - along))
    return jnp.where(place == 3, (center + after) * 0.5, jnp.where(place == 0, (center + before) * 0.5, center))


def stiffness_sum(padded):
    return edge_average(edge_average(padded, 2), 3)


def ocean_substep(tracers, wet_mask, kappa):
    eastern = jnp.roll(tracers, -1, axis=2)
    western = jnp.roll(tracers, 1, axis=2)
    mask_east = jnp.roll(wet_mask, -1, axis=0)
    mask_west = jnp.roll(wet_mask, 1, axis=0)
    northern = jnp.concatenate([tracers[:, :, :, 1:], jnp.flip(tracers[:, :, :, -1:], axis=2)], axis=3)
    mask_north = jnp.concatenate([wet_mask[:, 1:], jnp.flip(wet_mask[:, -1:], axis=0)], axis=1)
    southern = jnp.concatenate([jnp.zeros_like(tracers[:, :, :, :1]), tracers[:, :, :, :-1]], axis=3)
    mask_south = jnp.concatenate([jnp.zeros_like(wet_mask[:, :1]), wet_mask[:, :-1]], axis=1)
    laplace_sum = mask_east * (eastern - tracers) + mask_west * (western - tracers)
    laplace_sum = laplace_sum + mask_north * (northern - tracers)
    laplace_sum = laplace_sum + mask_south * (southern - tracers)
    return tracers + wet_mask * (kappa[:, :, None, None] * laplace_sum)


def reference(atm_state, ocean_state, land_mask, elem_op, column_mix, kappa, remap_weight, intersection):
    stepped = element_step(atm_state, elem_op, column_mix)
    padded = jnp.pad(stepped, ((0, 0), (0, 0), (1, 1), (1, 1)), mode="wrap")
    atm_next = stiffness_sum(padded)
    surface = atm_next[:, LEV - 1].astype(jnp.bfloat16)
    surface_rows = jnp.transpose(surface.reshape(2, NAX, TILES_Y, AY), (1, 0, 2, 3))

    def forward(pair):
        weight_row, surface_row = pair
        return jnp.einsum("jtqp,fjp->jtfq", weight_row.astype(jnp.float32), surface_row.astype(jnp.float32), precision=lax.Precision.HIGHEST)

    contrib = lax.map(forward, (remap_weight, surface_rows))
    flat_terms = contrib.reshape(-1, 2, OY)
    ocean_ids = intersection.reshape(-1).astype(jnp.int32)
    totals = jnp.zeros((TILES * OX, 2, OY), jnp.float32).at[ocean_ids].add(flat_terms)
    forcing = jnp.transpose(totals.reshape(TILES_X, TILES_Y, OX, 2, OY), (3, 0, 2, 1, 4)).reshape(2, ONX, ONY)
    wet_mask = land_mask.astype(jnp.float32)
    tracers = ocean_state
    for repeat in range(OSUB):
        tracers = ocean_substep(tracers, wet_mask, kappa)
    surface_level = tracers[:, 0] + wet_mask * (FLUX_GAIN * forcing)
    ocean_next = tracers.at[:, 0].set(surface_level)
    sea_surface = ocean_next[:, 0].astype(jnp.bfloat16)
    ocean_blocks = jnp.transpose(sea_surface.reshape(2, TILES_X, OX, TILES_Y, OY), (1, 3, 2, 0, 4)).reshape(TILES * OX, 2, OY)
    entry_values = ocean_blocks[ocean_ids].reshape(NAX, TILES_Y, TOP, 2, OY)

    def backward(pair):
        weight_row, value_row = pair
        return jnp.einsum("jtqp,jtfq->fjp", weight_row.astype(jnp.float32), value_row.astype(jnp.float32), precision=lax.Precision.HIGHEST)

    returned = lax.map(backward, (remap_weight, entry_values))
    surface_on_atm = jnp.transpose(returned, (1, 0, 2, 3)).reshape(2, NAX, NAY)
    return atm_next, ocean_next, surface_on_atm
```

```python
import jax
import jax.numpy as jnp
from jax import lax
from jax.experimental import pallas as pl
from jax.experimental.pallas import tpu as pltpu
from jax.sharding import PartitionSpec as P

F32, BF16 = jnp.float32, jnp.bfloat16
LEV, LO, NR, NC = 72, 60, 64, 128
AT, O1, O2, MK, PAY = 0, 144, 272, 400, 416
OL = 2 * LO
TOP, CAP, TILES = 4, 5, 128
ENT = NR * TOP
SLOTS = TILES * CAP * 2
VM = 60 * 1024 * 1024


def iota(shape, dim):
    return lax.broadcasted_iota(jnp.int32, shape, dim)


def dot(a, b):
    return jnp.dot(a, b, preferred_element_type=F32)


def params(**more):
    return pltpu.CompilerParams(vmem_limit_bytes=VM, **more)


def whole(shape):
    return pl.BlockSpec(shape, lambda *_: (0,) * len(shape))


def mask_rows(first, second):
    place = iota((16, NC), 0)
    return jnp.where(place == 0, first, jnp.where(place == 1, second, 0.0)).astype(BF16)


def atm_kernel(x_ref, oa_ref, ob_ref, ma_ref, mb_ref, mix_ref, elem_ref, z_ref, sn_ref, sp_ref, zc_ref, b_ref):
    step = pl.program_id(0)

    @pl.when(step == 0)
    def _():
        row = iota((512, 16), 0)
        spread_in = (iota((512, 16), 1) == (row // 128) * 4 + row % 4).astype(BF16)
        col = iota((16, 512), 1)
        spread_out = (iota((16, 512), 0) == (col // 128) * 4 + col % 4).astype(BF16)
        elem = (0.5 * elem_ref[...]).astype(BF16)
        half = lax.dot_general(spread_in, elem, (((1,), (1,)), ((), ())), preferred_element_type=F32)
        full = dot(half.astype(BF16), spread_out)
        same = (iota((512, 512), 0) % 128) // 4 == (iota((512, 512), 1) % 128) // 4
        b_ref[...] = jnp.where(same, full, 0.0).astype(BF16)
        zc_ref[...] = jnp.zeros_like(zc_ref)
        for ref, o_ref, m_ref, at in ((sp_ref, oa_ref, ma_ref, 0), (sn_ref, ob_ref, mb_ref, 6)):
            ref[...] = jnp.zeros_like(ref)
            flat = o_ref.reshape(OL * 8, NC)
            m = m_ref[...].astype(F32)
            for k, base in ((0, O1), (1, O2)):
                u = flat[pl.ds(at + k, OL, stride=8), :] * m[at + k : at + k + 1]
                ref[base : base + 128, :] = jnp.concatenate([u, jnp.zeros((8, NC), F32)], 0).astype(BF16)
            ref[MK:PAY, :] = mask_rows(m[at : at + 1], m[at + 1 : at + 2])

    mix = (0.5 * mix_ref[...]).astype(BF16)
    flat = x_ref.reshape(2 * LEV * 8, NC)
    ys = []
    for big in range(2):
        for f in range(2):
            x = jnp.concatenate([flat[pl.ds(f * LEV * 8 + big * 4 + i, LEV, stride=8), :] for i in range(4)], 1)
            ys.append(x + dot(mix, x.astype(BF16)))
    y = jnp.concatenate(ys, 0)
    z = y + dot(y.astype(BF16), b_ref[...])
    out = z_ref.reshape(2 * LEV * 8, NC)
    lane = iota((2 * LEV, NC), 1)
    left, right = zc_ref[0], zc_ref[1]
    for big in range(2):
        for i in range(4):
            r = big * 4 + i
            rows = []
            for f in range(2):
                at = (big * 2 + f) * LEV
                piece = z[at : at + LEV, i * 128 : (i + 1) * 128]
                out[pl.ds(f * LEV * 8 + r, LEV, stride=8), :] = piece
                rows.append(piece)
            both = jnp.concatenate(rows, 0)
            here = step * 8 + r
            turned = pltpu.roll(both, here, 1)
            left = jnp.where(lane == here, turned, left)
            right = jnp.where(lane == (here + 127) % 128, turned, right)
            if r == 0:

                @pl.when(step == 0)
                def _():
                    sp_ref[AT:O1, :] = both.astype(BF16)

            if r == 7:

                @pl.when(step == 7)
                def _():
                    sn_ref[AT:O1, :] = both.astype(BF16)

    zc_ref[0] = left
    zc_ref[1] = right


def ocean_cols_kernel(o_ref, m_ref, c_ref):
    step = pl.program_id(0)

    @pl.when(step == 0)
    def _():
        c_ref[...] = jnp.zeros_like(c_ref)

    flat = o_ref.reshape(OL * 8, NC)
    m = m_ref[...].astype(F32)
    lane = iota((OL, NC), 1)
    acc = [c_ref[k, 0:OL] for k in range(4)]
    for r in range(8):
        here = step * 8 + r
        u = pltpu.roll(flat[pl.ds(r, OL, stride=8), :] * m[r : r + 1], here, 1)
        for k, shift in enumerate((0, 1, 126, 127)):
            acc[k] = jnp.where(lane == (here + shift) % 128, u, acc[k])
    for k in range(4):
        c_ref[k, 0:OL] = acc[k]


def cols_kernel(zc_ref, oc_ref, m_ref, rp_ref, rn_ref, ss_ref, sn_ref):
    lane = iota((144, NC), 1)
    place = lane % 4
    rp_at, rn_at = rp_ref[AT:O1, :].astype(F32), rn_ref[AT:O1, :].astype(F32)
    before, after = rp_ref[O2:MK, :].astype(F32), rn_ref[O1:O2, :].astype(F32)
    olane = iota((128, NC), 1)
    row = iota((64, NC), 0)
    m_before, m_after = rp_ref[MK:PAY, :].astype(F32)[1:2], rn_ref[MK:PAY, :].astype(F32)[0:1]
    tail = jnp.where(row == 0, m_before, jnp.where(row == 1, m_after, 0.0))
    m_t = jnp.transpose(jnp.concatenate([m_ref[...].astype(F32), tail], 0))
    for ref, c_at, ocs in ((ss_ref, 0, (0, 1)), (sn_ref, 127, (126, 127))):
        z = zc_ref[0] if c_at == 0 else pltpu.roll(zc_ref[1], 1, 1)
        nxt = jnp.where(lane == 63, rn_at[:, c_at : c_at + 1], pltpu.roll(z, 127, 1))
        prv = jnp.where(lane == 0, rp_at[:, c_at : c_at + 1], pltpu.roll(z, 1, 1))
        z = jnp.where(place == 3, (z + nxt) * 0.5, jnp.where(place == 0, (z + prv) * 0.5, z))
        ref[AT:O1, :] = z.astype(BF16)
        for k, c in enumerate(ocs):
            source = c if c < 2 else c - 124
            turned = pltpu.roll(oc_ref[source], (128 - c) % 128, 1) if c else oc_ref[source]
            u = jnp.where(
                olane < 64,
                turned,
                jnp.where(olane == 64, before[:, c : c + 1], jnp.where(olane == 65, after[:, c : c + 1], 0.0)),
            )
            base = (O1, O2)[k]
            ref[base : base + 128, :] = u.astype(BF16)
        ref[MK:PAY, :] = mask_rows(m_t[ocs[0] : ocs[0] + 1], m_t[ocs[1] : ocs[1] + 1])


def averaged(z, nxt, prv, place):
    return jnp.where(place == 3, (z + nxt) * 0.5, jnp.where(place == 0, (z + prv) * 0.5, z))


def stiffness(z, h_prev, h_next, c_south, c_north):
    row, lane = iota((NR, NC), 0), iota((NR, NC), 1)
    nxt = jnp.where(row == NR - 1, h_next, pltpu.roll(z, NR - 1, 0))
    prv = jnp.where(row == 0, h_prev, pltpu.roll(z, 1, 0))
    z = averaged(z, nxt, prv, row % 4)
    nxt = jnp.where(lane == NC - 1, c_north, pltpu.roll(z, NC - 1, 1))
    prv = jnp.where(lane == 0, c_south, pltpu.roll(z, 1, 1))
    return averaged(z, nxt, prv, lane % 4)


def surface_kernel(z_ref, rp_ref, rn_ref, cs_ref, cn_ref, s_ref):
    rp, rn = rp_ref[AT:O1, :].astype(F32), rn_ref[AT:O1, :].astype(F32)
    cs, cn = cs_ref[AT:O1, :].astype(F32), cn_ref[AT:O1, :].astype(F32)
    for f in range(2):
        top = f * LEV + LEV - 8
        south = jnp.transpose(cs[top : top + 8])[:NR, 7:8]
        north = jnp.transpose(cn[top : top + 8])[:NR, 7:8]
        last = top + 7
        s = stiffness(z_ref[f, 0], rp[last : last + 1], rn[last : last + 1], south, north)
        s_ref[f] = s.astype(BF16)


def finish_kernel(z_ref, rp_ref, rn_ref, cs_ref, cn_ref, o_ref, h_ref):
    step = pl.program_id(0)

    @pl.when(step == 0)
    def _():
        for k, ref in enumerate((rp_ref, rn_ref, cs_ref, cn_ref)):
            h_ref[k] = ref[AT:O1, :].astype(F32)

    for f in range(2):
        rows = pl.ds(pl.multiple_of(f * LEV + step * 8, 8), 8)
        rp, rn = h_ref[0, rows, :], h_ref[1, rows, :]
        south = jnp.transpose(h_ref[2, rows, :])[:NR]
        north = jnp.transpose(h_ref[3, rows, :])[:NR]
        for l in range(8):
            o_ref[f, l] = stiffness(
                z_ref[f, l], rp[l : l + 1], rn[l : l + 1], south[:, l : l + 1], north[:, l : l + 1]
            )


OB = 4


def ocean_kernel(
    at_ref, k_ref, o_ref, m_ref, kc_ref, sp_ref, sn_ref, ss_ref, st_ref, rp_ref, rn_ref, cs_ref, cn_ref, fo_ref,
    out_ref, row_ref, col_ref, wet_ref, cnt_ref,
):
    step = pl.program_id(0)

    @pl.when(step == 0)
    def _():
        is_top, is_low = at_ref[0] == 7, at_ref[0] == 0
        lane = iota((128, NC), 1)

        def part(ref, base):
            return ref[base : base + 128, :].astype(F32)

        def masks(ref):
            m = ref[MK:PAY, :].astype(F32)
            return m[0:1], m[1:2]

        fr, fc = iota((NC, NC), 0), iota((NC, NC), 1)
        flip = (((fr < 64) & (fc == 63 - fr)) | ((fr == 64) & (fc == 65)) | ((fr == 65) & (fc == 64))).astype(BF16)
        turned = dot(fo_ref[...], flip)
        n0 = jnp.where(is_top, turned[O2:MK], part(cn_ref, O1))
        n1 = jnp.where(is_top, turned[O1:O2], part(cn_ref, O2))
        mc0, mc1 = masks(cn_ref)
        mn0 = jnp.where(is_top, turned[MK + 1 : MK + 2], mc0)
        mn1 = jnp.where(is_top, turned[MK : MK + 1], mc1)
        keep = jnp.where(is_low, 0.0, 1.0)
        s2, s1 = part(cs_ref, O1) * keep, part(cs_ref, O2) * keep
        ms2, ms1 = masks(cs_ref)
        ms2, ms1 = ms2 * keep, ms1 * keep
        um2, um1 = part(rp_ref, O1), part(rp_ref, O2)
        mm2, mm1 = masks(rp_ref)
        u64, u65 = part(rn_ref, O1), part(rn_ref, O2)
        m64, m65 = masks(rn_ref)
        own0, own63 = part(sp_ref, O1), part(sn_ref, O2)
        mo0, mo63 = masks(sp_ref)[0], masks(sn_ref)[1]
        west0, east127 = part(ss_ref, O1), part(st_ref, O2)
        mw0, me127 = masks(ss_ref)[0], masks(st_ref)[1]
        kap = kc_ref[...]

        def along(u, low, high, end):
            where = lane[: u.shape[0]]
            return jnp.where(where == end, high, pltpu.roll(u, 127, 1)) + jnp.where(
                where == 0, low, pltpu.roll(u, 1, 1)
            )

        def advance(u, wet, inner, outer, m_inner, m_outer, low, high, m_low, m_high, end):
            total = inner + outer + along(u, low, high, end)
            m8 = jnp.broadcast_to(wet, (8, NC))
            count = m_inner + m_outer + along(m8, m_low, m_high, end)[0:1]
            return u + kap * (wet * total - count * u)

        def corner(x, at):
            return x[:, at : at + 1]

        row_ref[0] = um1
        row_ref[1] = u64
        row_ref[2] = advance(
            um1, mm1, own0, um2, mo0, mm2, corner(s1, 64), corner(n0, 64), corner(ms1, 64), corner(mn0, 64), 127
        )
        row_ref[3] = advance(
            u64, m64, own63, u65, mo63, m65, corner(s1, 65), corner(n0, 65), corner(ms1, 65), corner(mn0, 65), 127
        )
        west = advance(
            s1, ms1, west0, s2, mw0, ms2, corner(s1, 64), corner(s1, 65), corner(ms1, 64), corner(ms1, 65), 63
        )
        east = advance(
            n0, mn0, east127, n1, me127, mn1, corner(n0, 64), corner(n0, 65), corner(mn0, 64), corner(mn0, 65), 63
        )
        for k, x in enumerate((s1, n0, west, east)):
            col_ref[k] = jnp.transpose(x)[:NR]
        wet = m_ref[...].astype(F32)
        r, c = iota((NR, NC), 0), iota((NR, NC), 1)
        m_north = jnp.transpose(jnp.broadcast_to(mn0, (8, NC)))[:NR, 0:1]
        m_south = jnp.transpose(jnp.broadcast_to(ms1, (8, NC)))[:NR, 0:1]
        count = jnp.where(r == NR - 1, m64, pltpu.roll(wet, NR - 1, 0)) + jnp.where(
            r == 0, mm1, pltpu.roll(wet, 1, 0)
        )
        count = count + jnp.where(c == NC - 1, m_north, pltpu.roll(wet, NC - 1, 1))
        count = count + jnp.where(c == 0, m_south, pltpu.roll(wet, 1, 1))
        wet_ref[...] = wet
        cnt_ref[...] = count

    r, c = iota((NR, NC), 0), iota((NR, NC), 1)
    wet, count = wet_ref[...], cnt_ref[...]
    for f in range(2):
        for l in range(OB):
            level = step * OB + l
            index = f * LO + level
            t = o_ref[f, l]
            kw = k_ref[f, level] * wet
            for sub in range(2):
                u = wet * t
                total = jnp.where(r == NR - 1, row_ref[2 * sub + 1, pl.ds(index, 1), :], pltpu.roll(u, NR - 1, 0))
                total = total + jnp.where(r == 0, row_ref[2 * sub, pl.ds(index, 1), :], pltpu.roll(u, 1, 0))
                north = pltpu.roll(col_ref[2 * sub + 1], 127 - index, 1)
                south = pltpu.roll(col_ref[2 * sub], (128 - index) % 128, 1)
                total = total + jnp.where(c == NC - 1, north, pltpu.roll(u, NC - 1, 1))
                total = total + jnp.where(c == 0, south, pltpu.roll(u, 1, 1))
                t = t + kw * (total - count * t)
            out_ref[f, l] = t


def index_kernel(at_ref, ids_ref, srow_ref, scol_ref, rrow_ref, rcol_ref):
    gx, gy = at_ref[0], at_ref[1]
    own_tile = gx * 8 + gy
    block = ids_ref[:, pl.ds(pl.multiple_of((gx // 2) * 128, 128), 128)]
    block = pltpu.roll(block, (gx % 2) * 64, 1)
    rows = iota((32, 128), 0)
    tile_row, lane = iota((128, 128), 0), iota((128, 128), 1)
    before = (tile_row < lane).astype(BF16)
    ones = jnp.ones((128, 128), BF16)
    earlier = jnp.zeros((128, 128), F32)
    tiles, ranks = [], []
    for t in range(TOP):
        ids = jnp.sum(jnp.where(rows == gy * 4 + t, block, 0), 0, keepdims=True)
        hit = (ids // 64 == tile_row) & (lane < 64)
        hot = hit.astype(BF16)
        rank = dot(hot, before) + earlier
        earlier = earlier + dot(hot, ones)
        ranks.append(jnp.sum(jnp.where(hit, rank, 0.0), 0, keepdims=True))
        tiles.append((ids // 64).astype(F32))
    place = iota((8, 128), 0)
    stack = jnp.zeros((8, 128), F32)
    for t in range(TOP):
        stack = jnp.where(place == t, tiles[t], jnp.where(place == t + 4, ranks[t], stack))
    spread = (iota((128, 512), 1) // 8 == iota((128, 512), 0)).astype(BF16)
    wide = dot(stack.astype(BF16), spread)
    col, row8 = iota((8, 512), 1), iota((8, 512), 0)
    wide = jnp.where(row8 % 4 == (col // 2) % 4, wide * jnp.where(row8 < 4, 10.0, 2.0), 0.0)
    slot = jnp.sum(wide, 0, keepdims=True) + (iota((1, 512), 1) % 2).astype(F32)
    srow_ref[...] = jnp.broadcast_to(slot, (8, 512))
    scol_ref[...] = jnp.transpose(jnp.broadcast_to(slot, (128, 512)))
    halves = (tile_row // 64) == (lane // 64)
    before2 = (halves & (tile_row < lane)).astype(BF16)
    ones2 = halves.astype(BF16)
    r32, c32 = iota((32, 32), 0), iota((32, 32), 1)
    lower = ((r32 // 4 == c32 // 4) & (c32 % 4 < r32 % 4)).astype(BF16)
    sr, sc = iota((160, 160), 0), iota((160, 160), 1)
    pick = (((sr // 10) % 8 == (sc % 32) // 4) & ((sr % 10) // 2 == sc // 32)).astype(BF16)
    side = iota((160, 128), 0) // 80 == iota((160, 128), 1) // 64
    for b in range(8):
        ids = ids_ref[:, b * 128 : (b + 1) * 128]
        hit = ids // 64 == own_tile
        hot = hit.astype(BF16)
        rank = dot(hot, before2) + dot(lower, dot(hot, ones2).astype(BF16))
        value = (ids % 64 + 1).astype(F32)
        stacked = jnp.concatenate([jnp.where(hit & (rank == float(k)), value, 0.0) for k in range(CAP)], 0)
        found = jnp.where(side, dot(pick, stacked.astype(BF16)), 0.0)
        rcol_ref[b * 160 : (b + 1) * 160, :] = dot(found.astype(BF16), ones)
    for b in range(SLOTS // 128):
        turned = jnp.transpose(rcol_ref[b * 128 : (b + 1) * 128, :])
        rrow_ref[:, b * 128 : (b + 1) * 128] = turned[0:8]


def pack_kernel(c_ref, srow_ref, out_ref):
    slot = srow_ref[0:1, :].astype(jnp.int32)
    hot = jnp.where(slot == iota((SLOTS, 512), 0), 1.0, 0.0).astype(BF16)
    out_ref[...] = dot(hot, c_ref[...].astype(BF16)).astype(BF16)


def ocean_surface_kernel(in_ref, rrow_ref, rcol_ref, m_ref, t_ref, out_ref, back_ref):
    row, col = iota((128, SLOTS), 0), iota((128, SLOTS), 1)
    take = (rrow_ref[0:1, :].astype(jnp.int32) - 1 == row % 64) & (col % 2 == row // 64)
    forcing = dot(jnp.where(take, 1.0, 0.0).astype(BF16), in_ref[...])
    wet = 0.25 * m_ref[...].astype(F32)
    news = []
    for f in range(2):
        new = t_ref[f, 0] + wet * forcing[f * 64 : (f + 1) * 64]
        out_ref[f, 0] = new
        news.append(new)
    sea = jnp.concatenate(news, 0).astype(BF16)
    row, col = iota((SLOTS, 128), 0), iota((SLOTS, 128), 1)
    give = (rcol_ref[...].astype(jnp.int32) - 1 == col % 64) & (row % 2 == col // 64)
    back_ref[...] = dot(jnp.where(give, 1.0, 0.0).astype(BF16), sea).astype(BF16)


def entry_kernel(in_ref, scol_ref, out_ref):
    total = jnp.zeros((512, 128), F32)
    slot = scol_ref[...].astype(jnp.int32)
    for b in range(SLOTS // 128):
        hot = jnp.where(slot == iota((512, 128), 1) + b * 128, 1.0, 0.0).astype(BF16)
        total = total + dot(hot, in_ref[b * 128 : (b + 1) * 128, :])
    out_ref[...] = total.astype(BF16)


def shape(dims, dtype=F32):
    return jax.ShapeDtypeStruct(dims, dtype)


def shifted(x, axis, by):
    count = lax.axis_size(axis)
    return lax.ppermute(x, axis, [(i, (i + by) % count) for i in range(count)])


def per_device(atm_state, ocean_state, land_mask, elem_op, column_mix, kappa, remap_weight, intersection):
    gx, gy = lax.axis_index("gx"), lax.axis_index("gy")
    at = jnp.stack([gx, gy]).astype(jnp.int32)
    smem = pl.BlockSpec(memory_space=pltpu.SMEM)
    full = whole((PAY, NC))

    z, send_next, send_prev, z_cols = pl.pallas_call(
        atm_kernel,
        grid=(8,),
        in_specs=[
            pl.BlockSpec((2, LEV, 8, NC), lambda i: (0, 0, i, 0)),
            pl.BlockSpec((2, LO, 8, NC), lambda i: (0, 0, 0, 0)),
            pl.BlockSpec((2, LO, 8, NC), lambda i: (0, 0, 7, 0)),
            pl.BlockSpec((8, NC), lambda i: (0, 0)),
            pl.BlockSpec((8, NC), lambda i: (7, 0)),
            whole((LEV, LEV)),
            whole((16, 16)),
        ],
        out_specs=[pl.BlockSpec((2, LEV, 8, NC), lambda i: (0, 0, i, 0)), full, full, whole((2, 144, NC))],
        out_shape=[shape(atm_state.shape), shape((PAY, NC), BF16), shape((PAY, NC), BF16), shape((2, 144, NC))],
        scratch_shapes=[pltpu.VMEM((512, 512), BF16)],
        compiler_params=params(),
        name="atm",
    )(atm_state, ocean_state, ocean_state, land_mask, land_mask, column_mix, elem_op)

    from_prev = shifted(send_next, "gx", 1)
    from_next = shifted(send_prev, "gx", -1)

    ocean_cols = pl.pallas_call(
        ocean_cols_kernel,
        grid=(8,),
        in_specs=[
            pl.BlockSpec((2, LO, 8, NC), lambda i: (0, 0, i, 0)),
            pl.BlockSpec((8, NC), lambda i: (i, 0)),
        ],
        out_specs=whole((4, 128, NC)),
        out_shape=shape((4, 128, NC)),
        compiler_params=params(),
        cost_estimate=pl.CostEstimate(flops=4000000, bytes_accessed=4200000, transcendentals=0),
        name="ocean_cols",
    )(ocean_state, land_mask)

    send_south, send_north = pl.pallas_call(
        cols_kernel,
        out_shape=[shape((PAY, NC), BF16)] * 2,
        compiler_params=params(),
        name="cols",
    )(z_cols, ocean_cols, land_mask, from_prev, from_next)

    from_south = shifted(send_north, "gy", 1)
    from_north = shifted(send_south, "gy", -1)
    gx_count, gy_count = lax.axis_size("gx"), lax.axis_size("gy")
    top = gy_count - 1
    folded = lax.ppermute(
        send_north, ("gx", "gy"), [(i * gy_count + top, (gx_count - 1 - i) * gy_count + top) for i in range(gx_count)]
    )

    ids = jnp.transpose(intersection, (1, 2, 0)).reshape(32, 1024)
    slot_row, slot_col, recv_row, recv_col = pl.pallas_call(
        index_kernel,
        in_specs=[smem, pl.BlockSpec(memory_space=pltpu.VMEM)],
        out_shape=[shape((8, 512)), shape((512, 128)), shape((8, SLOTS)), shape((SLOTS, 128))],
        compiler_params=params(),
        cost_estimate=pl.CostEstimate(flops=4000000, bytes_accessed=4200000, transcendentals=0),
        name="index",
    )(at, ids)

    surface = pl.pallas_call(
        surface_kernel,
        grid=(1,),
        in_specs=[pl.BlockSpec((2, 1, NR, NC), lambda i: (0, LEV - 1, 0, 0)), full, full, full, full],
        out_specs=whole((2, NR, NC)),
        out_shape=shape((2, NR, NC), BF16),
        compiler_params=params(),
        name="surface",
    )(z, from_prev, from_next, from_south, from_north)

    weights = remap_weight[:, 0]
    products = lax.dot_general(
        weights, surface, (((3,), (2,)), ((0,), (1,))), preferred_element_type=F32
    )
    contrib = jnp.transpose(products, (0, 1, 3, 2)).reshape(2 * ENT, NC)
    outgoing = pl.pallas_call(
        pack_kernel,
        out_shape=shape((SLOTS, NC), BF16),
        compiler_params=params(),
        name="pack",
    )(contrib, slot_row)
    incoming = lax.all_to_all(
        outgoing.reshape(TILES, CAP, 2, NC), ("gx", "gy"), split_axis=0, concat_axis=0, tiled=True
    ).reshape(SLOTS, NC)

    kap_col = jnp.broadcast_to(jnp.pad(kappa.reshape(OL, 1), ((0, 8), (0, 0))), (128, NC))
    ocean_block = pl.BlockSpec((2, OB, NR, NC), lambda i: (0, i, 0, 0))
    ocean_mid = pl.pallas_call(
        ocean_kernel,
        grid=(LO // OB,),
        in_specs=[smem, smem, ocean_block, whole((NR, NC)), whole((128, NC))] + [full] * 9,
        out_specs=ocean_block,
        out_shape=shape(ocean_state.shape),
        scratch_shapes=[
            pltpu.VMEM((4, 128, NC), F32),
            pltpu.VMEM((4, NR, NC), F32),
            pltpu.VMEM((NR, NC), F32),
            pltpu.VMEM((NR, NC), F32),
        ],
        compiler_params=params(),
        cost_estimate=pl.CostEstimate(flops=30000000, bytes_accessed=8000000, transcendentals=0),
        name="ocean",
    )(
        at[1:], kappa, ocean_state, land_mask, kap_col, send_prev, send_next, send_south, send_north,
        from_prev, from_next, from_south, from_north, folded,
    )

    level_zero = pl.BlockSpec((2, 1, NR, NC), lambda i: (0, 0, 0, 0))
    ocean_next, back_out = pl.pallas_call(
        ocean_surface_kernel,
        grid=(1,),
        in_specs=[whole((SLOTS, NC)), whole((8, SLOTS)), whole((SLOTS, 128)), whole((NR, NC)), level_zero],
        out_specs=[level_zero, whole((SLOTS, NC))],
        out_shape=[shape(ocean_state.shape), shape((SLOTS, NC), BF16)],
        input_output_aliases={4: 0},
        compiler_params=params(),
        name="ocean_surface",
    )(incoming, recv_row, recv_col, land_mask, ocean_mid)

    back_in = lax.all_to_all(
        back_out.reshape(TILES, CAP, 2, NC), ("gx", "gy"), split_axis=0, concat_axis=0, tiled=True
    ).reshape(SLOTS, NC)

    atm_block = pl.BlockSpec((2, 8, NR, NC), lambda i: (0, i, 0, 0))
    atm_next = pl.pallas_call(
        finish_kernel,
        grid=(LEV // 8,),
        in_specs=[atm_block, full, full, full, full],
        out_specs=atm_block,
        out_shape=shape(atm_state.shape),
        scratch_shapes=[pltpu.VMEM((4, 144, NC), F32)],
        compiler_params=params(),
        cost_estimate=pl.CostEstimate(flops=20000000, bytes_accessed=9400000, transcendentals=0),
        name="finish",
    )(z, from_prev, from_next, from_south, from_north)

    entries = pl.pallas_call(
        entry_kernel,
        out_shape=shape((2 * ENT, NC), BF16),
        compiler_params=params(),
        name="entries",
    )(back_in, slot_col)
    returned = lax.dot_general(
        weights,
        entries.reshape(NR, TOP, 2, NC),
        (((1, 2), (1, 3)), ((0,), (0,))),
        preferred_element_type=F32,
    )
    return atm_next, ocean_next, jnp.transpose(returned, (2, 0, 1))


def solution(mesh):
    placed = (
        P(None, None, "gx", "gy"),
        P(None, None, "gx", "gy"),
        P("gx", "gy"),
        P(),
        P(),
        P(),
        P("gx", "gy", None, None, None),
        P(),
    )
    return jax.shard_map(
        per_device,
        mesh=mesh,
        in_specs=placed,
        out_specs=(P(None, None, "gx", "gy"), P(None, None, "gx", "gy"), P(None, "gx", "gy")),
        check_vma=False,
    )
```

```python
import jax
import jax.numpy as jnp
from jax import lax
from jax.experimental import pallas as pl
from jax.experimental.pallas import tpu as pltpu
from jax.sharding import PartitionSpec as P

F32, BF16 = jnp.float32, jnp.bfloat16
LEV, LO, NR, NC = 72, 60, 64, 128
AT, O1, O2, MK, PAY = 0, 144, 272, 400, 416
OL = 2 * LO
TOP, CAP, TILES = 4, 5, 128
ENT = NR * TOP
SLOTS = TILES * CAP * 2
MIB = 1024 * 1024


def iota(shape, dim):
    return lax.broadcasted_iota(jnp.int32, shape, dim)


def dot(a, b):
    return jnp.dot(a, b, preferred_element_type=F32)


def params(mib=6):
    return pltpu.CompilerParams(vmem_limit_bytes=mib * MIB)


def whole(shape):
    return pl.BlockSpec(shape, lambda *_: (0,) * len(shape))


def mask_rows(first, second):
    place = iota((16, NC), 0)
    return jnp.where(place == 0, first, jnp.where(place == 1, second, 0.0)).astype(BF16)


def element_rows(x_s, mix, b):
    fields = [jnp.swapaxes(x_s[f], 0, 1) for f in range(2)]
    ys = []
    for big in range(2):
        for f in range(2):
            x = jnp.concatenate([fields[f][big * 4 + k] for k in range(4)], 1)
            ys.append(x + dot(mix, x.astype(BF16)))
    y = jnp.concatenate(ys, 0)
    z = y + dot(y.astype(BF16), b)
    pieces = [[], []]
    for r in range(8):
        for f in range(2):
            at = ((r // 4) * 2 + f) * LEV
            pieces[f].append(z[at : at + LEV, (r % 4) * NC : (r % 4 + 1) * NC])
    return pieces


def store_rows(z_ref, pieces, at):
    for f in range(2):
        z_ref[f, :, pl.ds(at, 8), :] = jnp.swapaxes(jnp.stack(pieces[f], 0), 0, 1)


def atm_rim_kernel(
    x_hbm, o_hbm, m_hbm, mix_hbm, elem_hbm, z_hbm, sn_ref, sp_ref, b_ref, x_s, o_s, m_s, mix_s, elem_s, z_s, sems
):
    sources = (elem_hbm, mix_hbm, x_hbm.at[:, :, pl.ds(0, 8), :], x_hbm.at[:, :, pl.ds(NR - 8, 8), :], m_hbm) + tuple(
        o_hbm.at[:, :, pl.ds(at, 8), :] for at in (0, NR - 8)
    )
    targets = (elem_s, mix_s, x_s.at[0], x_s.at[1], m_s, o_s.at[0], o_s.at[1])
    copies = [pltpu.make_async_copy(a, b, sems.at[k]) for k, (a, b) in enumerate(zip(sources, targets))]
    outs = [
        pltpu.make_async_copy(z_s.at[k], z_hbm.at[:, :, pl.ds(k * (NR - 8), 8), :], sems.at[7 + k]) for k in range(2)
    ]
    for copy in copies:
        copy.start()
    copies[0].wait()
    row = iota((512, 16), 0)
    spread_in = (iota((512, 16), 1) == (row // 128) * 4 + row % 4).astype(BF16)
    col = iota((16, 512), 1)
    spread_out = (iota((16, 512), 0) == (col // 128) * 4 + col % 4).astype(BF16)
    elem = (0.5 * elem_s[...]).astype(BF16)
    half = lax.dot_general(spread_in, elem, (((1,), (1,)), ((), ())), preferred_element_type=F32)
    spread = dot(half.astype(BF16), spread_out)
    same = (iota((512, 512), 0) % 128) // 4 == (iota((512, 512), 1) % 128) // 4
    b = jnp.where(same, spread, 0.0).astype(BF16)
    b_ref[...] = b
    copies[1].wait()
    mix = (0.5 * mix_s[...]).astype(BF16)
    for k, ref in ((0, sp_ref), (1, sn_ref)):
        copies[2 + k].wait()
        pieces = element_rows(x_s.at[k], mix, b)
        store_rows(z_s.at[k], pieces, 0)
        outs[k].start()
        ref[AT:O1, :] = jnp.concatenate([pieces[f][7 * k] for f in range(2)], 0).astype(BF16)
    for k in (4, 5, 6):
        copies[k].wait()
    m = m_s[...].astype(F32)
    for ref, k, first in ((sp_ref, 0, 0), (sn_ref, 1, 6)):
        rows = jnp.swapaxes(o_s[k].reshape(OL, 8, NC), 0, 1)
        at = k * (NR - 8) + first
        for j, base in ((0, O1), (1, O2)):
            u = rows[first + j] * m[at + j : at + j + 1]
            ref[base : base + 128, :] = jnp.concatenate([u, jnp.zeros((8, NC), F32)], 0).astype(BF16)
        ref[MK:PAY, :] = mask_rows(m[at : at + 1], m[at + 1 : at + 2])
    for copy in outs:
        copy.wait()


INNER = NR // 8 - 2


def pick_columns(columns):
    k, at = iota((8 * len(columns), 8 * NC), 0), iota((8 * len(columns), 8 * NC), 1)
    wanted = jnp.zeros_like(k)
    for j, c in enumerate(columns):
        wanted = jnp.where(k // 8 == j, c, wanted)
    return ((at // NC == k % 8) & (at % NC == wanted)).astype(BF16)


def take_columns(pick, tiles):
    side = jnp.concatenate([t.astype(BF16) for t in tiles], 1)
    got = lax.dot_general(pick, side, (((1,), (1,)), ((), ())), preferred_element_type=F32)
    return jnp.concatenate([got, jnp.zeros_like(got)], 1)


def inner_kernel(
    x_hbm, mix_hbm, o_hbm, b_ref, m_ref, rim_hbm, w_hbm, z_hbm, top_ref, zc_ref, oc_ref, w_ref,
    x_s, z_s, o_s, mix_s, sems, rest,
):
    mix_copy = pltpu.make_async_copy(mix_hbm, mix_s, rest.at[0])
    ocean_copy = pltpu.make_async_copy(o_hbm, o_s, rest.at[1])
    rims = [
        pltpu.make_async_copy(
            rim_hbm.at[:, :, pl.ds(at, 8), :], z_s.at[:, :, pl.ds(at, 8), :], rest.at[2 + k]
        )
        for k, at in enumerate((0, NR - 8))
    ]

    def chunk(i):
        return pltpu.make_async_copy(x_hbm.at[:, :, pl.ds(i * 8 + 8, 8), :], x_s.at[i], sems.at[i])

    def leave(i):
        rows = pl.ds(pl.multiple_of(i * 8 + 8, 8), 8)
        return pltpu.make_async_copy(z_s.at[:, :, rows, :], z_hbm.at[:, :, rows, :], sems.at[INNER + i])

    mix_copy.start()
    for i in range(INNER):
        chunk(i).start()
    for copy in rims:
        copy.start()
    ocean_copy.start()
    weight_copy = pltpu.make_async_copy(w_hbm, w_ref, rest.at[4])
    weight_copy.start()
    mix_copy.wait()
    mix = (0.5 * mix_s[...]).astype(BF16)

    def step(i, carry):
        chunk(i).wait()
        store_rows(z_s, element_rows(x_s.at[i], mix, b_ref[...]), pl.multiple_of(i * 8 + 8, 8))
        leave(i).start()
        return carry

    lax.fori_loop(0, INNER, step, 0)
    for copy in rims:
        copy.wait()
    pick = pick_columns((0, NC - 1))

    def atm(i, carry):
        for f in range(2):
            got = take_columns(pick, [z_s[f, i * 8 + l] for l in range(8)])
            at = pl.multiple_of(f * LEV + i * 8, 8)
            for k in range(2):
                zc_ref[k, pl.ds(at, 8), :] = got[k * 8 : k * 8 + 8]
        return carry

    lax.fori_loop(0, LEV // 8, atm, 0, unroll=3)
    for f in range(2):
        top_ref[f] = z_s[f, LEV - 1]
    ocean_copy.wait()
    wet = m_ref[...].astype(F32)
    pick = pick_columns((0, 1, NC - 2, NC - 1))

    def ocean(i, carry):
        tiles = [i * 8 + l for l in range(8)]
        got = take_columns(pick, [wet * o_s[t // LO, t % LO] for t in tiles])
        for k in range(4):
            oc_ref[k, pl.ds(pl.multiple_of(i * 8, 8), 8), :] = got[k * 8 : k * 8 + 8]
        return carry

    lax.fori_loop(0, OL // 8, ocean, 0, unroll=3)
    oc_ref[:, OL:, :] = jnp.zeros((4, 8, NC), F32)
    for i in range(INNER):
        leave(i).wait()
    weight_copy.wait()


def cols_kernel(zc_ref, oc_ref, m_ref, rp_ref, rn_ref, ss_ref, sn_ref):
    lane = iota((144, NC), 1)
    place = lane % 4
    rp_at, rn_at = rp_ref[AT:O1, :].astype(F32), rn_ref[AT:O1, :].astype(F32)
    before, after = rp_ref[O2:MK, :].astype(F32), rn_ref[O1:O2, :].astype(F32)
    olane = iota((128, NC), 1)
    row = iota((64, NC), 0)
    m_before, m_after = rp_ref[MK:PAY, :].astype(F32)[1:2], rn_ref[MK:PAY, :].astype(F32)[0:1]
    tail = jnp.where(row == 0, m_before, jnp.where(row == 1, m_after, 0.0))
    m_t = jnp.transpose(jnp.concatenate([m_ref[...].astype(F32), tail], 0))
    for ref, c_at, ocs in ((ss_ref, 0, (0, 1)), (sn_ref, 127, (126, 127))):
        z = zc_ref[0 if c_at == 0 else 1]
        nxt = jnp.where(lane == 63, rn_at[:, c_at : c_at + 1], pltpu.roll(z, 127, 1))
        prv = jnp.where(lane == 0, rp_at[:, c_at : c_at + 1], pltpu.roll(z, 1, 1))
        z = jnp.where(place == 3, (z + nxt) * 0.5, jnp.where(place == 0, (z + prv) * 0.5, z))
        ref[AT:O1, :] = z.astype(BF16)
        for k, c in enumerate(ocs):
            source = c if c < 2 else c - 124
            u = jnp.where(
                olane < 64,
                oc_ref[source],
                jnp.where(olane == 64, before[:, c : c + 1], jnp.where(olane == 65, after[:, c : c + 1], 0.0)),
            )
            base = (O1, O2)[k]
            ref[base : base + 128, :] = u.astype(BF16)
        ref[MK:PAY, :] = mask_rows(m_t[ocs[0] : ocs[0] + 1], m_t[ocs[1] : ocs[1] + 1])


def averaged(z, nxt, prv, place):
    return jnp.where(place == 3, (z + nxt) * 0.5, jnp.where(place == 0, (z + prv) * 0.5, z))


def stiffness(z, h_prev, h_next, c_south, c_north):
    row, lane = iota((NR, NC), 0), iota((NR, NC), 1)
    nxt = jnp.where(row == NR - 1, h_next, pltpu.roll(z, NR - 1, 0))
    prv = jnp.where(row == 0, h_prev, pltpu.roll(z, 1, 0))
    z = averaged(z, nxt, prv, row % 4)
    nxt = jnp.where(lane == NC - 1, c_north, pltpu.roll(z, NC - 1, 1))
    prv = jnp.where(lane == 0, c_south, pltpu.roll(z, 1, 1))
    return averaged(z, nxt, prv, lane % 4)


def surface_kernel(z_ref, rp_ref, rn_ref, cs_ref, cn_ref, s_ref):
    rp, rn = rp_ref[AT:O1, :].astype(F32), rn_ref[AT:O1, :].astype(F32)
    cs, cn = cs_ref[AT:O1, :].astype(F32), cn_ref[AT:O1, :].astype(F32)
    for f in range(2):
        top = f * LEV + LEV - 8
        south = jnp.transpose(cs[top : top + 8])[:NR, 7:8]
        north = jnp.transpose(cn[top : top + 8])[:NR, 7:8]
        last = top + 7
        s = stiffness(z_ref[f], rp[last : last + 1], rn[last : last + 1], south, north)
        s_ref[f] = s.astype(BF16)


def edge_spread(tiles, scale):
    k, c = iota((2 * tiles, tiles * NC), 0), iota((2 * tiles, tiles * NC), 1)
    mine = k % tiles == c // NC
    end = c % NC == jnp.where(k < tiles, 0, NC - 1)
    return jnp.where(mine & end, scale, 0.0).astype(BF16)


def add_ends(x, first, last):
    row = iota((8, NC), 0)
    return jnp.concatenate(
        [
            x[0:8] + jnp.where(row == 0, first, 0.0),
            x[8 : NR - 8],
            x[NR - 8 :] + jnp.where(row == 7, last, 0.0),
        ],
        0,
    )


def column_halo(columns, spread):
    return lax.dot_general(columns, spread, (((0,), (0,)), ((), ())), preferred_element_type=F32)[:NR]


FB = 8


def finish_kernel(z_hbm, rp_ref, rn_ref, cs_ref, cn_ref, o_hbm, z_s, o_s, h_ref, sems):
    def enter(i):
        return pltpu.make_async_copy(z_hbm.at[:, pl.ds(i * FB, FB)], z_s.at[i], sems.at[LEV // FB + i])

    for i in range(LEV // FB):
        enter(i).start()
    for k, ref in enumerate((rp_ref, rn_ref, cs_ref, cn_ref)):
        h_ref[k] = ref[AT:O1, :].astype(F32)
    spread = edge_spread(2 * FB, 0.5)
    row, lane = iota((NR, NC), 0), iota((NR, NC), 1)

    def weights(place, at, end):
        low = jnp.where((place == 0) & (at != 0), 0.5, 0.0)
        high = jnp.where((place == 3) & (at != end), 0.5, 0.0)
        return jnp.where((place == 0) | (place == 3), 0.5, 1.0), low, high

    own_r, low_r, high_r = weights(row % 4, row, NR - 1)
    own_c, low_c, high_c = weights(lane % 4, lane, NC - 1)

    def chunk(i):
        return pltpu.make_async_copy(o_s.at[i], o_hbm.at[:, pl.ds(i * FB, FB)], sems.at[i])

    def step(i, carry):
        enter(i).wait()

        def halo(k, f):
            return h_ref[k, pl.ds(pl.multiple_of(f * LEV + i * FB, 8), FB), :]

        columns = jnp.concatenate([halo(2, 0), halo(2, 1), halo(3, 0), halo(3, 1)], 0).astype(BF16)
        edges = column_halo(columns, spread)
        for f in range(2):
            first, last = 0.5 * halo(0, f), 0.5 * halo(1, f)
            for l in range(FB):
                t = z_s[i, f, l]
                t = own_r * t + high_r * pltpu.roll(t, NR - 1, 0) + low_r * pltpu.roll(t, 1, 0)
                t = add_ends(t, first[l : l + 1], last[l : l + 1])
                t = own_c * t + high_c * pltpu.roll(t, NC - 1, 1) + low_c * pltpu.roll(t, 1, 1)
                tile = f * FB + l
                o_s[i, f, l] = t + edges[:, tile * NC : (tile + 1) * NC]
        chunk(i).start()
        return carry

    lax.fori_loop(0, LEV // FB, step, 0)
    for i in range(LEV // FB):
        chunk(i).wait()


OB = 4


def ocean_kernel(
    at_ref, k_ref, o_hbm, m_ref, kc_ref, sp_ref, sn_ref, ss_ref, st_ref, rp_ref, rn_ref, cs_ref, cn_ref, fo_ref,
    out_hbm, out_s, row_ref, col_ref, sems,
):
    def enter(i):
        return pltpu.make_async_copy(o_hbm.at[:, pl.ds(i * OB, OB)], out_s.at[i], sems.at[LO // OB + i])

    for i in range(LO // OB):
        enter(i).start()
    is_top, is_low = at_ref[0] == 7, at_ref[0] == 0
    lane = iota((128, NC), 1)

    def part(ref, base):
        return ref[base : base + 128, :].astype(F32)

    def masks(ref):
        m = ref[MK:PAY, :].astype(F32)
        return m[0:1], m[1:2]

    fr, fc = iota((NC, NC), 0), iota((NC, NC), 1)
    flip = (((fr < 64) & (fc == 63 - fr)) | ((fr == 64) & (fc == 65)) | ((fr == 65) & (fc == 64))).astype(BF16)
    turned = dot(fo_ref[...], flip)
    n0 = jnp.where(is_top, turned[O2:MK], part(cn_ref, O1))
    n1 = jnp.where(is_top, turned[O1:O2], part(cn_ref, O2))
    mc0, mc1 = masks(cn_ref)
    mn0 = jnp.where(is_top, turned[MK + 1 : MK + 2], mc0)
    mn1 = jnp.where(is_top, turned[MK : MK + 1], mc1)
    keep = jnp.where(is_low, 0.0, 1.0)
    s2, s1 = part(cs_ref, O1) * keep, part(cs_ref, O2) * keep
    ms2, ms1 = masks(cs_ref)
    ms2, ms1 = ms2 * keep, ms1 * keep
    um2, um1 = part(rp_ref, O1), part(rp_ref, O2)
    mm2, mm1 = masks(rp_ref)
    u64, u65 = part(rn_ref, O1), part(rn_ref, O2)
    m64, m65 = masks(rn_ref)
    own0, own63 = part(sp_ref, O1), part(sn_ref, O2)
    mo0, mo63 = masks(sp_ref)[0], masks(sn_ref)[1]
    west0, east127 = part(ss_ref, O1), part(st_ref, O2)
    mw0, me127 = masks(ss_ref)[0], masks(st_ref)[1]
    kap = kc_ref[...]

    def along(u, low, high, end):
        where = lane[: u.shape[0]]
        return jnp.where(where == end, high, pltpu.roll(u, 127, 1)) + jnp.where(
            where == 0, low, pltpu.roll(u, 1, 1)
        )

    def advance(u, wet, inner, outer, m_inner, m_outer, low, high, m_low, m_high, end):
        total = inner + outer + along(u, low, high, end)
        m8 = jnp.broadcast_to(wet, (8, NC))
        count = m_inner + m_outer + along(m8, m_low, m_high, end)[0:1]
        return u + kap * (wet * total - count * u)

    def corner(x, at):
        return x[:, at : at + 1]

    row_ref[0] = um1
    row_ref[1] = u64
    row_ref[2] = advance(
        um1, mm1, own0, um2, mo0, mm2, corner(s1, 64), corner(n0, 64), corner(ms1, 64), corner(mn0, 64), 127
    )
    row_ref[3] = advance(
        u64, m64, own63, u65, mo63, m65, corner(s1, 65), corner(n0, 65), corner(ms1, 65), corner(mn0, 65), 127
    )
    west = advance(
        s1, ms1, west0, s2, mw0, ms2, corner(s1, 64), corner(s1, 65), corner(ms1, 64), corner(ms1, 65), 63
    )
    east = advance(
        n0, mn0, east127, n1, me127, mn1, corner(n0, 64), corner(n0, 65), corner(mn0, 64), corner(mn0, 65), 63
    )
    for sub, (low, high) in enumerate(((s1, n0), (west, east))):
        for block in range(LO // OB):
            at = block * OB
            col_ref[sub, block] = jnp.concatenate(
                [x[f * LO + at : f * LO + at + OB] for x in (low, high) for f in range(2)], 0
            )
    spread = edge_spread(2 * OB, 1.0)
    a, b = iota((NR, NR), 0), iota((NR, NR), 1)
    ew = (jnp.abs(a - b) == 1).astype(BF16)
    a, b = iota((NC, NC), 0), iota((NC, NC), 1)
    ns = (jnp.abs(a - b) == 1).astype(BF16)
    wet = m_ref[...].astype(F32)
    r, c = iota((NR, NC), 0), iota((NR, NC), 1)
    m_north = jnp.transpose(jnp.broadcast_to(mn0, (8, NC)))[:NR, 0:1]
    m_south = jnp.transpose(jnp.broadcast_to(ms1, (8, NC)))[:NR, 0:1]
    count = jnp.where(r == NR - 1, m64, pltpu.roll(wet, NR - 1, 0)) + jnp.where(
        r == 0, mm1, pltpu.roll(wet, 1, 0)
    )
    count = count + jnp.where(c == NC - 1, m_north, pltpu.roll(wet, NC - 1, 1))
    count = count + jnp.where(c == 0, m_south, pltpu.roll(wet, 1, 1))

    places = [(f, l) for f in range(2) for l in range(OB)]

    def chunk(i):
        return pltpu.make_async_copy(out_s.at[i], out_hbm.at[:, pl.ds(i * OB, OB)], sems.at[i])

    def step(i, carry):
        enter(i).wait()
        ts = [out_s[i, f, l] for f, l in places]
        for sub in range(2):
            us = [(wet * t).astype(BF16) for t in ts]
            rows = dot(ew, jnp.concatenate(us, 1))
            cols = dot(jnp.concatenate(us, 0), ns)
            ends = column_halo(col_ref[sub, i].astype(BF16), spread)
            for j, (f, l) in enumerate(places):
                level = i * OB + l
                here = pl.ds(f * LO + level, 1)
                total = rows[:, j * NC : (j + 1) * NC] + cols[j * NR : (j + 1) * NR] + ends[:, j * NC : (j + 1) * NC]
                total = add_ends(total, row_ref[2 * sub, here, :], row_ref[2 * sub + 1, here, :])
                ts[j] = ts[j] + (k_ref[f, level] * wet) * (total - count * ts[j])
        for j, (f, l) in enumerate(places):
            out_s[i, f, l] = ts[j]
        chunk(i).start()
        return carry

    lax.fori_loop(0, LO // OB, step, 0)
    for i in range(LO // OB):
        chunk(i).wait()


def index_kernel(at_ref, ids_ref, srow_ref, scol_ref, rrow_ref, rcol_ref):
    gx, gy = at_ref[0], at_ref[1]
    own_tile = gx * 8 + gy
    block = ids_ref[:, pl.ds(pl.multiple_of((gx // 2) * 128, 128), 128)]
    block = pltpu.roll(block, (gx % 2) * 64, 1)
    rows = iota((32, 128), 0)
    tile_row, lane = iota((128, 128), 0), iota((128, 128), 1)
    before = (tile_row < lane).astype(BF16)
    ones = jnp.ones((128, 128), BF16)
    earlier = jnp.zeros((128, 128), F32)
    tiles, ranks = [], []
    for t in range(TOP):
        ids = jnp.sum(jnp.where(rows == gy * 4 + t, block, 0), 0, keepdims=True)
        hit = (ids // 64 == tile_row) & (lane < 64)
        hot = hit.astype(BF16)
        rank = dot(hot, before) + earlier
        earlier = earlier + dot(hot, ones)
        ranks.append(jnp.sum(jnp.where(hit, rank, 0.0), 0, keepdims=True))
        tiles.append((ids // 64).astype(F32))
    place = iota((8, 128), 0)
    stack = jnp.zeros((8, 128), F32)
    for t in range(TOP):
        stack = jnp.where(place == t, tiles[t], jnp.where(place == t + 4, ranks[t], stack))
    spread = (iota((128, 512), 1) // 8 == iota((128, 512), 0)).astype(BF16)
    wide = dot(stack.astype(BF16), spread)
    col, row8 = iota((8, 512), 1), iota((8, 512), 0)
    wide = jnp.where(row8 % 4 == (col // 2) % 4, wide * jnp.where(row8 < 4, 10.0, 2.0), 0.0)
    slot = jnp.sum(wide, 0, keepdims=True) + (iota((1, 512), 1) % 2).astype(F32)
    srow_ref[...] = jnp.broadcast_to(slot, (8, 512))
    scol_ref[...] = jnp.transpose(jnp.broadcast_to(slot, (128, 512)))
    halves = (tile_row // 64) == (lane // 64)
    before2 = (halves & (tile_row < lane)).astype(BF16)
    ones2 = halves.astype(BF16)
    r32, c32 = iota((32, 32), 0), iota((32, 32), 1)
    lower = ((r32 // 4 == c32 // 4) & (c32 % 4 < r32 % 4)).astype(BF16)
    sr, sc = iota((160, 160), 0), iota((160, 160), 1)
    pick = (((sr // 10) % 8 == (sc % 32) // 4) & ((sr % 10) // 2 == sc // 32)).astype(BF16)
    side = iota((160, 128), 0) // 80 == iota((160, 128), 1) // 64
    for b in range(8):
        ids = ids_ref[:, b * 128 : (b + 1) * 128]
        hit = ids // 64 == own_tile
        hot = hit.astype(BF16)
        rank = dot(hot, before2) + dot(lower, dot(hot, ones2).astype(BF16))
        value = (ids % 64 + 1).astype(F32)
        stacked = jnp.concatenate([jnp.where(hit & (rank == float(k)), value, 0.0) for k in range(CAP)], 0)
        found = jnp.where(side, dot(pick, stacked.astype(BF16)), 0.0)
        rcol_ref[b * 160 : (b + 1) * 160, :] = dot(found.astype(BF16), ones)
    for b in range(SLOTS // 128):
        turned = jnp.transpose(rcol_ref[b * 128 : (b + 1) * 128, :])
        rrow_ref[:, b * 128 : (b + 1) * 128] = turned[0:8]


def pack_kernel(c_ref, srow_ref, fold_ref, out_ref):
    del fold_ref
    slot = srow_ref[0:1, :].astype(jnp.int32)
    hot = jnp.where(slot == iota((SLOTS, 512), 0), 1.0, 0.0).astype(BF16)
    out_ref[...] = dot(hot, c_ref[...].astype(BF16)).astype(BF16)


def ocean_surface_kernel(in_ref, rrow_ref, rcol_ref, m_ref, t_ref, out_ref, back_ref):
    row, col = iota((128, SLOTS), 0), iota((128, SLOTS), 1)
    take = (rrow_ref[0:1, :].astype(jnp.int32) - 1 == row % 64) & (col % 2 == row // 64)
    forcing = dot(jnp.where(take, 1.0, 0.0).astype(BF16), in_ref[...])
    wet = 0.25 * m_ref[...].astype(F32)
    news = []
    for f in range(2):
        new = t_ref[f, 0] + wet * forcing[f * 64 : (f + 1) * 64]
        out_ref[f, 0] = new
        news.append(new)
    sea = jnp.concatenate(news, 0).astype(BF16)
    row, col = iota((SLOTS, 128), 0), iota((SLOTS, 128), 1)
    give = (rcol_ref[...].astype(jnp.int32) - 1 == col % 64) & (row % 2 == col // 64)
    back_ref[...] = dot(jnp.where(give, 1.0, 0.0).astype(BF16), sea).astype(BF16)


def entry_kernel(in_ref, scol_ref, out_ref):
    total = jnp.zeros((512, 128), F32)
    slot = scol_ref[...].astype(jnp.int32)
    for b in range(SLOTS // 128):
        hot = jnp.where(slot == iota((512, 128), 1) + b * 128, 1.0, 0.0).astype(BF16)
        total = total + dot(hot, in_ref[b * 128 : (b + 1) * 128, :])
    out_ref[...] = total.astype(BF16)


def shape(dims, dtype=F32):
    return jax.ShapeDtypeStruct(dims, dtype)


def shifted(x, axis, by):
    count = lax.axis_size(axis)
    return lax.ppermute(x, axis, [(i, (i + by) % count) for i in range(count)])


def per_device(atm_state, ocean_state, land_mask, elem_op, column_mix, kappa, remap_weight, intersection):
    gx, gy = lax.axis_index("gx"), lax.axis_index("gy")
    at = jnp.stack([gx, gy]).astype(jnp.int32)
    smem = pl.BlockSpec(memory_space=pltpu.SMEM)
    full = whole((PAY, NC))

    vmem = pl.BlockSpec(memory_space=pltpu.VMEM)
    hbm = pl.BlockSpec(memory_space=pl.ANY)

    def pinned(x):
        return pltpu.with_memory_space_constraint(x, pltpu.HBM)

    atm_in, ocean_in, mask_in = pinned(atm_state), pinned(ocean_state), pinned(land_mask)
    mix_in, elem_in = pinned(column_mix), pinned(elem_op)
    payload = shape((PAY, NC), BF16)
    rim, send_next, send_prev, element = pl.pallas_call(
        atm_rim_kernel,
        in_specs=[hbm] * 5,
        out_specs=[hbm] + [vmem] * 3,
        out_shape=[pltpu.HBM(atm_state.shape, F32), payload, payload, shape((512, 512), BF16)],
        scratch_shapes=[
            pltpu.VMEM((2, 2, LEV, 8, NC), F32),
            pltpu.VMEM((2, 2, LO, 8, NC), F32),
            pltpu.VMEM((NR, NC), jnp.int32),
            pltpu.VMEM((LEV, LEV), F32),
            pltpu.VMEM((16, 16), F32),
            pltpu.VMEM((2, 2, LEV, 8, NC), F32),
            pltpu.SemaphoreType.DMA((9,)),
        ],
        compiler_params=params(16),
        name="atm_rim",
    )(atm_in, ocean_in, mask_in, mix_in, elem_in)

    from_prev = shifted(send_next, "gx", 1)
    from_next = shifted(send_prev, "gx", -1)

    weights = remap_weight[:, 0]
    weights_in = pinned(weights)
    z, top_level, z_cols, ocean_cols, near_weights = pl.pallas_call(
        inner_kernel,
        in_specs=[hbm, hbm, hbm, vmem, vmem, hbm, hbm],
        out_specs=[hbm] + [vmem] * 4,
        out_shape=[pltpu.HBM(atm_state.shape, F32), shape((2, NR, NC)), shape((2, 144, NC)), shape((4, 128, NC)),
                   pltpu.VMEM(weights.shape, BF16)],
        scratch_shapes=[
            pltpu.VMEM((INNER, 2, LEV, 8, NC), F32),
            pltpu.VMEM(atm_state.shape, F32),
            pltpu.VMEM(ocean_state.shape, F32),
            pltpu.VMEM((LEV, LEV), F32),
            pltpu.SemaphoreType.DMA((2 * INNER,)),
            pltpu.SemaphoreType.DMA((5,)),
        ],
        input_output_aliases={5: 0},
        compiler_params=params(24),
        cost_estimate=pl.CostEstimate(flops=1000000000, bytes_accessed=14000000, transcendentals=0),
        name="inner",
    )(atm_in, mix_in, ocean_in, element, land_mask, rim, weights_in)

    send_south, send_north = pl.pallas_call(
        cols_kernel,
        out_shape=[shape((PAY, NC), BF16)] * 2,
        compiler_params=params(),
        name="cols",
    )(z_cols, ocean_cols, land_mask, from_prev, from_next)

    from_south = shifted(send_north, "gy", 1)
    from_north = shifted(send_south, "gy", -1)
    gx_count, gy_count = lax.axis_size("gx"), lax.axis_size("gy")
    top = gy_count - 1
    folded = lax.ppermute(
        send_north, ("gx", "gy"), [(i * gy_count + top, (gx_count - 1 - i) * gy_count + top) for i in range(gx_count)]
    )

    ids = jnp.transpose(intersection, (1, 2, 0)).reshape(32, 1024)
    slot_row, slot_col, recv_row, recv_col = pl.pallas_call(
        index_kernel,
        in_specs=[smem, pl.BlockSpec(memory_space=pltpu.VMEM)],
        out_shape=[shape((8, 512)), shape((512, 128)), shape((8, SLOTS)), shape((SLOTS, 128))],
        compiler_params=params(),
        cost_estimate=pl.CostEstimate(flops=4000000, bytes_accessed=4200000, transcendentals=0),
        name="index",
    )(at, ids)

    surface = pl.pallas_call(
        surface_kernel,
        in_specs=[vmem] * 5,
        out_shape=shape((2, NR, NC), BF16),
        compiler_params=params(),
        name="surface",
    )(top_level, from_prev, from_next, from_south, from_north)

    products = lax.dot_general(
        near_weights, surface, (((3,), (2,)), ((0,), (1,))), preferred_element_type=F32
    )
    contrib = jnp.transpose(products, (0, 1, 3, 2)).reshape(2 * ENT, NC)
    outgoing = pl.pallas_call(
        pack_kernel,
        in_specs=[pl.BlockSpec(memory_space=pltpu.VMEM)] * 2 + [pl.BlockSpec(memory_space=pl.ANY)],
        out_shape=shape((SLOTS, NC), BF16),
        compiler_params=params(),
        name="pack",
    )(contrib, slot_row, folded)
    incoming = lax.all_to_all(
        outgoing.reshape(TILES, CAP, 2, NC), ("gx", "gy"), split_axis=0, concat_axis=0, tiled=True
    ).reshape(SLOTS, NC)

    kap_col = jnp.broadcast_to(jnp.pad(kappa.reshape(OL, 1), ((0, 8), (0, 0))), (128, NC))
    ocean_mid = pl.pallas_call(
        ocean_kernel,
        in_specs=[smem, smem, hbm] + [vmem] * 11,
        out_specs=hbm,
        out_shape=pltpu.HBM(ocean_state.shape, F32),
        scratch_shapes=[
            pltpu.VMEM((LO // OB, 2, OB, NR, NC), F32),
            pltpu.VMEM((4, 128, NC), F32),
            pltpu.VMEM((2, LO // OB, 4 * OB, NC), F32),
            pltpu.SemaphoreType.DMA((2 * (LO // OB),)),
        ],
        compiler_params=params(16),
        cost_estimate=pl.CostEstimate(flops=30000000, bytes_accessed=8000000, transcendentals=0),
        name="ocean",
    )(
        at[1:], kappa, ocean_in, land_mask, kap_col, send_prev, send_next, send_south, send_north,
        from_prev, from_next, from_south, from_north, folded,
    )

    level_zero = pl.BlockSpec((2, 1, NR, NC), lambda i: (0, 0, 0, 0))
    ocean_next, back_out = pl.pallas_call(
        ocean_surface_kernel,
        grid=(1,),
        in_specs=[whole((SLOTS, NC)), whole((8, SLOTS)), whole((SLOTS, 128)), whole((NR, NC)), level_zero],
        out_specs=[level_zero, whole((SLOTS, NC))],
        out_shape=[pltpu.HBM(ocean_state.shape, F32), shape((SLOTS, NC), BF16)],
        input_output_aliases={4: 0},
        compiler_params=params(),
        name="ocean_surface",
    )(incoming, recv_row, recv_col, land_mask, ocean_mid)

    back_in = lax.all_to_all(
        back_out.reshape(TILES, CAP, 2, NC), ("gx", "gy"), split_axis=0, concat_axis=0, tiled=True
    ).reshape(SLOTS, NC)

    atm_next = pl.pallas_call(
        finish_kernel,
        in_specs=[hbm] + [vmem] * 4,
        out_specs=hbm,
        out_shape=pltpu.HBM(atm_state.shape, F32),
        scratch_shapes=[
            pltpu.VMEM((LEV // FB, 2, FB, NR, NC), F32),
            pltpu.VMEM((LEV // FB, 2, FB, NR, NC), F32),
            pltpu.VMEM((4, 144, NC), F32),
            pltpu.SemaphoreType.DMA((2 * (LEV // FB),)),
        ],
        compiler_params=params(16),
        cost_estimate=pl.CostEstimate(flops=20000000, bytes_accessed=9400000, transcendentals=0),
        name="finish",
    )(pinned(z), from_prev, from_next, from_south, from_north)

    entries = pl.pallas_call(
        entry_kernel,
        out_shape=shape((2 * ENT, NC), BF16),
        compiler_params=params(),
        name="entries",
    )(back_in, slot_col)
    returned = lax.dot_general(
        weights,
        entries.reshape(NR, TOP, 2, NC),
        (((1, 2), (1, 3)), ((0,), (0,))),
        preferred_element_type=F32,
    )
    return atm_next, ocean_next, jnp.transpose(returned, (2, 0, 1))


def solution(mesh):
    placed = (
        P(None, None, "gx", "gy"),
        P(None, None, "gx", "gy"),
        P("gx", "gy"),
        P(),
        P(),
        P(),
        P("gx", "gy", None, None, None),
        P(),
    )
    return jax.shard_map(
        per_device,
        mesh=mesh,
        in_specs=placed,
        out_specs=(P(None, None, "gx", "gy"), P(None, None, "gx", "gy"), P(None, "gx", "gy")),
        check_vma=False,
    )
```

```python
import jax
import jax.numpy as jnp
from jax import lax
from jax.experimental import pallas as pl
from jax.experimental.pallas import tpu as pltpu
from jax.sharding import PartitionSpec as P

F32, BF16 = jnp.float32, jnp.bfloat16
LEV, LO, NR, NC = 72, 60, 64, 128
AT, O1, O2, MK, PAY = 0, 144, 272, 400, 416
OL = 2 * LO
TOP, CAP, TILES = 4, 5, 128
ENT = NR * TOP
SLOTS = TILES * CAP * 2
MIB = 1024 * 1024


def iota(shape, dim):
    return lax.broadcasted_iota(jnp.int32, shape, dim)


def dot(a, b):
    return jnp.dot(a, b, preferred_element_type=F32)


def params(mib=6):
    return pltpu.CompilerParams(vmem_limit_bytes=mib * MIB)


def whole(shape):
    return pl.BlockSpec(shape, lambda *_: (0,) * len(shape))


def mask_rows(first, second):
    place = iota((16, NC), 0)
    return jnp.where(place == 0, first, jnp.where(place == 1, second, 0.0)).astype(BF16)


def element_rows(x_s, mix, b):
    fields = [jnp.swapaxes(x_s[f], 0, 1) for f in range(2)]
    ys = []
    for big in range(2):
        for f in range(2):
            x = jnp.concatenate([fields[f][big * 4 + k] for k in range(4)], 1)
            ys.append(x + dot(mix, x.astype(BF16)))
    y = jnp.concatenate(ys, 0)
    z = y + dot(y.astype(BF16), b)
    pieces = [[], []]
    for r in range(8):
        for f in range(2):
            at = ((r // 4) * 2 + f) * LEV
            pieces[f].append(z[at : at + LEV, (r % 4) * NC : (r % 4 + 1) * NC])
    return pieces


def store_rows(z_ref, pieces, at):
    for f in range(2):
        z_ref[f, :, pl.ds(at, 8), :] = jnp.swapaxes(jnp.stack(pieces[f], 0), 0, 1)


def atm_rim_kernel(
    x_hbm, o_hbm, m_hbm, mix_hbm, elem_hbm, z_hbm, sn_ref, sp_ref, b_ref, x_s, o_s, m_s, mix_s, elem_s, z_s, sems
):
    sources = (elem_hbm, mix_hbm, x_hbm.at[:, :, pl.ds(0, 8), :], x_hbm.at[:, :, pl.ds(NR - 8, 8), :], m_hbm) + tuple(
        o_hbm.at[:, :, pl.ds(at, 8), :] for at in (0, NR - 8)
    )
    targets = (elem_s, mix_s, x_s.at[0], x_s.at[1], m_s, o_s.at[0], o_s.at[1])
    copies = [pltpu.make_async_copy(a, b, sems.at[k]) for k, (a, b) in enumerate(zip(sources, targets))]
    outs = [
        pltpu.make_async_copy(z_s.at[k], z_hbm.at[:, :, pl.ds(k * (NR - 8), 8), :], sems.at[7 + k]) for k in range(2)
    ]
    for copy in copies:
        copy.start()
    copies[0].wait()
    row = iota((512, 16), 0)
    spread_in = (iota((512, 16), 1) == (row // 128) * 4 + row % 4).astype(BF16)
    col = iota((16, 512), 1)
    spread_out = (iota((16, 512), 0) == (col // 128) * 4 + col % 4).astype(BF16)
    elem = (0.5 * elem_s[...]).astype(BF16)
    half = lax.dot_general(spread_in, elem, (((1,), (1,)), ((), ())), preferred_element_type=F32)
    spread = dot(half.astype(BF16), spread_out)
    same = (iota((512, 512), 0) % 128) // 4 == (iota((512, 512), 1) % 128) // 4
    b = jnp.where(same, spread, 0.0).astype(BF16)
    b_ref[...] = b
    copies[1].wait()
    mix = (0.5 * mix_s[...]).astype(BF16)
    for k, ref in ((0, sp_ref), (1, sn_ref)):
        copies[2 + k].wait()
        pieces = element_rows(x_s.at[k], mix, b)
        store_rows(z_s.at[k], pieces, 0)
        outs[k].start()
        ref[AT:O1, :] = jnp.concatenate([pieces[f][7 * k] for f in range(2)], 0).astype(BF16)
    for k in (4, 5, 6):
        copies[k].wait()
    m = m_s[...].astype(F32)
    for ref, k, first in ((sp_ref, 0, 0), (sn_ref, 1, 6)):
        rows = jnp.swapaxes(o_s[k].reshape(OL, 8, NC), 0, 1)
        at = k * (NR - 8) + first
        for j, base in ((0, O1), (1, O2)):
            u = rows[first + j] * m[at + j : at + j + 1]
            ref[base : base + 128, :] = jnp.concatenate([u, jnp.zeros((8, NC), F32)], 0).astype(BF16)
        ref[MK:PAY, :] = mask_rows(m[at : at + 1], m[at + 1 : at + 2])
    for copy in outs:
        copy.wait()


INNER = NR // 8 - 2


def pick_columns(columns):
    k, at = iota((8 * len(columns), 8 * NC), 0), iota((8 * len(columns), 8 * NC), 1)
    wanted = jnp.zeros_like(k)
    for j, c in enumerate(columns):
        wanted = jnp.where(k // 8 == j, c, wanted)
    return ((at // NC == k % 8) & (at % NC == wanted)).astype(BF16)


def take_columns(pick, tiles):
    side = jnp.concatenate([t.astype(BF16) for t in tiles], 1)
    got = lax.dot_general(pick, side, (((1,), (1,)), ((), ())), preferred_element_type=F32)
    return jnp.concatenate([got, jnp.zeros_like(got)], 1)


def inner_kernel(
    x_hbm, mix_hbm, o_hbm, b_ref, m_ref, rim_hbm, w_hbm, z_hbm, top_ref, zc_ref, oc_ref, w_ref,
    x_s, z_s, o_s, mix_s, sems, rest,
):
    mix_copy = pltpu.make_async_copy(mix_hbm, mix_s, rest.at[0])
    ocean_copy = pltpu.make_async_copy(o_hbm, o_s, rest.at[1])
    rims = [
        pltpu.make_async_copy(
            rim_hbm.at[:, :, pl.ds(at, 8), :], z_s.at[:, :, pl.ds(at, 8), :], rest.at[2 + k]
        )
        for k, at in enumerate((0, NR - 8))
    ]

    def chunk(i):
        return pltpu.make_async_copy(x_hbm.at[:, :, pl.ds(i * 8 + 8, 8), :], x_s.at[i], sems.at[i])

    def leave(i):
        rows = pl.ds(pl.multiple_of(i * 8 + 8, 8), 8)
        return pltpu.make_async_copy(z_s.at[:, :, rows, :], z_hbm.at[:, :, rows, :], sems.at[INNER + i])

    mix_copy.start()
    for i in range(INNER):
        chunk(i).start()
    for copy in rims:
        copy.start()
    ocean_copy.start()
    weight_copy = pltpu.make_async_copy(w_hbm, w_ref, rest.at[4])
    weight_copy.start()
    mix_copy.wait()
    mix = (0.5 * mix_s[...]).astype(BF16)

    def step(i, carry):
        chunk(i).wait()
        store_rows(z_s, element_rows(x_s.at[i], mix, b_ref[...]), pl.multiple_of(i * 8 + 8, 8))
        leave(i).start()
        return carry

    lax.fori_loop(0, INNER, step, 0)
    for copy in rims:
        copy.wait()
    pick = pick_columns((0, NC - 1))

    def atm(i, carry):
        for f in range(2):
            got = take_columns(pick, [z_s[f, i * 8 + l] for l in range(8)])
            at = pl.multiple_of(f * LEV + i * 8, 8)
            for k in range(2):
                zc_ref[k, pl.ds(at, 8), :] = got[k * 8 : k * 8 + 8]
        return carry

    lax.fori_loop(0, LEV // 8, atm, 0, unroll=3)
    for f in range(2):
        top_ref[f] = z_s[f, LEV - 1]
    ocean_copy.wait()
    wet = m_ref[...].astype(F32)
    pick = pick_columns((0, 1, NC - 2, NC - 1))

    def ocean(i, carry):
        tiles = [i * 8 + l for l in range(8)]
        got = take_columns(pick, [wet * o_s[t // LO, t % LO] for t in tiles])
        for k in range(4):
            oc_ref[k, pl.ds(pl.multiple_of(i * 8, 8), 8), :] = got[k * 8 : k * 8 + 8]
        return carry

    lax.fori_loop(0, OL // 8, ocean, 0, unroll=3)
    oc_ref[:, OL:, :] = jnp.zeros((4, 8, NC), F32)
    for i in range(INNER):
        leave(i).wait()
    weight_copy.wait()


def cols_kernel(zc_ref, oc_ref, m_ref, rp_ref, rn_ref, ss_ref, sn_ref):
    lane = iota((144, NC), 1)
    place = lane % 4
    rp_at, rn_at = rp_ref[AT:O1, :].astype(F32), rn_ref[AT:O1, :].astype(F32)
    before, after = rp_ref[O2:MK, :].astype(F32), rn_ref[O1:O2, :].astype(F32)
    olane = iota((128, NC), 1)
    row = iota((64, NC), 0)
    m_before, m_after = rp_ref[MK:PAY, :].astype(F32)[1:2], rn_ref[MK:PAY, :].astype(F32)[0:1]
    tail = jnp.where(row == 0, m_before, jnp.where(row == 1, m_after, 0.0))
    m_t = jnp.transpose(jnp.concatenate([m_ref[...].astype(F32), tail], 0))
    for ref, c_at, ocs in ((ss_ref, 0, (0, 1)), (sn_ref, 127, (126, 127))):
        z = zc_ref[0 if c_at == 0 else 1]
        nxt = jnp.where(lane == 63, rn_at[:, c_at : c_at + 1], pltpu.roll(z, 127, 1))
        prv = jnp.where(lane == 0, rp_at[:, c_at : c_at + 1], pltpu.roll(z, 1, 1))
        z = jnp.where(place == 3, (z + nxt) * 0.5, jnp.where(place == 0, (z + prv) * 0.5, z))
        ref[AT:O1, :] = z.astype(BF16)
        for k, c in enumerate(ocs):
            source = c if c < 2 else c - 124
            u = jnp.where(
                olane < 64,
                oc_ref[source],
                jnp.where(olane == 64, before[:, c : c + 1], jnp.where(olane == 65, after[:, c : c + 1], 0.0)),
            )
            base = (O1, O2)[k]
            ref[base : base + 128, :] = u.astype(BF16)
        ref[MK:PAY, :] = mask_rows(m_t[ocs[0] : ocs[0] + 1], m_t[ocs[1] : ocs[1] + 1])


def averaged(z, nxt, prv, place):
    return jnp.where(place == 3, (z + nxt) * 0.5, jnp.where(place == 0, (z + prv) * 0.5, z))


def stiffness(z, h_prev, h_next, c_south, c_north):
    row, lane = iota((NR, NC), 0), iota((NR, NC), 1)
    nxt = jnp.where(row == NR - 1, h_next, pltpu.roll(z, NR - 1, 0))
    prv = jnp.where(row == 0, h_prev, pltpu.roll(z, 1, 0))
    z = averaged(z, nxt, prv, row % 4)
    nxt = jnp.where(lane == NC - 1, c_north, pltpu.roll(z, NC - 1, 1))
    prv = jnp.where(lane == 0, c_south, pltpu.roll(z, 1, 1))
    return averaged(z, nxt, prv, lane % 4)


def surface_kernel(z_ref, rp_ref, rn_ref, cs_ref, cn_ref, s_ref):
    rp, rn = rp_ref[AT:O1, :].astype(F32), rn_ref[AT:O1, :].astype(F32)
    cs, cn = cs_ref[AT:O1, :].astype(F32), cn_ref[AT:O1, :].astype(F32)
    for f in range(2):
        top = f * LEV + LEV - 8
        south = jnp.transpose(cs[top : top + 8])[:NR, 7:8]
        north = jnp.transpose(cn[top : top + 8])[:NR, 7:8]
        last = top + 7
        s = stiffness(z_ref[f], rp[last : last + 1], rn[last : last + 1], south, north)
        s_ref[f] = s.astype(BF16)


def edge_spread(tiles, scale):
    k, c = iota((2 * tiles, tiles * NC), 0), iota((2 * tiles, tiles * NC), 1)
    mine = k % tiles == c // NC
    end = c % NC == jnp.where(k < tiles, 0, NC - 1)
    return jnp.where(mine & end, scale, 0.0).astype(BF16)


def add_ends(x, first, last):
    row = iota((8, NC), 0)
    return jnp.concatenate(
        [
            x[0:8] + jnp.where(row == 0, first, 0.0),
            x[8 : NR - 8],
            x[NR - 8 :] + jnp.where(row == 7, last, 0.0),
        ],
        0,
    )


def column_halo(columns, spread):
    return lax.dot_general(columns, spread, (((0,), (0,)), ((), ())), preferred_element_type=F32)[:NR]


FB = 8


def finish_kernel(
    z_hbm, rp_ref, rn_ref, cs_ref, cn_ref, new_ref, mid_hbm, o_hbm, ocean_hbm, z_s, o_s, h_ref, sems, level_sem
):
    del mid_hbm
    level = pltpu.make_async_copy(new_ref, ocean_hbm.at[:, 0], level_sem)
    level.start()

    def enter(i):
        return pltpu.make_async_copy(z_hbm.at[:, pl.ds(i * FB, FB)], z_s.at[i], sems.at[LEV // FB + i])

    for i in range(LEV // FB):
        enter(i).start()
    for k, ref in enumerate((rp_ref, rn_ref, cs_ref, cn_ref)):
        h_ref[k] = ref[AT:O1, :].astype(F32)
    spread = edge_spread(2 * FB, 0.5)
    row, lane = iota((NR, NC), 0), iota((NR, NC), 1)

    def weights(place, at, end):
        low = jnp.where((place == 0) & (at != 0), 0.5, 0.0)
        high = jnp.where((place == 3) & (at != end), 0.5, 0.0)
        return jnp.where((place == 0) | (place == 3), 0.5, 1.0), low, high

    own_r, low_r, high_r = weights(row % 4, row, NR - 1)
    own_c, low_c, high_c = weights(lane % 4, lane, NC - 1)

    def chunk(i):
        return pltpu.make_async_copy(o_s.at[i], o_hbm.at[:, pl.ds(i * FB, FB)], sems.at[i])

    def step(i, carry):
        enter(i).wait()

        def halo(k, f):
            return h_ref[k, pl.ds(pl.multiple_of(f * LEV + i * FB, 8), FB), :]

        columns = jnp.concatenate([halo(2, 0), halo(2, 1), halo(3, 0), halo(3, 1)], 0).astype(BF16)
        edges = column_halo(columns, spread)
        for f in range(2):
            first, last = 0.5 * halo(0, f), 0.5 * halo(1, f)
            for l in range(FB):
                t = z_s[i, f, l]
                t = own_r * t + high_r * pltpu.roll(t, NR - 1, 0) + low_r * pltpu.roll(t, 1, 0)
                t = add_ends(t, first[l : l + 1], last[l : l + 1])
                t = own_c * t + high_c * pltpu.roll(t, NC - 1, 1) + low_c * pltpu.roll(t, 1, 1)
                tile = f * FB + l
                o_s[i, f, l] = t + edges[:, tile * NC : (tile + 1) * NC]
        chunk(i).start()
        return carry

    lax.fori_loop(0, LEV // FB, step, 0)
    level.wait()
    for i in range(LEV // FB):
        chunk(i).wait()


OB = 12


def ocean_kernel(
    at_ref, k_ref, o_hbm, m_ref, kc_ref, sp_ref, sn_ref, ss_ref, st_ref, rp_ref, rn_ref, cs_ref, cn_ref, fo_ref,
    out_hbm, first_ref, out_s, row_ref, col_ref, sems,
):
    def enter(i):
        return pltpu.make_async_copy(o_hbm.at[:, pl.ds(i * OB, OB)], out_s.at[i], sems.at[LO // OB + i])

    for i in range(LO // OB):
        enter(i).start()
    is_top, is_low = at_ref[0] == 7, at_ref[0] == 0
    lane = iota((128, NC), 1)

    def part(ref, base):
        return ref[base : base + 128, :].astype(F32)

    def masks(ref):
        m = ref[MK:PAY, :].astype(F32)
        return m[0:1], m[1:2]

    fr, fc = iota((NC, NC), 0), iota((NC, NC), 1)
    flip = (((fr < 64) & (fc == 63 - fr)) | ((fr == 64) & (fc == 65)) | ((fr == 65) & (fc == 64))).astype(BF16)
    turned = dot(fo_ref[...], flip)
    n0 = jnp.where(is_top, turned[O2:MK], part(cn_ref, O1))
    n1 = jnp.where(is_top, turned[O1:O2], part(cn_ref, O2))
    mc0, mc1 = masks(cn_ref)
    mn0 = jnp.where(is_top, turned[MK + 1 : MK + 2], mc0)
    mn1 = jnp.where(is_top, turned[MK : MK + 1], mc1)
    keep = jnp.where(is_low, 0.0, 1.0)
    s2, s1 = part(cs_ref, O1) * keep, part(cs_ref, O2) * keep
    ms2, ms1 = masks(cs_ref)
    ms2, ms1 = ms2 * keep, ms1 * keep
    um2, um1 = part(rp_ref, O1), part(rp_ref, O2)
    mm2, mm1 = masks(rp_ref)
    u64, u65 = part(rn_ref, O1), part(rn_ref, O2)
    m64, m65 = masks(rn_ref)
    own0, own63 = part(sp_ref, O1), part(sn_ref, O2)
    mo0, mo63 = masks(sp_ref)[0], masks(sn_ref)[1]
    west0, east127 = part(ss_ref, O1), part(st_ref, O2)
    mw0, me127 = masks(ss_ref)[0], masks(st_ref)[1]
    at, l60 = iota((128, LO), 0), iota((128, LO), 1)
    kap = sum(
        jnp.sum(jnp.where(at - f * LO == l60, kc_ref[f : f + 1, :], 0.0), 1, keepdims=True) for f in range(2)
    )

    def along(u, low, high, end):
        where = lane[: u.shape[0]]
        return jnp.where(where == end, high, pltpu.roll(u, 127, 1)) + jnp.where(
            where == 0, low, pltpu.roll(u, 1, 1)
        )

    def advance(u, wet, inner, outer, m_inner, m_outer, low, high, m_low, m_high, end):
        total = inner + outer + along(u, low, high, end)
        m8 = jnp.broadcast_to(wet, (8, NC))
        count = m_inner + m_outer + along(m8, m_low, m_high, end)[0:1]
        return u + kap * (wet * total - count * u)

    def corner(x, at):
        return x[:, at : at + 1]

    row_ref[0] = um1
    row_ref[1] = u64
    row_ref[2] = advance(
        um1, mm1, own0, um2, mo0, mm2, corner(s1, 64), corner(n0, 64), corner(ms1, 64), corner(mn0, 64), 127
    )
    row_ref[3] = advance(
        u64, m64, own63, u65, mo63, m65, corner(s1, 65), corner(n0, 65), corner(ms1, 65), corner(mn0, 65), 127
    )
    west = advance(
        s1, ms1, west0, s2, mw0, ms2, corner(s1, 64), corner(s1, 65), corner(ms1, 64), corner(ms1, 65), 63
    )
    east = advance(
        n0, mn0, east127, n1, me127, mn1, corner(n0, 64), corner(n0, 65), corner(mn0, 64), corner(mn0, 65), 63
    )
    here = iota((NR, NC), 1)
    for sub, (low, high) in enumerate(((s1, n0), (west, east))):
        low, high = jnp.transpose(low)[:NR], jnp.transpose(high)[:NR]
        for f in range(2):
            col_ref[2 * sub + f] = jnp.where(
                here < 64, pltpu.roll(low, (NC - LO * f) % NC, 1), pltpu.roll(high, (NC + 64 - LO * f) % NC, 1)
            )
    a, b = iota((NC, NC), 0), iota((NC, NC), 1)
    ends = ((a == 0) & (b == 0)) | ((a == 64) & (b == NC - 1))
    ns = jnp.concatenate([(jnp.abs(a - b) == 1).astype(BF16), ends.astype(BF16)], 0)
    wet = m_ref[...].astype(F32)
    r, c = iota((NR, NC), 0), iota((NR, NC), 1)
    m_north = jnp.transpose(jnp.broadcast_to(mn0, (8, NC)))[:NR, 0:1]
    m_south = jnp.transpose(jnp.broadcast_to(ms1, (8, NC)))[:NR, 0:1]
    count = jnp.where(r == NR - 1, m64, pltpu.roll(wet, NR - 1, 0)) + jnp.where(
        r == 0, mm1, pltpu.roll(wet, 1, 0)
    )
    count = count + jnp.where(c == NC - 1, m_north, pltpu.roll(wet, NC - 1, 1))
    count = count + jnp.where(c == 0, m_south, pltpu.roll(wet, 1, 1))

    places = [(f, l) for f in range(2) for l in range(OB)]

    def chunk(i):
        return pltpu.make_async_copy(out_s.at[i], out_hbm.at[:, pl.ds(i * OB, OB)], sems.at[i])

    def step(i, carry):
        enter(i).wait()
        ts = [out_s[i, f, l] for f, l in places]
        for sub in range(2):
            us = [wet * t for t in ts]
            halos = [pltpu.roll(col_ref[2 * sub + f], (NC - i * OB - l) % NC, 1) for f, l in places]
            side = jnp.concatenate([jnp.concatenate(us, 0), jnp.concatenate(halos, 0)], 1)
            cols = dot(side.astype(BF16), ns)
            for j, (f, l) in enumerate(places):
                level = i * OB + l
                here = pl.ds(f * LO + level, 1)
                u = us[j]
                total = pltpu.roll(u, NR - 1, 0) + pltpu.roll(u, 1, 0) + cols[j * NR : (j + 1) * NR]
                total = add_ends(
                    total, row_ref[2 * sub, here, :] - u[NR - 1 :], row_ref[2 * sub + 1, here, :] - u[0:1]
                )
                ts[j] = ts[j] + (k_ref[f, level] * wet) * (total - count * ts[j])
        for j, (f, l) in enumerate(places):
            out_s[i, f, l] = ts[j]
        chunk(i).start()
        return carry

    lax.fori_loop(0, LO // OB, step, 0)
    for f in range(2):
        first_ref[f] = out_s[0, f, 0]
    for i in range(LO // OB):
        chunk(i).wait()


def send_map_kernel(at_ref, ids_ref, out_ref, scol_ref):
    gx, gy = at_ref[0], at_ref[1]
    block = ids_ref[:, pl.ds(pl.multiple_of((gx // 2) * 128, 128), 128)]
    block = pltpu.roll(block, (gx % 2) * 64, 1)
    rows = iota((32, 128), 0)
    tile_row, lane = iota((128, 128), 0), iota((128, 128), 1)
    before = (tile_row < lane).astype(BF16)
    ones = jnp.ones((128, 128), BF16)
    earlier = jnp.zeros((128, 128), F32)
    tiles, ranks = [], []
    for t in range(TOP):
        ids = jnp.sum(jnp.where(rows == gy * 4 + t, block, 0), 0, keepdims=True)
        hit = (ids // 64 == tile_row) & (lane < 64)
        hot = hit.astype(BF16)
        rank = dot(hot, before) + earlier
        earlier = earlier + dot(hot, ones)
        ranks.append(jnp.sum(jnp.where(hit, rank, 0.0), 0, keepdims=True))
        tiles.append((ids // 64).astype(F32))
    place = iota((8, 128), 0)
    stack = jnp.zeros((8, 128), F32)
    for t in range(TOP):
        stack = jnp.where(place == t, tiles[t], jnp.where(place == t + 4, ranks[t], stack))
    spread = (iota((128, 512), 1) // 8 == iota((128, 512), 0)).astype(BF16)
    wide = dot(stack.astype(BF16), spread)
    col, row8 = iota((8, 512), 1), iota((8, 512), 0)
    wide = jnp.where(row8 % 4 == (col // 2) % 4, wide * jnp.where(row8 < 4, 10.0, 2.0), 0.0)
    slot = jnp.sum(wide, 0, keepdims=True) + (iota((1, 512), 1) % 2).astype(F32)
    out_ref[...] = jnp.where(slot.astype(jnp.int32) == iota((SLOTS, 512), 0), 1.0, 0.0).astype(BF16)
    scol_ref[...] = jnp.transpose(jnp.broadcast_to(slot, (128, 512)))


def receive_map_kernel(at_ref, ids_ref, take_ref, give_ref):
    own_tile = at_ref[0] * 8 + at_ref[1]
    tile_row, lane = iota((128, 128), 0), iota((128, 128), 1)
    ones = jnp.ones((128, 128), BF16)
    halves = (tile_row // 64) == (lane // 64)
    before2 = (halves & (tile_row < lane)).astype(BF16)
    ones2 = halves.astype(BF16)
    r32, c32 = iota((32, 32), 0), iota((32, 32), 1)
    lower = ((r32 // 4 == c32 // 4) & (c32 % 4 < r32 % 4)).astype(BF16)
    sr, sc = iota((160, 160), 0), iota((160, 160), 1)
    pick = (((sr // 10) % 8 == (sc % 32) // 4) & ((sr % 10) // 2 == sc // 32)).astype(BF16)
    side = iota((160, 128), 0) // 80 == iota((160, 128), 1) // 64
    for b in range(8):
        ids = ids_ref[:, b * 128 : (b + 1) * 128]
        hit = ids // 64 == own_tile
        hot = hit.astype(BF16)
        rank = dot(hot, before2) + dot(lower, dot(hot, ones2).astype(BF16))
        value = (ids % 64 + 1).astype(F32)
        stacked = jnp.concatenate([jnp.where(hit & (rank == float(k)), value, 0.0) for k in range(CAP)], 0)
        found = jnp.where(side, dot(pick, stacked.astype(BF16)), 0.0)
        held = dot(found.astype(BF16), ones).astype(jnp.int32)
        row, col = iota((160, 128), 0), iota((160, 128), 1)
        give_ref[b * 160 : (b + 1) * 160, :] = jnp.where(
            (held - 1 == col % 64) & (row % 2 == col // 64), 1.0, 0.0
        ).astype(BF16)
    for b in range(SLOTS // 128):
        block = slice(b * 128, (b + 1) * 128)
        take_ref[:, block] = jnp.transpose(give_ref[block, :].astype(F32)).astype(BF16)


def pack_kernel(c_ref, map_ref, fold_ref, out_ref):
    del fold_ref
    out_ref[...] = dot(map_ref[...], c_ref[...].astype(BF16)).astype(BF16)


def ocean_surface_kernel(in_ref, take_ref, give_ref, m_ref, first_ref, new_ref, back_ref):
    forcing = dot(take_ref[...], in_ref[...])
    wet = 0.25 * m_ref[...].astype(F32)
    news = []
    for f in range(2):
        new = first_ref[f] + wet * forcing[f * NR : (f + 1) * NR]
        new_ref[f] = new
        news.append(new)
    sea = jnp.concatenate(news, 0).astype(BF16)
    back_ref[...] = dot(give_ref[...], sea).astype(BF16)


WB = 8


def return_kernel(in_ref, scol_ref, w_hbm, out_ref, w_s, e_s, p_s, sems):
    def chunk(i):
        return pltpu.make_async_copy(w_hbm.at[pl.ds(i * WB, WB)], w_s.at[i], sems.at[i])

    for i in range(NR // WB):
        chunk(i).start()
    total = jnp.zeros((512, 128), F32)
    slot = scol_ref[...].astype(jnp.int32)
    for b in range(SLOTS // 128):
        hot = jnp.where(slot == iota((512, 128), 1) + b * 128, 1.0, 0.0).astype(BF16)
        total = total + dot(hot, in_ref[b * 128 : (b + 1) * 128, :])
    term = (iota((512, 128), 0) % 8) // 2
    e_s[...] = jnp.concatenate([jnp.where(term == t, total, 0.0) for t in range(TOP)], 1)

    def step(i, carry):
        chunk(i).wait()
        for k in range(WB):
            rows = pl.ds(pl.multiple_of((i * WB + k) * 8, 8), 8)
            p_s[rows, :] = dot(e_s[rows, :].astype(BF16), w_s[i, k].reshape(TOP * NC, NC))
        return carry

    lax.fori_loop(0, NR // WB, step, 0)
    r, c = iota((128, 512), 0), iota((128, 512), 1)
    gather = ((c // 8 == r % NR) & (c % 2 == r // NR)).astype(F32)
    done = jnp.dot(gather, p_s[...], preferred_element_type=F32, precision=lax.Precision.HIGHEST)
    for f in range(2):
        out_ref[f] = done[f * NR : (f + 1) * NR]


def shape(dims, dtype=F32):
    return jax.ShapeDtypeStruct(dims, dtype)


def shifted(x, axis, by):
    count = lax.axis_size(axis)
    return lax.ppermute(x, axis, [(i, (i + by) % count) for i in range(count)])


def per_device(atm_state, ocean_state, land_mask, elem_op, column_mix, kappa, remap_weight, intersection):
    gx, gy = lax.axis_index("gx"), lax.axis_index("gy")
    at = jnp.stack([gx, gy]).astype(jnp.int32)
    smem = pl.BlockSpec(memory_space=pltpu.SMEM)
    full = whole((PAY, NC))

    vmem = pl.BlockSpec(memory_space=pltpu.VMEM)
    hbm = pl.BlockSpec(memory_space=pl.ANY)

    def pinned(x):
        return pltpu.with_memory_space_constraint(x, pltpu.HBM)

    atm_in, ocean_in, mask_in = pinned(atm_state), pinned(ocean_state), pinned(land_mask)
    mix_in, elem_in = pinned(column_mix), pinned(elem_op)
    payload = shape((PAY, NC), BF16)
    rim, send_next, send_prev, element = pl.pallas_call(
        atm_rim_kernel,
        in_specs=[hbm] * 5,
        out_specs=[hbm] + [vmem] * 3,
        out_shape=[pltpu.HBM(atm_state.shape, F32), payload, payload, shape((512, 512), BF16)],
        scratch_shapes=[
            pltpu.VMEM((2, 2, LEV, 8, NC), F32),
            pltpu.VMEM((2, 2, LO, 8, NC), F32),
            pltpu.VMEM((NR, NC), jnp.int32),
            pltpu.VMEM((LEV, LEV), F32),
            pltpu.VMEM((16, 16), F32),
            pltpu.VMEM((2, 2, LEV, 8, NC), F32),
            pltpu.SemaphoreType.DMA((9,)),
        ],
        compiler_params=params(16),
        name="atm_rim",
    )(atm_in, ocean_in, mask_in, mix_in, elem_in)

    from_prev = shifted(send_next, "gx", 1)
    from_next = shifted(send_prev, "gx", -1)

    weights = remap_weight[:, 0]
    weights_in = pinned(weights)
    z, top_level, z_cols, ocean_cols, near_weights = pl.pallas_call(
        inner_kernel,
        in_specs=[hbm, hbm, hbm, vmem, vmem, hbm, hbm],
        out_specs=[hbm] + [vmem] * 4,
        out_shape=[pltpu.HBM(atm_state.shape, F32), shape((2, NR, NC)), shape((2, 144, NC)), shape((4, 128, NC)),
                   pltpu.VMEM(weights.shape, BF16)],
        scratch_shapes=[
            pltpu.VMEM((INNER, 2, LEV, 8, NC), F32),
            pltpu.VMEM(atm_state.shape, F32),
            pltpu.VMEM(ocean_state.shape, F32),
            pltpu.VMEM((LEV, LEV), F32),
            pltpu.SemaphoreType.DMA((2 * INNER,)),
            pltpu.SemaphoreType.DMA((5,)),
        ],
        input_output_aliases={5: 0},
        compiler_params=params(24),
        cost_estimate=pl.CostEstimate(flops=1000000000, bytes_accessed=14000000, transcendentals=0),
        name="inner",
    )(atm_in, mix_in, ocean_in, element, land_mask, rim, weights_in)

    send_south, send_north = pl.pallas_call(
        cols_kernel,
        out_shape=[shape((PAY, NC), BF16)] * 2,
        compiler_params=params(),
        name="cols",
    )(z_cols, ocean_cols, land_mask, from_prev, from_next)

    from_south = shifted(send_north, "gy", 1)
    from_north = shifted(send_south, "gy", -1)
    gx_count, gy_count = lax.axis_size("gx"), lax.axis_size("gy")
    top = gy_count - 1
    folded = lax.ppermute(
        send_north, ("gx", "gy"), [(i * gy_count + top, (gx_count - 1 - i) * gy_count + top) for i in range(gx_count)]
    )

    ids = jnp.transpose(intersection, (1, 2, 0)).reshape(32, 1024)
    send_map, slot_col = pl.pallas_call(
        send_map_kernel,
        in_specs=[smem, vmem],
        out_shape=[shape((SLOTS, 512), BF16), shape((512, 128))],
        compiler_params=params(),
        cost_estimate=pl.CostEstimate(flops=4000000, bytes_accessed=4200000, transcendentals=0),
        name="send_map",
    )(at, ids)

    surface = pl.pallas_call(
        surface_kernel,
        in_specs=[vmem] * 5,
        out_shape=shape((2, NR, NC), BF16),
        compiler_params=params(),
        name="surface",
    )(top_level, from_prev, from_next, from_south, from_north)

    products = lax.dot_general(
        near_weights, surface, (((3,), (2,)), ((0,), (1,))), preferred_element_type=F32
    )
    contrib = jnp.transpose(products, (0, 1, 3, 2)).reshape(2 * ENT, NC)
    outgoing = pl.pallas_call(
        pack_kernel,
        in_specs=[pl.BlockSpec(memory_space=pltpu.VMEM)] * 2 + [pl.BlockSpec(memory_space=pl.ANY)],
        out_shape=shape((SLOTS, NC), BF16),
        compiler_params=params(),
        name="pack",
    )(contrib, send_map, folded)
    incoming = lax.all_to_all(
        outgoing.reshape(TILES, CAP, 2, NC), ("gx", "gy"), split_axis=0, concat_axis=0, tiled=True
    ).reshape(SLOTS, NC)

    ocean_mid, first_level = pl.pallas_call(
        ocean_kernel,
        in_specs=[smem, smem, hbm] + [vmem] * 11,
        out_specs=[hbm, vmem],
        out_shape=[pltpu.HBM(ocean_state.shape, F32), shape((2, NR, NC))],
        scratch_shapes=[
            pltpu.VMEM((LO // OB, 2, OB, NR, NC), F32),
            pltpu.VMEM((4, 128, NC), F32),
            pltpu.VMEM((4, NR, NC), F32),
            pltpu.SemaphoreType.DMA((2 * (LO // OB),)),
        ],
        compiler_params=params(16),
        cost_estimate=pl.CostEstimate(flops=30000000, bytes_accessed=8000000, transcendentals=0),
        name="ocean",
    )(
        at[1:], kappa, ocean_in, land_mask, kappa, send_prev, send_next, send_south, send_north,
        from_prev, from_next, from_south, from_north, folded,
    )

    take, give = pl.pallas_call(
        receive_map_kernel,
        in_specs=[smem, vmem],
        out_shape=[shape((128, SLOTS), BF16), shape((SLOTS, 128), BF16)],
        compiler_params=params(),
        cost_estimate=pl.CostEstimate(flops=4000000, bytes_accessed=4200000, transcendentals=0),
        name="receive_map",
    )(at, ids)

    new_level, back_out = pl.pallas_call(
        ocean_surface_kernel,
        out_shape=[shape((2, NR, NC)), shape((SLOTS, NC), BF16)],
        compiler_params=params(),
        name="ocean_surface",
    )(incoming, take, give, land_mask, first_level)

    back_in = lax.all_to_all(
        back_out.reshape(TILES, CAP, 2, NC), ("gx", "gy"), split_axis=0, concat_axis=0, tiled=True
    ).reshape(SLOTS, NC)

    atm_next, ocean_next = pl.pallas_call(
        finish_kernel,
        in_specs=[hbm] + [vmem] * 5 + [hbm],
        out_specs=[hbm, hbm],
        out_shape=[pltpu.HBM(atm_state.shape, F32), pltpu.HBM(ocean_state.shape, F32)],
        input_output_aliases={6: 1},
        scratch_shapes=[
            pltpu.VMEM((LEV // FB, 2, FB, NR, NC), F32),
            pltpu.VMEM((LEV // FB, 2, FB, NR, NC), F32),
            pltpu.VMEM((4, 144, NC), F32),
            pltpu.SemaphoreType.DMA((2 * (LEV // FB),)),
            pltpu.SemaphoreType.DMA(()),
        ],
        compiler_params=params(16),
        cost_estimate=pl.CostEstimate(flops=20000000, bytes_accessed=9400000, transcendentals=0),
        name="finish",
    )(pinned(z), from_prev, from_next, from_south, from_north, new_level, ocean_mid)

    returned = pl.pallas_call(
        return_kernel,
        in_specs=[vmem, vmem, hbm],
        out_specs=vmem,
        out_shape=shape((2, NR, NC)),
        scratch_shapes=[
            pltpu.VMEM((NR // WB, WB, TOP, NC, NC), BF16),
            pltpu.VMEM((512, 512), F32),
            pltpu.VMEM((512, NC), F32),
            pltpu.SemaphoreType.DMA((NR // WB,)),
        ],
        compiler_params=params(16),
        name="returned",
    )(back_in, slot_col, weights_in)
    return atm_next, ocean_next, returned


def solution(mesh):
    placed = (
        P(None, None, "gx", "gy"),
        P(None, None, "gx", "gy"),
        P("gx", "gy"),
        P(),
        P(),
        P(),
        P("gx", "gy", None, None, None),
        P(),
    )
    return jax.shard_map(
        per_device,
        mesh=mesh,
        in_specs=placed,
        out_specs=(P(None, None, "gx", "gy"), P(None, None, "gx", "gy"), P(None, "gx", "gy")),
        check_vma=False,
    )
```

```python
import jax
import jax.numpy as jnp
from jax import lax
from jax.experimental import pallas as pl
from jax.experimental.pallas import tpu as pltpu
from jax.sharding import PartitionSpec as P

F32, BF16 = jnp.float32, jnp.bfloat16
LEV, LO, NR, NC = 72, 60, 64, 128
AT, O1, O2, MK, PAY = 0, 144, 272, 400, 416
OL = 2 * LO
TOP, CAP, TILES = 4, 5, 128
ENT = NR * TOP
SLOTS = TILES * CAP * 2
MIB = 1024 * 1024


def iota(shape, dim):
    return lax.broadcasted_iota(jnp.int32, shape, dim)


def dot(a, b):
    return jnp.dot(a, b, preferred_element_type=F32)


def params(mib=6):
    return pltpu.CompilerParams(vmem_limit_bytes=mib * MIB)


def whole(shape):
    return pl.BlockSpec(shape, lambda *_: (0,) * len(shape))


def mask_rows(first, second):
    place = iota((16, NC), 0)
    return jnp.where(place == 0, first, jnp.where(place == 1, second, 0.0)).astype(BF16)


def element_rows(x_s, mix, b):
    fields = [jnp.swapaxes(x_s[f], 0, 1) for f in range(2)]
    ys = []
    for big in range(2):
        for f in range(2):
            x = jnp.concatenate([fields[f][big * 4 + k] for k in range(4)], 1)
            ys.append(x + dot(mix, x.astype(BF16)))
    y = jnp.concatenate(ys, 0)
    z = y + dot(y.astype(BF16), b)
    pieces = [[], []]
    for r in range(8):
        for f in range(2):
            at = ((r // 4) * 2 + f) * LEV
            pieces[f].append(z[at : at + LEV, (r % 4) * NC : (r % 4 + 1) * NC])
    return pieces


def store_rows(z_ref, pieces, at):
    for f in range(2):
        z_ref[f, :, pl.ds(at, 8), :] = jnp.swapaxes(jnp.stack(pieces[f], 0), 0, 1)


def atm_rim_kernel(
    x_hbm, o_hbm, m_hbm, mix_hbm, elem_hbm, z_hbm, sn_ref, sp_ref, b_ref, x_s, o_s, m_s, mix_s, elem_s, z_s, sems
):
    sources = (elem_hbm, mix_hbm, x_hbm.at[:, :, pl.ds(0, 8), :], x_hbm.at[:, :, pl.ds(NR - 8, 8), :], m_hbm) + tuple(
        o_hbm.at[:, :, pl.ds(at, 8), :] for at in (0, NR - 8)
    )
    targets = (elem_s, mix_s, x_s.at[0], x_s.at[1], m_s, o_s.at[0], o_s.at[1])
    copies = [pltpu.make_async_copy(a, b, sems.at[k]) for k, (a, b) in enumerate(zip(sources, targets))]
    outs = [
        pltpu.make_async_copy(z_s.at[k], z_hbm.at[:, :, pl.ds(k * (NR - 8), 8), :], sems.at[7 + k]) for k in range(2)
    ]
    for copy in copies:
        copy.start()
    copies[0].wait()
    row = iota((512, 16), 0)
    spread_in = (iota((512, 16), 1) == (row // 128) * 4 + row % 4).astype(BF16)
    col = iota((16, 512), 1)
    spread_out = (iota((16, 512), 0) == (col // 128) * 4 + col % 4).astype(BF16)
    elem = (0.5 * elem_s[...]).astype(BF16)
    half = lax.dot_general(spread_in, elem, (((1,), (1,)), ((), ())), preferred_element_type=F32)
    spread = dot(half.astype(BF16), spread_out)
    same = (iota((512, 512), 0) % 128) // 4 == (iota((512, 512), 1) % 128) // 4
    b = jnp.where(same, spread, 0.0).astype(BF16)
    b_ref[...] = b
    copies[1].wait()
    mix = (0.5 * mix_s[...]).astype(BF16)
    for k, ref in ((0, sp_ref), (1, sn_ref)):
        copies[2 + k].wait()
        pieces = element_rows(x_s.at[k], mix, b)
        store_rows(z_s.at[k], pieces, 0)
        outs[k].start()
        ref[AT:O1, :] = jnp.concatenate([pieces[f][7 * k] for f in range(2)], 0).astype(BF16)
    for k in (4, 5, 6):
        copies[k].wait()
    m = m_s[...].astype(F32)
    for ref, k, first in ((sp_ref, 0, 0), (sn_ref, 1, 6)):
        rows = jnp.swapaxes(o_s[k].reshape(OL, 8, NC), 0, 1)
        at = k * (NR - 8) + first
        for j, base in ((0, O1), (1, O2)):
            u = rows[first + j] * m[at + j : at + j + 1]
            ref[base : base + 128, :] = jnp.concatenate([u, jnp.zeros((8, NC), F32)], 0).astype(BF16)
        ref[MK:PAY, :] = mask_rows(m[at : at + 1], m[at + 1 : at + 2])
    for copy in outs:
        copy.wait()


INNER = NR // 8 - 2


def pick_columns(columns):
    k, at = iota((8 * len(columns), 8 * NC), 0), iota((8 * len(columns), 8 * NC), 1)
    wanted = jnp.zeros_like(k)
    for j, c in enumerate(columns):
        wanted = jnp.where(k // 8 == j, c, wanted)
    return ((at // NC == k % 8) & (at % NC == wanted)).astype(BF16)


def take_columns(pick, tiles):
    side = jnp.concatenate([t.astype(BF16) for t in tiles], 1)
    got = lax.dot_general(pick, side, (((1,), (1,)), ((), ())), preferred_element_type=F32)
    return jnp.concatenate([got, jnp.zeros_like(got)], 1)


def inner_kernel(
    x_hbm, mix_hbm, o_hbm, b_ref, m_ref, rim_hbm, z_hbm, top_ref, zc_ref, oc_ref,
    x_s, z_s, o_s, mix_s, sems, rest,
):
    mix_copy = pltpu.make_async_copy(mix_hbm, mix_s, rest.at[0])
    ocean_copy = pltpu.make_async_copy(o_hbm, o_s, rest.at[1])
    rims = [
        pltpu.make_async_copy(
            rim_hbm.at[:, :, pl.ds(at, 8), :], z_s.at[:, :, pl.ds(at, 8), :], rest.at[2 + k]
        )
        for k, at in enumerate((0, NR - 8))
    ]

    def chunk(i):
        return pltpu.make_async_copy(x_hbm.at[:, :, pl.ds(i * 8 + 8, 8), :], x_s.at[i], sems.at[i])

    def leave(i):
        rows = pl.ds(pl.multiple_of(i * 8 + 8, 8), 8)
        return pltpu.make_async_copy(z_s.at[:, :, rows, :], z_hbm.at[:, :, rows, :], sems.at[INNER + i])

    mix_copy.start()
    for i in range(INNER):
        chunk(i).start()
    for copy in rims:
        copy.start()
    ocean_copy.start()
    mix_copy.wait()
    mix = (0.5 * mix_s[...]).astype(BF16)

    def step(i, carry):
        chunk(i).wait()
        store_rows(z_s, element_rows(x_s.at[i], mix, b_ref[...]), pl.multiple_of(i * 8 + 8, 8))
        leave(i).start()
        return carry

    lax.fori_loop(0, INNER, step, 0)
    for copy in rims:
        copy.wait()
    pick = pick_columns((0, NC - 1))

    def atm(i, carry):
        for f in range(2):
            got = take_columns(pick, [z_s[f, i * 8 + l] for l in range(8)])
            at = pl.multiple_of(f * LEV + i * 8, 8)
            for k in range(2):
                zc_ref[k, pl.ds(at, 8), :] = got[k * 8 : k * 8 + 8]
        return carry

    lax.fori_loop(0, LEV // 8, atm, 0, unroll=3)
    for f in range(2):
        top_ref[f] = z_s[f, LEV - 1]
    ocean_copy.wait()
    wet = m_ref[...].astype(F32)
    pick = pick_columns((0, 1, NC - 2, NC - 1))

    def ocean(i, carry):
        tiles = [i * 8 + l for l in range(8)]
        got = take_columns(pick, [wet * o_s[t // LO, t % LO] for t in tiles])
        for k in range(4):
            oc_ref[k, pl.ds(pl.multiple_of(i * 8, 8), 8), :] = got[k * 8 : k * 8 + 8]
        return carry

    lax.fori_loop(0, OL // 8, ocean, 0, unroll=3)
    oc_ref[:, OL:, :] = jnp.zeros((4, 8, NC), F32)
    for i in range(INNER):
        leave(i).wait()


def cols_kernel(zc_ref, oc_ref, m_ref, rp_ref, rn_ref, ss_ref, sn_ref):
    lane = iota((144, NC), 1)
    place = lane % 4
    rp_at, rn_at = rp_ref[AT:O1, :].astype(F32), rn_ref[AT:O1, :].astype(F32)
    before, after = rp_ref[O2:MK, :].astype(F32), rn_ref[O1:O2, :].astype(F32)
    olane = iota((128, NC), 1)
    row = iota((64, NC), 0)
    m_before, m_after = rp_ref[MK:PAY, :].astype(F32)[1:2], rn_ref[MK:PAY, :].astype(F32)[0:1]
    tail = jnp.where(row == 0, m_before, jnp.where(row == 1, m_after, 0.0))
    m_t = jnp.transpose(jnp.concatenate([m_ref[...].astype(F32), tail], 0))
    for ref, c_at, ocs in ((ss_ref, 0, (0, 1)), (sn_ref, 127, (126, 127))):
        z = zc_ref[0 if c_at == 0 else 1]
        nxt = jnp.where(lane == 63, rn_at[:, c_at : c_at + 1], pltpu.roll(z, 127, 1))
        prv = jnp.where(lane == 0, rp_at[:, c_at : c_at + 1], pltpu.roll(z, 1, 1))
        z = jnp.where(place == 3, (z + nxt) * 0.5, jnp.where(place == 0, (z + prv) * 0.5, z))
        ref[AT:O1, :] = z.astype(BF16)
        for k, c in enumerate(ocs):
            source = c if c < 2 else c - 124
            u = jnp.where(
                olane < 64,
                oc_ref[source],
                jnp.where(olane == 64, before[:, c : c + 1], jnp.where(olane == 65, after[:, c : c + 1], 0.0)),
            )
            base = (O1, O2)[k]
            ref[base : base + 128, :] = u.astype(BF16)
        ref[MK:PAY, :] = mask_rows(m_t[ocs[0] : ocs[0] + 1], m_t[ocs[1] : ocs[1] + 1])


def averaged(z, nxt, prv, place):
    return jnp.where(place == 3, (z + nxt) * 0.5, jnp.where(place == 0, (z + prv) * 0.5, z))


def stiffness(z, h_prev, h_next, c_south, c_north):
    row, lane = iota((NR, NC), 0), iota((NR, NC), 1)
    nxt = jnp.where(row == NR - 1, h_next, pltpu.roll(z, NR - 1, 0))
    prv = jnp.where(row == 0, h_prev, pltpu.roll(z, 1, 0))
    z = averaged(z, nxt, prv, row % 4)
    nxt = jnp.where(lane == NC - 1, c_north, pltpu.roll(z, NC - 1, 1))
    prv = jnp.where(lane == 0, c_south, pltpu.roll(z, 1, 1))
    return averaged(z, nxt, prv, lane % 4)


def surface_kernel(z_ref, rp_ref, rn_ref, cs_ref, cn_ref, fold_ref, s_ref):
    del fold_ref
    rp, rn = rp_ref[AT:O1, :].astype(F32), rn_ref[AT:O1, :].astype(F32)
    cs, cn = cs_ref[AT:O1, :].astype(F32), cn_ref[AT:O1, :].astype(F32)
    for f in range(2):
        top = f * LEV + LEV - 8
        south = jnp.transpose(cs[top : top + 8])[:NR, 7:8]
        north = jnp.transpose(cn[top : top + 8])[:NR, 7:8]
        last = top + 7
        s = stiffness(z_ref[f], rp[last : last + 1], rn[last : last + 1], south, north)
        s_ref[f] = s.astype(BF16)


def edge_spread(tiles, scale):
    k, c = iota((2 * tiles, tiles * NC), 0), iota((2 * tiles, tiles * NC), 1)
    mine = k % tiles == c // NC
    end = c % NC == jnp.where(k < tiles, 0, NC - 1)
    return jnp.where(mine & end, scale, 0.0).astype(BF16)


def add_ends(x, first, last):
    row = iota((8, NC), 0)
    return jnp.concatenate(
        [
            x[0:8] + jnp.where(row == 0, first, 0.0),
            x[8 : NR - 8],
            x[NR - 8 :] + jnp.where(row == 7, last, 0.0),
        ],
        0,
    )


def column_halo(columns, spread):
    return lax.dot_general(columns, spread, (((0,), (0,)), ((), ())), preferred_element_type=F32)[:NR]


FB = 8


def finish_kernel(
    z_hbm, rp_ref, rn_ref, cs_ref, cn_ref, new_ref, mid_hbm, o_hbm, ocean_hbm, z_s, o_s, h_ref, sems, level_sem
):
    del mid_hbm
    level = pltpu.make_async_copy(new_ref, ocean_hbm.at[:, 0], level_sem)
    level.start()

    def enter(i):
        return pltpu.make_async_copy(z_hbm.at[:, pl.ds(i * FB, FB)], z_s.at[i], sems.at[LEV // FB + i])

    for i in range(LEV // FB):
        enter(i).start()
    for k, ref in enumerate((rp_ref, rn_ref, cs_ref, cn_ref)):
        h_ref[k] = ref[AT:O1, :].astype(F32)
    spread = edge_spread(2 * FB, 0.5)
    row, lane = iota((NR, NC), 0), iota((NR, NC), 1)

    def weights(place, at, end):
        low = jnp.where((place == 0) & (at != 0), 0.5, 0.0)
        high = jnp.where((place == 3) & (at != end), 0.5, 0.0)
        return jnp.where((place == 0) | (place == 3), 0.5, 1.0), low, high

    own_r, low_r, high_r = weights(row % 4, row, NR - 1)
    own_c, low_c, high_c = weights(lane % 4, lane, NC - 1)

    def chunk(i):
        return pltpu.make_async_copy(o_s.at[i], o_hbm.at[:, pl.ds(i * FB, FB)], sems.at[i])

    def step(i, carry):
        enter(i).wait()

        def halo(k, f):
            return h_ref[k, pl.ds(pl.multiple_of(f * LEV + i * FB, 8), FB), :]

        columns = jnp.concatenate([halo(2, 0), halo(2, 1), halo(3, 0), halo(3, 1)], 0).astype(BF16)
        edges = column_halo(columns, spread)
        for f in range(2):
            first, last = 0.5 * halo(0, f), 0.5 * halo(1, f)
            for l in range(FB):
                t = z_s[i, f, l]
                t = own_r * t + high_r * pltpu.roll(t, NR - 1, 0) + low_r * pltpu.roll(t, 1, 0)
                t = add_ends(t, first[l : l + 1], last[l : l + 1])
                t = own_c * t + high_c * pltpu.roll(t, NC - 1, 1) + low_c * pltpu.roll(t, 1, 1)
                tile = f * FB + l
                o_s[i, f, l] = t + edges[:, tile * NC : (tile + 1) * NC]
        chunk(i).start()
        return carry

    lax.fori_loop(0, LEV // FB, step, 0)
    level.wait()
    for i in range(LEV // FB):
        chunk(i).wait()


OB = 12


def ocean_kernel(
    at_ref, k_ref, o_hbm, m_ref, kc_ref, sp_ref, sn_ref, ss_ref, st_ref, rp_ref, rn_ref, cs_ref, cn_ref, fo_ref,
    out_hbm, first_ref, out_s, row_ref, col_ref, sems,
):
    def enter(i):
        return pltpu.make_async_copy(o_hbm.at[:, pl.ds(i * OB, OB)], out_s.at[i], sems.at[LO // OB + i])

    for i in range(LO // OB):
        enter(i).start()
    is_top, is_low = at_ref[0] == 7, at_ref[0] == 0
    lane = iota((128, NC), 1)

    def part(ref, base):
        return ref[base : base + 128, :].astype(F32)

    def masks(ref):
        m = ref[MK:PAY, :].astype(F32)
        return m[0:1], m[1:2]

    fr, fc = iota((NC, NC), 0), iota((NC, NC), 1)
    flip = (((fr < 64) & (fc == 63 - fr)) | ((fr == 64) & (fc == 65)) | ((fr == 65) & (fc == 64))).astype(BF16)
    turned = dot(fo_ref[...], flip)
    n0 = jnp.where(is_top, turned[O2:MK], part(cn_ref, O1))
    n1 = jnp.where(is_top, turned[O1:O2], part(cn_ref, O2))
    mc0, mc1 = masks(cn_ref)
    mn0 = jnp.where(is_top, turned[MK + 1 : MK + 2], mc0)
    mn1 = jnp.where(is_top, turned[MK : MK + 1], mc1)
    keep = jnp.where(is_low, 0.0, 1.0)
    s2, s1 = part(cs_ref, O1) * keep, part(cs_ref, O2) * keep
    ms2, ms1 = masks(cs_ref)
    ms2, ms1 = ms2 * keep, ms1 * keep
    um2, um1 = part(rp_ref, O1), part(rp_ref, O2)
    mm2, mm1 = masks(rp_ref)
    u64, u65 = part(rn_ref, O1), part(rn_ref, O2)
    m64, m65 = masks(rn_ref)
    own0, own63 = part(sp_ref, O1), part(sn_ref, O2)
    mo0, mo63 = masks(sp_ref)[0], masks(sn_ref)[1]
    west0, east127 = part(ss_ref, O1), part(st_ref, O2)
    mw0, me127 = masks(ss_ref)[0], masks(st_ref)[1]
    at, l60 = iota((128, LO), 0), iota((128, LO), 1)
    kap = sum(
        jnp.sum(jnp.where(at - f * LO == l60, kc_ref[f : f + 1, :], 0.0), 1, keepdims=True) for f in range(2)
    )

    def along(u, low, high, end):
        where = lane[: u.shape[0]]
        return jnp.where(where == end, high, pltpu.roll(u, 127, 1)) + jnp.where(
            where == 0, low, pltpu.roll(u, 1, 1)
        )

    def advance(u, wet, inner, outer, m_inner, m_outer, low, high, m_low, m_high, end):
        total = inner + outer + along(u, low, high, end)
        m8 = jnp.broadcast_to(wet, (8, NC))
        count = m_inner + m_outer + along(m8, m_low, m_high, end)[0:1]
        return u + kap * (wet * total - count * u)

    def corner(x, at):
        return x[:, at : at + 1]

    row_ref[0] = um1
    row_ref[1] = u64
    row_ref[2] = advance(
        um1, mm1, own0, um2, mo0, mm2, corner(s1, 64), corner(n0, 64), corner(ms1, 64), corner(mn0, 64), 127
    )
    row_ref[3] = advance(
        u64, m64, own63, u65, mo63, m65, corner(s1, 65), corner(n0, 65), corner(ms1, 65), corner(mn0, 65), 127
    )
    west = advance(
        s1, ms1, west0, s2, mw0, ms2, corner(s1, 64), corner(s1, 65), corner(ms1, 64), corner(ms1, 65), 63
    )
    east = advance(
        n0, mn0, east127, n1, me127, mn1, corner(n0, 64), corner(n0, 65), corner(mn0, 64), corner(mn0, 65), 63
    )
    here = iota((NR, NC), 1)
    for sub, (low, high) in enumerate(((s1, n0), (west, east))):
        low, high = jnp.transpose(low)[:NR], jnp.transpose(high)[:NR]
        for f in range(2):
            col_ref[2 * sub + f] = jnp.where(
                here < 64, pltpu.roll(low, (NC - LO * f) % NC, 1), pltpu.roll(high, (NC + 64 - LO * f) % NC, 1)
            )
    a, b = iota((NC, NC), 0), iota((NC, NC), 1)
    ends = ((a == 0) & (b == 0)) | ((a == 64) & (b == NC - 1))
    ns = jnp.concatenate([(jnp.abs(a - b) == 1).astype(BF16), ends.astype(BF16)], 0)
    wet = m_ref[...].astype(F32)
    r, c = iota((NR, NC), 0), iota((NR, NC), 1)
    m_north = jnp.transpose(jnp.broadcast_to(mn0, (8, NC)))[:NR, 0:1]
    m_south = jnp.transpose(jnp.broadcast_to(ms1, (8, NC)))[:NR, 0:1]
    count = jnp.where(r == NR - 1, m64, pltpu.roll(wet, NR - 1, 0)) + jnp.where(
        r == 0, mm1, pltpu.roll(wet, 1, 0)
    )
    count = count + jnp.where(c == NC - 1, m_north, pltpu.roll(wet, NC - 1, 1))
    count = count + jnp.where(c == 0, m_south, pltpu.roll(wet, 1, 1))

    places = [(f, l) for f in range(2) for l in range(OB)]

    def chunk(i):
        return pltpu.make_async_copy(out_s.at[i], out_hbm.at[:, pl.ds(i * OB, OB)], sems.at[i])

    def step(i, carry):
        enter(i).wait()
        ts = [out_s[i, f, l] for f, l in places]
        for sub in range(2):
            us = [wet * t for t in ts]
            halos = [pltpu.roll(col_ref[2 * sub + f], (NC - i * OB - l) % NC, 1) for f, l in places]
            side = jnp.concatenate([jnp.concatenate(us, 0), jnp.concatenate(halos, 0)], 1)
            cols = dot(side.astype(BF16), ns)
            for j, (f, l) in enumerate(places):
                level = i * OB + l
                here = pl.ds(f * LO + level, 1)
                u = us[j]
                total = pltpu.roll(u, NR - 1, 0) + pltpu.roll(u, 1, 0) + cols[j * NR : (j + 1) * NR]
                total = add_ends(
                    total, row_ref[2 * sub, here, :] - u[NR - 1 :], row_ref[2 * sub + 1, here, :] - u[0:1]
                )
                ts[j] = ts[j] + (k_ref[f, level] * wet) * (total - count * ts[j])
        for j, (f, l) in enumerate(places):
            out_s[i, f, l] = ts[j]
        chunk(i).start()
        return carry

    lax.fori_loop(0, LO // OB, step, 0)
    for f in range(2):
        first_ref[f] = out_s[0, f, 0]
    for i in range(LO // OB):
        chunk(i).wait()


def send_map_kernel(at_ref, ids_ref, w_hbm, out_ref, scol_ref, w_ref, sems):
    parts = w_hbm.shape[0] // WB
    copies = [
        pltpu.make_async_copy(w_hbm.at[pl.ds(i * WB, WB)], w_ref.at[pl.ds(i * WB, WB)], sems.at[i])
        for i in range(parts)
    ]
    for copy in copies:
        copy.start()
    gx, gy = at_ref[0], at_ref[1]
    block = ids_ref[:, pl.ds(pl.multiple_of((gx // 2) * 128, 128), 128)]
    block = pltpu.roll(block, (gx % 2) * 64, 1)
    rows = iota((32, 128), 0)
    tile_row, lane = iota((128, 128), 0), iota((128, 128), 1)
    before = (tile_row < lane).astype(BF16)
    ones = jnp.ones((128, 128), BF16)
    earlier = jnp.zeros((128, 128), F32)
    tiles, ranks = [], []
    for t in range(TOP):
        ids = jnp.sum(jnp.where(rows == gy * 4 + t, block, 0), 0, keepdims=True)
        hit = (ids // 64 == tile_row) & (lane < 64)
        hot = hit.astype(BF16)
        rank = dot(hot, before) + earlier
        earlier = earlier + dot(hot, ones)
        ranks.append(jnp.sum(jnp.where(hit, rank, 0.0), 0, keepdims=True))
        tiles.append((ids // 64).astype(F32))
    place = iota((8, 128), 0)
    stack = jnp.zeros((8, 128), F32)
    for t in range(TOP):
        stack = jnp.where(place == t, tiles[t], jnp.where(place == t + 4, ranks[t], stack))
    spread = (iota((128, 512), 1) // 8 == iota((128, 512), 0)).astype(BF16)
    wide = dot(stack.astype(BF16), spread)
    col, row8 = iota((8, 512), 1), iota((8, 512), 0)
    wide = jnp.where(row8 % 4 == (col // 2) % 4, wide * jnp.where(row8 < 4, 10.0, 2.0), 0.0)
    slot = jnp.sum(wide, 0, keepdims=True) + (iota((1, 512), 1) % 2).astype(F32)
    out_ref[...] = jnp.where(slot.astype(jnp.int32) == iota((SLOTS, 512), 0), 1.0, 0.0).astype(BF16)
    scol_ref[...] = jnp.transpose(jnp.broadcast_to(slot, (128, 512)))
    for copy in copies:
        copy.wait()


def receive_map_kernel(at_ref, ids_ref, take_ref, give_ref):
    own_tile = at_ref[0] * 8 + at_ref[1]
    blocks = 8
    row, lane = iota((128, 128), 0), iota((128, 128), 1)
    halves = (row // 64) == (lane // 64)
    before = jnp.concatenate([(halves & (row < lane)).astype(BF16), halves.astype(BF16)], 1)
    r, c = iota((256, 256), 0), iota((256, 256), 1)
    lower = ((r // 4 == c // 4) & (c % 4 < r % 4)).astype(BF16)
    sr, sc = iota((160, 160), 0), iota((160, 160), 1)
    pick = (((sr // 10) % 8 == (sc % 32) // 4) & ((sr % 10) // 2 == sc // 32)).astype(BF16)
    side = iota((160, NC), 0) // 80 == iota((160, NC), 1) // 64
    ids = jnp.concatenate([ids_ref[:, b * NC : (b + 1) * NC] for b in range(blocks)], 0)
    hit = ids // 64 == own_tile
    counts = dot(hit.astype(BF16), before)
    rank = counts[:, 0:NC] + dot(lower, counts[:, NC:].astype(BF16))
    value = (ids % 64 + 1).astype(F32)
    held = [jnp.where(hit & (rank == float(k)), value, 0.0) for k in range(CAP)]
    stacked = jnp.concatenate(
        [jnp.concatenate([h[b * 32 : (b + 1) * 32] for h in held], 0) for b in range(blocks)], 1
    )
    found = dot(pick, stacked.astype(BF16))
    found = jnp.concatenate(
        [jnp.where(side, found[:, b * NC : (b + 1) * NC], 0.0) for b in range(blocks)], 0
    )
    local = dot(found.astype(BF16), jnp.ones((NC, NC), BF16)).astype(jnp.int32)
    row, col = iota((SLOTS, NC), 0), iota((SLOTS, NC), 1)
    give = jnp.where((local - 1 == col % 64) & (row % 2 == col // 64), 1.0, 0.0)
    give_ref[...] = give.astype(BF16)
    for b in range(SLOTS // NC):
        take_ref[:, b * NC : (b + 1) * NC] = jnp.transpose(give[b * NC : (b + 1) * NC]).astype(BF16)


def pack_kernel(c_ref, map_ref, out_ref):
    out_ref[...] = dot(map_ref[...], c_ref[...].astype(BF16)).astype(BF16)


def ocean_surface_kernel(in_ref, take_ref, give_ref, m_ref, first_ref, new_ref, back_ref):
    forcing = dot(take_ref[...], in_ref[...])
    wet = 0.25 * m_ref[...].astype(F32)
    news = []
    for f in range(2):
        new = first_ref[f] + wet * forcing[f * NR : (f + 1) * NR]
        new_ref[f] = new
        news.append(new)
    sea = jnp.concatenate(news, 0).astype(BF16)
    back_ref[...] = dot(give_ref[...], sea).astype(BF16)


WB = 8


def return_kernel(in_ref, scol_ref, w_hbm, out_ref, w_s, e_s, p_s, sems):
    def chunk(i):
        return pltpu.make_async_copy(w_hbm.at[pl.ds(i * WB, WB)], w_s.at[i], sems.at[i])

    for i in range(NR // WB):
        chunk(i).start()
    total = jnp.zeros((512, 128), F32)
    slot = scol_ref[...].astype(jnp.int32)
    for b in range(SLOTS // 128):
        hot = jnp.where(slot == iota((512, 128), 1) + b * 128, 1.0, 0.0).astype(BF16)
        total = total + dot(hot, in_ref[b * 128 : (b + 1) * 128, :])
    term = (iota((512, 128), 0) % 8) // 2
    e_s[...] = jnp.concatenate([jnp.where(term == t, total, 0.0) for t in range(TOP)], 1)

    def step(i, carry):
        chunk(i).wait()
        for k in range(WB):
            rows = pl.ds(pl.multiple_of((i * WB + k) * 8, 8), 8)
            p_s[rows, :] = dot(e_s[rows, :].astype(BF16), w_s[i, k].reshape(TOP * NC, NC))
        return carry

    lax.fori_loop(0, NR // WB, step, 0)
    r, c = iota((128, 512), 0), iota((128, 512), 1)
    gather = ((c // 8 == r % NR) & (c % 2 == r // NR)).astype(F32)
    done = jnp.dot(gather, p_s[...], preferred_element_type=F32, precision=lax.Precision.HIGHEST)
    for f in range(2):
        out_ref[f] = done[f * NR : (f + 1) * NR]


def shape(dims, dtype=F32):
    return jax.ShapeDtypeStruct(dims, dtype)


def shifted(x, axis, by):
    count = lax.axis_size(axis)
    return lax.ppermute(x, axis, [(i, (i + by) % count) for i in range(count)])


def per_device(atm_state, ocean_state, land_mask, elem_op, column_mix, kappa, remap_weight, intersection):
    gx, gy = lax.axis_index("gx"), lax.axis_index("gy")
    at = jnp.stack([gx, gy]).astype(jnp.int32)
    smem = pl.BlockSpec(memory_space=pltpu.SMEM)
    full = whole((PAY, NC))

    vmem = pl.BlockSpec(memory_space=pltpu.VMEM)
    hbm = pl.BlockSpec(memory_space=pl.ANY)

    def pinned(x):
        return pltpu.with_memory_space_constraint(x, pltpu.HBM)

    atm_in, ocean_in, mask_in = pinned(atm_state), pinned(ocean_state), pinned(land_mask)
    mix_in, elem_in = pinned(column_mix), pinned(elem_op)
    payload = shape((PAY, NC), BF16)
    rim, send_next, send_prev, element = pl.pallas_call(
        atm_rim_kernel,
        in_specs=[hbm] * 5,
        out_specs=[hbm] + [vmem] * 3,
        out_shape=[pltpu.HBM(atm_state.shape, F32), payload, payload, shape((512, 512), BF16)],
        scratch_shapes=[
            pltpu.VMEM((2, 2, LEV, 8, NC), F32),
            pltpu.VMEM((2, 2, LO, 8, NC), F32),
            pltpu.VMEM((NR, NC), jnp.int32),
            pltpu.VMEM((LEV, LEV), F32),
            pltpu.VMEM((16, 16), F32),
            pltpu.VMEM((2, 2, LEV, 8, NC), F32),
            pltpu.SemaphoreType.DMA((9,)),
        ],
        compiler_params=params(16),
        name="atm_rim",
    )(atm_in, ocean_in, mask_in, mix_in, elem_in)

    from_prev = shifted(send_next, "gx", 1)
    from_next = shifted(send_prev, "gx", -1)

    weights = remap_weight[:, 0]
    weights_in = pinned(weights)
    z, top_level, z_cols, ocean_cols = pl.pallas_call(
        inner_kernel,
        in_specs=[hbm, hbm, hbm, vmem, vmem, hbm],
        out_specs=[hbm] + [vmem] * 3,
        out_shape=[pltpu.HBM(atm_state.shape, F32), shape((2, NR, NC)), shape((2, 144, NC)), shape((4, 128, NC))],
        scratch_shapes=[
            pltpu.VMEM((INNER, 2, LEV, 8, NC), F32),
            pltpu.VMEM(atm_state.shape, F32),
            pltpu.VMEM(ocean_state.shape, F32),
            pltpu.VMEM((LEV, LEV), F32),
            pltpu.SemaphoreType.DMA((2 * INNER,)),
            pltpu.SemaphoreType.DMA((4,)),
        ],
        input_output_aliases={5: 0},
        compiler_params=params(24),
        cost_estimate=pl.CostEstimate(flops=1000000000, bytes_accessed=14000000, transcendentals=0),
        name="inner",
    )(atm_in, mix_in, ocean_in, element, land_mask, rim)

    send_south, send_north = pl.pallas_call(
        cols_kernel,
        out_shape=[shape((PAY, NC), BF16)] * 2,
        compiler_params=params(),
        name="cols",
    )(z_cols, ocean_cols, land_mask, from_prev, from_next)

    from_south = shifted(send_north, "gy", 1)
    from_north = shifted(send_south, "gy", -1)
    gx_count, gy_count = lax.axis_size("gx"), lax.axis_size("gy")
    top = gy_count - 1
    folded = lax.ppermute(
        send_north, ("gx", "gy"), [(i * gy_count + top, (gx_count - 1 - i) * gy_count + top) for i in range(gx_count)]
    )

    ids = jnp.transpose(intersection, (1, 2, 0)).reshape(32, 1024)
    send_map, slot_col, near_weights = pl.pallas_call(
        send_map_kernel,
        in_specs=[smem, vmem, hbm],
        out_specs=[vmem] * 3,
        out_shape=[shape((SLOTS, 512), BF16), shape((512, 128)), pltpu.VMEM(weights.shape, BF16)],
        scratch_shapes=[pltpu.SemaphoreType.DMA((NR // WB,))],
        compiler_params=params(),
        cost_estimate=pl.CostEstimate(flops=4000000, bytes_accessed=9000000, transcendentals=0),
        name="send_map",
    )(at, ids, weights_in)

    surface = pl.pallas_call(
        surface_kernel,
        in_specs=[vmem] * 5 + [hbm],
        out_shape=shape((2, NR, NC), BF16),
        compiler_params=params(),
        name="surface",
    )(top_level, from_prev, from_next, from_south, from_north, folded)

    products = lax.dot_general(
        near_weights, surface, (((3,), (2,)), ((0,), (1,))), preferred_element_type=F32
    )
    contrib = jnp.transpose(products, (0, 1, 3, 2)).reshape(2 * ENT, NC)
    outgoing = pl.pallas_call(
        pack_kernel,
        out_shape=shape((SLOTS, NC), BF16),
        compiler_params=params(),
        name="pack",
    )(contrib, send_map)
    incoming = lax.all_to_all(
        outgoing.reshape(TILES, CAP, 2, NC), ("gx", "gy"), split_axis=0, concat_axis=0, tiled=True
    ).reshape(SLOTS, NC)

    ocean_mid, first_level = pl.pallas_call(
        ocean_kernel,
        in_specs=[smem, smem, hbm] + [vmem] * 11,
        out_specs=[hbm, vmem],
        out_shape=[pltpu.HBM(ocean_state.shape, F32), shape((2, NR, NC))],
        scratch_shapes=[
            pltpu.VMEM((LO // OB, 2, OB, NR, NC), F32),
            pltpu.VMEM((4, 128, NC), F32),
            pltpu.VMEM((4, NR, NC), F32),
            pltpu.SemaphoreType.DMA((2 * (LO // OB),)),
        ],
        compiler_params=params(16),
        cost_estimate=pl.CostEstimate(flops=30000000, bytes_accessed=8000000, transcendentals=0),
        name="ocean",
    )(
        at[1:], kappa, ocean_in, land_mask, kappa, send_prev, send_next, send_south, send_north,
        from_prev, from_next, from_south, from_north, folded,
    )

    take, give = pl.pallas_call(
        receive_map_kernel,
        in_specs=[smem, vmem],
        out_shape=[shape((128, SLOTS), BF16), shape((SLOTS, 128), BF16)],
        compiler_params=params(),
        cost_estimate=pl.CostEstimate(flops=4000000, bytes_accessed=4200000, transcendentals=0),
        name="receive_map",
    )(at, ids)

    new_level, back_out = pl.pallas_call(
        ocean_surface_kernel,
        out_shape=[shape((2, NR, NC)), shape((SLOTS, NC), BF16)],
        compiler_params=params(),
        name="ocean_surface",
    )(incoming, take, give, land_mask, first_level)

    back_in = lax.all_to_all(
        back_out.reshape(TILES, CAP, 2, NC), ("gx", "gy"), split_axis=0, concat_axis=0, tiled=True
    ).reshape(SLOTS, NC)

    atm_next, ocean_next = pl.pallas_call(
        finish_kernel,
        in_specs=[hbm] + [vmem] * 5 + [hbm],
        out_specs=[hbm, hbm],
        out_shape=[pltpu.HBM(atm_state.shape, F32), pltpu.HBM(ocean_state.shape, F32)],
        input_output_aliases={6: 1},
        scratch_shapes=[
            pltpu.VMEM((LEV // FB, 2, FB, NR, NC), F32),
            pltpu.VMEM((LEV // FB, 2, FB, NR, NC), F32),
            pltpu.VMEM((4, 144, NC), F32),
            pltpu.SemaphoreType.DMA((2 * (LEV // FB),)),
            pltpu.SemaphoreType.DMA(()),
        ],
        compiler_params=params(16),
        cost_estimate=pl.CostEstimate(flops=20000000, bytes_accessed=9400000, transcendentals=0),
        name="finish",
    )(pinned(z), from_prev, from_next, from_south, from_north, new_level, ocean_mid)

    returned = pl.pallas_call(
        return_kernel,
        in_specs=[vmem, vmem, hbm],
        out_specs=vmem,
        out_shape=shape((2, NR, NC)),
        scratch_shapes=[
            pltpu.VMEM((NR // WB, WB, TOP, NC, NC), BF16),
            pltpu.VMEM((512, 512), F32),
            pltpu.VMEM((512, NC), F32),
            pltpu.SemaphoreType.DMA((NR // WB,)),
        ],
        compiler_params=params(16),
        name="returned",
    )(back_in, slot_col, weights_in)
    return atm_next, ocean_next, returned


def solution(mesh):
    placed = (
        P(None, None, "gx", "gy"),
        P(None, None, "gx", "gy"),
        P("gx", "gy"),
        P(),
        P(),
        P(),
        P("gx", "gy", None, None, None),
        P(),
    )
    return jax.shard_map(
        per_device,
        mesh=mesh,
        in_specs=placed,
        out_specs=(P(None, None, "gx", "gy"), P(None, None, "gx", "gy"), P(None, "gx", "gy")),
        check_vma=False,
    )
```

```python
import jax
import jax.numpy as jnp
from jax import lax
from jax.experimental import pallas as pl
from jax.experimental.pallas import tpu as pltpu
from jax.sharding import PartitionSpec as P

F32, BF16 = jnp.float32, jnp.bfloat16
LEV, LO, NR, NC = 72, 60, 64, 128
AT, O1, O2, MK, PAY = 0, 144, 272, 400, 416
OL = 2 * LO
TOP, CAP, TILES = 4, 5, 128
ENT = NR * TOP
SLOTS = TILES * CAP * 2
MIB = 1024 * 1024


def iota(shape, dim):
    return lax.broadcasted_iota(jnp.int32, shape, dim)


def dot(a, b):
    return jnp.dot(a, b, preferred_element_type=F32)


def params(mib=6):
    return pltpu.CompilerParams(vmem_limit_bytes=mib * MIB)


def whole(shape):
    return pl.BlockSpec(shape, lambda *_: (0,) * len(shape))


def mask_rows(first, second):
    place = iota((16, NC), 0)
    return jnp.where(place == 0, first, jnp.where(place == 1, second, 0.0)).astype(BF16)


def element_rows(x_s, mix, b):
    fields = [jnp.swapaxes(x_s[f], 0, 1) for f in range(2)]
    ys = []
    for big in range(2):
        for f in range(2):
            x = jnp.concatenate([fields[f][big * 4 + k] for k in range(4)], 1)
            ys.append(x + dot(mix, x.astype(BF16)))
    y = jnp.concatenate(ys, 0)
    z = y + dot(y.astype(BF16), b)
    pieces = [[], []]
    for r in range(8):
        for f in range(2):
            at = ((r // 4) * 2 + f) * LEV
            pieces[f].append(z[at : at + LEV, (r % 4) * NC : (r % 4 + 1) * NC])
    return pieces


def store_rows(z_ref, pieces, at):
    for f in range(2):
        z_ref[f, :, pl.ds(at, 8), :] = jnp.swapaxes(jnp.stack(pieces[f], 0), 0, 1)


def atm_rim_kernel(
    x_hbm, o_hbm, m_hbm, mix_hbm, elem_hbm, z_hbm, sn_ref, sp_ref, b_ref, x_s, o_s, m_s, mix_s, elem_s, z_s, sems
):
    sources = (elem_hbm, mix_hbm, x_hbm.at[:, :, pl.ds(0, 8), :], x_hbm.at[:, :, pl.ds(NR - 8, 8), :], m_hbm) + tuple(
        o_hbm.at[:, :, pl.ds(at, 8), :] for at in (0, NR - 8)
    )
    targets = (elem_s, mix_s, x_s.at[0], x_s.at[1], m_s, o_s.at[0], o_s.at[1])
    copies = [pltpu.make_async_copy(a, b, sems.at[k]) for k, (a, b) in enumerate(zip(sources, targets))]
    outs = [
        pltpu.make_async_copy(z_s.at[k], z_hbm.at[:, :, pl.ds(k * (NR - 8), 8), :], sems.at[7 + k]) for k in range(2)
    ]
    for copy in copies:
        copy.start()
    copies[0].wait()
    row = iota((512, 16), 0)
    spread_in = (iota((512, 16), 1) == (row // 128) * 4 + row % 4).astype(BF16)
    col = iota((16, 512), 1)
    spread_out = (iota((16, 512), 0) == (col // 128) * 4 + col % 4).astype(BF16)
    elem = (0.5 * elem_s[...]).astype(BF16)
    half = lax.dot_general(spread_in, elem, (((1,), (1,)), ((), ())), preferred_element_type=F32)
    spread = dot(half.astype(BF16), spread_out)
    same = (iota((512, 512), 0) % 128) // 4 == (iota((512, 512), 1) % 128) // 4
    b = jnp.where(same, spread, 0.0).astype(BF16)
    b_ref[...] = b
    copies[1].wait()
    mix = (0.5 * mix_s[...]).astype(BF16)
    for k, ref in ((0, sp_ref), (1, sn_ref)):
        copies[2 + k].wait()
        pieces = element_rows(x_s.at[k], mix, b)
        store_rows(z_s.at[k], pieces, 0)
        outs[k].start()
        ref[AT:O1, :] = jnp.concatenate([pieces[f][7 * k] for f in range(2)], 0).astype(BF16)
    for k in (4, 5, 6):
        copies[k].wait()
    m = m_s[...].astype(F32)
    for ref, k, first in ((sp_ref, 0, 0), (sn_ref, 1, 6)):
        rows = jnp.swapaxes(o_s[k].reshape(OL, 8, NC), 0, 1)
        at = k * (NR - 8) + first
        for j, base in ((0, O1), (1, O2)):
            u = rows[first + j] * m[at + j : at + j + 1]
            ref[base : base + 128, :] = jnp.concatenate([u, jnp.zeros((8, NC), F32)], 0).astype(BF16)
        ref[MK:PAY, :] = mask_rows(m[at : at + 1], m[at + 1 : at + 2])
    for copy in outs:
        copy.wait()


INNER = NR // 8 - 2


def pick_columns(columns):
    k, at = iota((8 * len(columns), 8 * NC), 0), iota((8 * len(columns), 8 * NC), 1)
    wanted = jnp.zeros_like(k)
    for j, c in enumerate(columns):
        wanted = jnp.where(k // 8 == j, c, wanted)
    return ((at // NC == k % 8) & (at % NC == wanted)).astype(BF16)


def take_columns(pick, tiles):
    side = jnp.concatenate([t.astype(BF16) for t in tiles], 1)
    got = lax.dot_general(pick, side, (((1,), (1,)), ((), ())), preferred_element_type=F32)
    return jnp.concatenate([got, jnp.zeros_like(got)], 1)


def inner_kernel(
    x_hbm, mix_hbm, o_hbm, b_ref, m_ref, rim_hbm, z_hbm, top_ref, zc_ref, oc_ref,
    x_s, z_s, o_s, mix_s, sems, rest,
):
    mix_copy = pltpu.make_async_copy(mix_hbm, mix_s, rest.at[0])
    ocean_copy = pltpu.make_async_copy(o_hbm, o_s, rest.at[1])
    rims = [
        pltpu.make_async_copy(
            rim_hbm.at[:, :, pl.ds(at, 8), :], z_s.at[:, :, pl.ds(at, 8), :], rest.at[2 + k]
        )
        for k, at in enumerate((0, NR - 8))
    ]

    def chunk(i):
        return pltpu.make_async_copy(x_hbm.at[:, :, pl.ds(i * 8 + 8, 8), :], x_s.at[i], sems.at[i])

    def leave(i):
        rows = pl.ds(pl.multiple_of(i * 8 + 8, 8), 8)
        return pltpu.make_async_copy(z_s.at[:, :, rows, :], z_hbm.at[:, :, rows, :], sems.at[INNER + i])

    mix_copy.start()
    for i in range(INNER):
        chunk(i).start()
    for copy in rims:
        copy.start()
    ocean_copy.start()
    mix_copy.wait()
    mix = (0.5 * mix_s[...]).astype(BF16)

    def step(i, carry):
        chunk(i).wait()
        store_rows(z_s, element_rows(x_s.at[i], mix, b_ref[...]), pl.multiple_of(i * 8 + 8, 8))
        leave(i).start()
        return carry

    lax.fori_loop(0, INNER, step, 0)
    for copy in rims:
        copy.wait()
    pick = pick_columns((0, NC - 1))

    def atm(i, carry):
        for f in range(2):
            got = take_columns(pick, [z_s[f, i * 8 + l] for l in range(8)])
            at = pl.multiple_of(f * LEV + i * 8, 8)
            for k in range(2):
                zc_ref[k, pl.ds(at, 8), :] = got[k * 8 : k * 8 + 8]
        return carry

    lax.fori_loop(0, LEV // 8, atm, 0, unroll=3)
    for f in range(2):
        top_ref[f] = z_s[f, LEV - 1]
    ocean_copy.wait()
    wet = m_ref[...].astype(F32)
    pick = pick_columns((0, 1, NC - 2, NC - 1))

    def ocean(i, carry):
        tiles = [i * 8 + l for l in range(8)]
        got = take_columns(pick, [wet * o_s[t // LO, t % LO] for t in tiles])
        for k in range(4):
            oc_ref[k, pl.ds(pl.multiple_of(i * 8, 8), 8), :] = got[k * 8 : k * 8 + 8]
        return carry

    lax.fori_loop(0, OL // 8, ocean, 0, unroll=3)
    oc_ref[:, OL:, :] = jnp.zeros((4, 8, NC), F32)
    for i in range(INNER):
        leave(i).wait()


def cols_kernel(zc_ref, oc_ref, m_ref, rp_ref, rn_ref, ss_ref, sn_ref):
    lane = iota((144, NC), 1)
    place = lane % 4
    rp_at, rn_at = rp_ref[AT:O1, :].astype(F32), rn_ref[AT:O1, :].astype(F32)
    before, after = rp_ref[O2:MK, :].astype(F32), rn_ref[O1:O2, :].astype(F32)
    olane = iota((128, NC), 1)
    row = iota((64, NC), 0)
    m_before, m_after = rp_ref[MK:PAY, :].astype(F32)[1:2], rn_ref[MK:PAY, :].astype(F32)[0:1]
    tail = jnp.where(row == 0, m_before, jnp.where(row == 1, m_after, 0.0))
    m_t = jnp.transpose(jnp.concatenate([m_ref[...].astype(F32), tail], 0))
    for ref, c_at, ocs in ((ss_ref, 0, (0, 1)), (sn_ref, 127, (126, 127))):
        z = zc_ref[0 if c_at == 0 else 1]
        nxt = jnp.where(lane == 63, rn_at[:, c_at : c_at + 1], pltpu.roll(z, 127, 1))
        prv = jnp.where(lane == 0, rp_at[:, c_at : c_at + 1], pltpu.roll(z, 1, 1))
        z = jnp.where(place == 3, (z + nxt) * 0.5, jnp.where(place == 0, (z + prv) * 0.5, z))
        ref[AT:O1, :] = z.astype(BF16)
        for k, c in enumerate(ocs):
            source = c if c < 2 else c - 124
            u = jnp.where(
                olane < 64,
                oc_ref[source],
                jnp.where(olane == 64, before[:, c : c + 1], jnp.where(olane == 65, after[:, c : c + 1], 0.0)),
            )
            base = (O1, O2)[k]
            ref[base : base + 128, :] = u.astype(BF16)
        ref[MK:PAY, :] = mask_rows(m_t[ocs[0] : ocs[0] + 1], m_t[ocs[1] : ocs[1] + 1])


def averaged(z, nxt, prv, place):
    return jnp.where(place == 3, (z + nxt) * 0.5, jnp.where(place == 0, (z + prv) * 0.5, z))


def stiffness(z, h_prev, h_next, c_south, c_north):
    row, lane = iota((NR, NC), 0), iota((NR, NC), 1)
    nxt = jnp.where(row == NR - 1, h_next, pltpu.roll(z, NR - 1, 0))
    prv = jnp.where(row == 0, h_prev, pltpu.roll(z, 1, 0))
    z = averaged(z, nxt, prv, row % 4)
    nxt = jnp.where(lane == NC - 1, c_north, pltpu.roll(z, NC - 1, 1))
    prv = jnp.where(lane == 0, c_south, pltpu.roll(z, 1, 1))
    return averaged(z, nxt, prv, lane % 4)


def surface_kernel(z_ref, rp_ref, rn_ref, cs_ref, cn_ref, s_ref):
    rp, rn = rp_ref[AT:O1, :].astype(F32), rn_ref[AT:O1, :].astype(F32)
    cs, cn = cs_ref[AT:O1, :].astype(F32), cn_ref[AT:O1, :].astype(F32)
    for f in range(2):
        top = f * LEV + LEV - 8
        south = jnp.transpose(cs[top : top + 8])[:NR, 7:8]
        north = jnp.transpose(cn[top : top + 8])[:NR, 7:8]
        last = top + 7
        s = stiffness(z_ref[f], rp[last : last + 1], rn[last : last + 1], south, north)
        s_ref[f] = s.astype(BF16)


def edge_spread(tiles, scale):
    k, c = iota((2 * tiles, tiles * NC), 0), iota((2 * tiles, tiles * NC), 1)
    mine = k % tiles == c // NC
    end = c % NC == jnp.where(k < tiles, 0, NC - 1)
    return jnp.where(mine & end, scale, 0.0).astype(BF16)


def add_ends(x, first, last):
    row = iota((8, NC), 0)
    return jnp.concatenate(
        [
            x[0:8] + jnp.where(row == 0, first, 0.0),
            x[8 : NR - 8],
            x[NR - 8 :] + jnp.where(row == 7, last, 0.0),
        ],
        0,
    )


def column_halo(columns, spread):
    return lax.dot_general(columns, spread, (((0,), (0,)), ((), ())), preferred_element_type=F32)[:NR]


FB = 8


def finish_kernel(
    z_hbm, rp_ref, rn_ref, cs_ref, cn_ref, new_ref, mid_hbm, o_hbm, ocean_hbm, z_s, o_s, h_ref, sems, level_sem
):
    del mid_hbm
    level = pltpu.make_async_copy(new_ref, ocean_hbm.at[:, 0], level_sem)
    level.start()

    def enter(i):
        return pltpu.make_async_copy(z_hbm.at[:, pl.ds(i * FB, FB)], z_s.at[i], sems.at[LEV // FB + i])

    for i in range(LEV // FB):
        enter(i).start()
    for k, ref in enumerate((rp_ref, rn_ref, cs_ref, cn_ref)):
        h_ref[k] = ref[AT:O1, :].astype(F32)
    spread = edge_spread(2 * FB, 0.5)
    row, lane = iota((NR, NC), 0), iota((NR, NC), 1)

    def weights(place, at, end):
        low = jnp.where((place == 0) & (at != 0), 0.5, 0.0)
        high = jnp.where((place == 3) & (at != end), 0.5, 0.0)
        return jnp.where((place == 0) | (place == 3), 0.5, 1.0), low, high

    own_r, low_r, high_r = weights(row % 4, row, NR - 1)
    own_c, low_c, high_c = weights(lane % 4, lane, NC - 1)

    def chunk(i):
        return pltpu.make_async_copy(o_s.at[i], o_hbm.at[:, pl.ds(i * FB, FB)], sems.at[i])

    def step(i, carry):
        enter(i).wait()

        def halo(k, f):
            return h_ref[k, pl.ds(pl.multiple_of(f * LEV + i * FB, 8), FB), :]

        columns = jnp.concatenate([halo(2, 0), halo(2, 1), halo(3, 0), halo(3, 1)], 0).astype(BF16)
        edges = column_halo(columns, spread)
        for f in range(2):
            first, last = 0.5 * halo(0, f), 0.5 * halo(1, f)
            for l in range(FB):
                t = z_s[i, f, l]
                t = own_r * t + high_r * pltpu.roll(t, NR - 1, 0) + low_r * pltpu.roll(t, 1, 0)
                t = add_ends(t, first[l : l + 1], last[l : l + 1])
                t = own_c * t + high_c * pltpu.roll(t, NC - 1, 1) + low_c * pltpu.roll(t, 1, 1)
                tile = f * FB + l
                o_s[i, f, l] = t + edges[:, tile * NC : (tile + 1) * NC]
        chunk(i).start()
        return carry

    lax.fori_loop(0, LEV // FB, step, 0)
    level.wait()
    for i in range(LEV // FB):
        chunk(i).wait()


OB = 12


def ocean_kernel(
    at_ref, k_ref, o_hbm, m_ref, kc_ref, sp_ref, sn_ref, ss_ref, st_ref, rp_ref, rn_ref, cs_ref, cn_ref, fo_ref,
    out_hbm, first_ref, out_s, row_ref, col_ref, sems,
):
    def enter(i):
        return pltpu.make_async_copy(o_hbm.at[:, pl.ds(i * OB, OB)], out_s.at[i], sems.at[LO // OB + i])

    for i in range(LO // OB):
        enter(i).start()
    is_top, is_low = at_ref[0] == 7, at_ref[0] == 0
    lane = iota((128, NC), 1)

    def part(ref, base):
        return ref[base : base + 128, :].astype(F32)

    def masks(ref):
        m = ref[MK:PAY, :].astype(F32)
        return m[0:1], m[1:2]

    fr, fc = iota((NC, NC), 0), iota((NC, NC), 1)
    flip = (((fr < 64) & (fc == 63 - fr)) | ((fr == 64) & (fc == 65)) | ((fr == 65) & (fc == 64))).astype(BF16)
    turned = dot(fo_ref[...], flip)
    n0 = jnp.where(is_top, turned[O2:MK], part(cn_ref, O1))
    n1 = jnp.where(is_top, turned[O1:O2], part(cn_ref, O2))
    mc0, mc1 = masks(cn_ref)
    mn0 = jnp.where(is_top, turned[MK + 1 : MK + 2], mc0)
    mn1 = jnp.where(is_top, turned[MK : MK + 1], mc1)
    keep = jnp.where(is_low, 0.0, 1.0)
    s2, s1 = part(cs_ref, O1) * keep, part(cs_ref, O2) * keep
    ms2, ms1 = masks(cs_ref)
    ms2, ms1 = ms2 * keep, ms1 * keep
    um2, um1 = part(rp_ref, O1), part(rp_ref, O2)
    mm2, mm1 = masks(rp_ref)
    u64, u65 = part(rn_ref, O1), part(rn_ref, O2)
    m64, m65 = masks(rn_ref)
    own0, own63 = part(sp_ref, O1), part(sn_ref, O2)
    mo0, mo63 = masks(sp_ref)[0], masks(sn_ref)[1]
    west0, east127 = part(ss_ref, O1), part(st_ref, O2)
    mw0, me127 = masks(ss_ref)[0], masks(st_ref)[1]
    at, l60 = iota((128, LO), 0), iota((128, LO), 1)
    kap = sum(
        jnp.sum(jnp.where(at - f * LO == l60, kc_ref[f : f + 1, :], 0.0), 1, keepdims=True) for f in range(2)
    )

    def along(u, low, high, end):
        where = lane[: u.shape[0]]
        return jnp.where(where == end, high, pltpu.roll(u, 127, 1)) + jnp.where(
            where == 0, low, pltpu.roll(u, 1, 1)
        )

    def advance(u, wet, inner, outer, m_inner, m_outer, low, high, m_low, m_high, end):
        total = inner + outer + along(u, low, high, end)
        m8 = jnp.broadcast_to(wet, (8, NC))
        count = m_inner + m_outer + along(m8, m_low, m_high, end)[0:1]
        return u + kap * (wet * total - count * u)

    def corner(x, at):
        return x[:, at : at + 1]

    row_ref[0] = um1
    row_ref[1] = u64
    row_ref[2] = advance(
        um1, mm1, own0, um2, mo0, mm2, corner(s1, 64), corner(n0, 64), corner(ms1, 64), corner(mn0, 64), 127
    )
    row_ref[3] = advance(
        u64, m64, own63, u65, mo63, m65, corner(s1, 65), corner(n0, 65), corner(ms1, 65), corner(mn0, 65), 127
    )
    west = advance(
        s1, ms1, west0, s2, mw0, ms2, corner(s1, 64), corner(s1, 65), corner(ms1, 64), corner(ms1, 65), 63
    )
    east = advance(
        n0, mn0, east127, n1, me127, mn1, corner(n0, 64), corner(n0, 65), corner(mn0, 64), corner(mn0, 65), 63
    )
    here = iota((NR, NC), 1)
    for sub, (low, high) in enumerate(((s1, n0), (west, east))):
        low, high = jnp.transpose(low)[:NR], jnp.transpose(high)[:NR]
        for f in range(2):
            col_ref[2 * sub + f] = jnp.where(
                here < 64, pltpu.roll(low, (NC - LO * f) % NC, 1), pltpu.roll(high, (NC + 64 - LO * f) % NC, 1)
            )
    a, b = iota((NC, NC), 0), iota((NC, NC), 1)
    ends = ((a == 0) & (b == 0)) | ((a == 64) & (b == NC - 1))
    ns = jnp.concatenate([(jnp.abs(a - b) == 1).astype(BF16), ends.astype(BF16)], 0)
    wet = m_ref[...].astype(F32)
    r, c = iota((NR, NC), 0), iota((NR, NC), 1)
    m_north = jnp.transpose(jnp.broadcast_to(mn0, (8, NC)))[:NR, 0:1]
    m_south = jnp.transpose(jnp.broadcast_to(ms1, (8, NC)))[:NR, 0:1]
    count = jnp.where(r == NR - 1, m64, pltpu.roll(wet, NR - 1, 0)) + jnp.where(
        r == 0, mm1, pltpu.roll(wet, 1, 0)
    )
    count = count + jnp.where(c == NC - 1, m_north, pltpu.roll(wet, NC - 1, 1))
    count = count + jnp.where(c == 0, m_south, pltpu.roll(wet, 1, 1))

    places = [(f, l) for f in range(2) for l in range(OB)]

    def chunk(i):
        return pltpu.make_async_copy(out_s.at[i], out_hbm.at[:, pl.ds(i * OB, OB)], sems.at[i])

    def step(i, carry):
        enter(i).wait()
        ts = [out_s[i, f, l] for f, l in places]
        for sub in range(2):
            us = [wet * t for t in ts]
            halos = [pltpu.roll(col_ref[2 * sub + f], (NC - i * OB - l) % NC, 1) for f, l in places]
            side = jnp.concatenate([jnp.concatenate(us, 0), jnp.concatenate(halos, 0)], 1)
            cols = dot(side.astype(BF16), ns)
            for j, (f, l) in enumerate(places):
                level = i * OB + l
                here = pl.ds(f * LO + level, 1)
                u = us[j]
                total = pltpu.roll(u, NR - 1, 0) + pltpu.roll(u, 1, 0) + cols[j * NR : (j + 1) * NR]
                total = add_ends(
                    total, row_ref[2 * sub, here, :] - u[NR - 1 :], row_ref[2 * sub + 1, here, :] - u[0:1]
                )
                ts[j] = ts[j] + (k_ref[f, level] * wet) * (total - count * ts[j])
        for j, (f, l) in enumerate(places):
            out_s[i, f, l] = ts[j]
        chunk(i).start()
        return carry

    lax.fori_loop(0, LO // OB, step, 0)
    for f in range(2):
        first_ref[f] = out_s[0, f, 0]
    for i in range(LO // OB):
        chunk(i).wait()


def send_map_kernel(at_ref, ids_ref, pass_hbm, out_ref, scol_ref, through_hbm):
    del pass_hbm, through_hbm
    gx, gy = at_ref[0], at_ref[1]
    block = ids_ref[:, pl.ds(pl.multiple_of((gx // 2) * 128, 128), 128)]
    block = pltpu.roll(block, (gx % 2) * 64, 1)
    rows = iota((32, 128), 0)
    tile_row, lane = iota((128, 128), 0), iota((128, 128), 1)
    before = (tile_row < lane).astype(BF16)
    ones = jnp.ones((128, 128), BF16)
    earlier = jnp.zeros((128, 128), F32)
    tiles, ranks = [], []
    for t in range(TOP):
        ids = jnp.sum(jnp.where(rows == gy * 4 + t, block, 0), 0, keepdims=True)
        hit = (ids // 64 == tile_row) & (lane < 64)
        hot = hit.astype(BF16)
        rank = dot(hot, before) + earlier
        earlier = earlier + dot(hot, ones)
        ranks.append(jnp.sum(jnp.where(hit, rank, 0.0), 0, keepdims=True))
        tiles.append((ids // 64).astype(F32))
    place = iota((8, 128), 0)
    stack = jnp.zeros((8, 128), F32)
    for t in range(TOP):
        stack = jnp.where(place == t, tiles[t], jnp.where(place == t + 4, ranks[t], stack))
    spread = (iota((128, 512), 1) // 8 == iota((128, 512), 0)).astype(BF16)
    wide = dot(stack.astype(BF16), spread)
    col, row8 = iota((8, 512), 1), iota((8, 512), 0)
    wide = jnp.where(row8 % 4 == (col // 2) % 4, wide * jnp.where(row8 < 4, 10.0, 2.0), 0.0)
    slot = jnp.sum(wide, 0, keepdims=True) + (iota((1, 512), 1) % 2).astype(F32)
    out_ref[...] = jnp.where(slot.astype(jnp.int32) == iota((SLOTS, 512), 0), 1.0, 0.0).astype(BF16)
    scol_ref[...] = jnp.transpose(jnp.broadcast_to(slot, (128, 512)))


def receive_map_kernel(at_ref, ids_ref, take_ref, give_ref):
    own_tile = at_ref[0] * 8 + at_ref[1]
    blocks = 8
    row, lane = iota((128, 128), 0), iota((128, 128), 1)
    halves = (row // 64) == (lane // 64)
    before = jnp.concatenate([(halves & (row < lane)).astype(BF16), halves.astype(BF16)], 1)
    r, c = iota((256, 256), 0), iota((256, 256), 1)
    lower = ((r // 4 == c // 4) & (c % 4 < r % 4)).astype(BF16)
    sr, sc = iota((160, 160), 0), iota((160, 160), 1)
    pick = (((sr // 10) % 8 == (sc % 32) // 4) & ((sr % 10) // 2 == sc // 32)).astype(BF16)
    side = iota((160, NC), 0) // 80 == iota((160, NC), 1) // 64
    ids = jnp.concatenate([ids_ref[:, b * NC : (b + 1) * NC] for b in range(blocks)], 0)
    hit = ids // 64 == own_tile
    counts = dot(hit.astype(BF16), before)
    rank = counts[:, 0:NC] + dot(lower, counts[:, NC:].astype(BF16))
    value = (ids % 64 + 1).astype(F32)
    held = [jnp.where(hit & (rank == float(k)), value, 0.0) for k in range(CAP)]
    stacked = jnp.concatenate(
        [jnp.concatenate([h[b * 32 : (b + 1) * 32] for h in held], 0) for b in range(blocks)], 1
    )
    found = dot(pick, stacked.astype(BF16))
    found = jnp.concatenate(
        [jnp.where(side, found[:, b * NC : (b + 1) * NC], 0.0) for b in range(blocks)], 0
    )
    local = dot(found.astype(BF16), jnp.ones((NC, NC), BF16)).astype(jnp.int32)
    row, col = iota((SLOTS, NC), 0), iota((SLOTS, NC), 1)
    give = jnp.where((local - 1 == col % 64) & (row % 2 == col // 64), 1.0, 0.0)
    give_ref[...] = give.astype(BF16)
    for b in range(SLOTS // NC):
        take_ref[:, b * NC : (b + 1) * NC] = jnp.transpose(give[b * NC : (b + 1) * NC]).astype(BF16)


def pack_kernel(c_ref, map_ref, fold_ref, out_ref):
    del fold_ref
    out_ref[...] = dot(map_ref[...], c_ref[...].astype(BF16)).astype(BF16)


def ocean_surface_kernel(in_ref, take_ref, give_ref, m_ref, first_ref, new_ref, back_ref):
    forcing = dot(take_ref[...], in_ref[...])
    wet = 0.25 * m_ref[...].astype(F32)
    news = []
    for f in range(2):
        new = first_ref[f] + wet * forcing[f * NR : (f + 1) * NR]
        new_ref[f] = new
        news.append(new)
    sea = jnp.concatenate(news, 0).astype(BF16)
    back_ref[...] = dot(give_ref[...], sea).astype(BF16)


WB = 8


def return_kernel(in_ref, scol_ref, w_hbm, out_ref, w_s, e_s, p_s, sems):
    def chunk(i):
        return pltpu.make_async_copy(w_hbm.at[pl.ds(i * WB, WB)], w_s.at[i], sems.at[i])

    for i in range(NR // WB):
        chunk(i).start()
    total = jnp.zeros((512, 128), F32)
    slot = scol_ref[...].astype(jnp.int32)
    for b in range(SLOTS // 128):
        hot = jnp.where(slot == iota((512, 128), 1) + b * 128, 1.0, 0.0).astype(BF16)
        total = total + dot(hot, in_ref[b * 128 : (b + 1) * 128, :])
    term = (iota((512, 128), 0) % 8) // 2
    e_s[...] = jnp.concatenate([jnp.where(term == t, total, 0.0) for t in range(TOP)], 1)

    def step(i, carry):
        chunk(i).wait()
        for k in range(WB):
            rows = pl.ds(pl.multiple_of((i * WB + k) * 8, 8), 8)
            p_s[rows, :] = dot(e_s[rows, :].astype(BF16), w_s[i, k].reshape(TOP * NC, NC))
        return carry

    lax.fori_loop(0, NR // WB, step, 0)
    r, c = iota((128, 512), 0), iota((128, 512), 1)
    gather = ((c // 8 == r % NR) & (c % 2 == r // NR)).astype(F32)
    done = jnp.dot(gather, p_s[...], preferred_element_type=F32, precision=lax.Precision.HIGHEST)
    for f in range(2):
        out_ref[f] = done[f * NR : (f + 1) * NR]


def shape(dims, dtype=F32):
    return jax.ShapeDtypeStruct(dims, dtype)


def shifted(x, axis, by):
    count = lax.axis_size(axis)
    return lax.ppermute(x, axis, [(i, (i + by) % count) for i in range(count)])


def per_device(atm_state, ocean_state, land_mask, elem_op, column_mix, kappa, remap_weight, intersection):
    gx, gy = lax.axis_index("gx"), lax.axis_index("gy")
    at = jnp.stack([gx, gy]).astype(jnp.int32)
    smem = pl.BlockSpec(memory_space=pltpu.SMEM)
    full = whole((PAY, NC))

    vmem = pl.BlockSpec(memory_space=pltpu.VMEM)
    hbm = pl.BlockSpec(memory_space=pl.ANY)

    def pinned(x):
        return pltpu.with_memory_space_constraint(x, pltpu.HBM)

    atm_in, ocean_in, mask_in = pinned(atm_state), pinned(ocean_state), pinned(land_mask)
    mix_in, elem_in = pinned(column_mix), pinned(elem_op)
    payload = shape((PAY, NC), BF16)
    rim, send_next, send_prev, element = pl.pallas_call(
        atm_rim_kernel,
        in_specs=[hbm] * 5,
        out_specs=[hbm] + [vmem] * 3,
        out_shape=[pltpu.HBM(atm_state.shape, F32), payload, payload, shape((512, 512), BF16)],
        scratch_shapes=[
            pltpu.VMEM((2, 2, LEV, 8, NC), F32),
            pltpu.VMEM((2, 2, LO, 8, NC), F32),
            pltpu.VMEM((NR, NC), jnp.int32),
            pltpu.VMEM((LEV, LEV), F32),
            pltpu.VMEM((16, 16), F32),
            pltpu.VMEM((2, 2, LEV, 8, NC), F32),
            pltpu.SemaphoreType.DMA((9,)),
        ],
        compiler_params=params(16),
        name="atm_rim",
    )(atm_in, ocean_in, mask_in, mix_in, elem_in)

    from_prev = shifted(send_next, "gx", 1)

    ids = jnp.transpose(intersection, (1, 2, 0)).reshape(32, 1024)
    send_map, slot_col, send_prev = pl.pallas_call(
        send_map_kernel,
        in_specs=[smem, vmem, hbm],
        out_specs=[vmem, vmem, hbm],
        out_shape=[shape((SLOTS, 512), BF16), shape((512, 128)), payload],
        input_output_aliases={2: 2},
        compiler_params=params(),
        cost_estimate=pl.CostEstimate(flops=4000000, bytes_accessed=4200000, transcendentals=0),
        name="send_map",
    )(at, ids, send_prev)
    from_next = shifted(send_prev, "gx", -1)

    weights = remap_weight[:, 0]
    weights_in = pinned(weights)
    z, top_level, z_cols, ocean_cols = pl.pallas_call(
        inner_kernel,
        in_specs=[hbm, hbm, hbm, vmem, vmem, hbm],
        out_specs=[hbm] + [vmem] * 3,
        out_shape=[pltpu.HBM(atm_state.shape, F32), shape((2, NR, NC)), shape((2, 144, NC)), shape((4, 128, NC))],
        scratch_shapes=[
            pltpu.VMEM((INNER, 2, LEV, 8, NC), F32),
            pltpu.VMEM(atm_state.shape, F32),
            pltpu.VMEM(ocean_state.shape, F32),
            pltpu.VMEM((LEV, LEV), F32),
            pltpu.SemaphoreType.DMA((2 * INNER,)),
            pltpu.SemaphoreType.DMA((4,)),
        ],
        input_output_aliases={5: 0},
        compiler_params=params(14),
        cost_estimate=pl.CostEstimate(flops=1000000000, bytes_accessed=14000000, transcendentals=0),
        name="inner",
    )(atm_in, mix_in, ocean_in, element, land_mask, rim)

    send_south, send_north = pl.pallas_call(
        cols_kernel,
        out_shape=[shape((PAY, NC), BF16)] * 2,
        compiler_params=params(),
        name="cols",
    )(z_cols, ocean_cols, land_mask, from_prev, from_next)

    from_south = shifted(send_north, "gy", 1)
    from_north = shifted(send_south, "gy", -1)
    gx_count, gy_count = lax.axis_size("gx"), lax.axis_size("gy")
    top = gy_count - 1
    folded = lax.ppermute(
        send_north, ("gx", "gy"), [(i * gy_count + top, (gx_count - 1 - i) * gy_count + top) for i in range(gx_count)]
    )

    surface = pl.pallas_call(
        surface_kernel,
        in_specs=[vmem] * 5,
        out_shape=shape((2, NR, NC), BF16),
        compiler_params=params(),
        name="surface",
    )(top_level, from_prev, from_next, from_south, from_north)

    products = lax.dot_general(
        weights, surface, (((3,), (2,)), ((0,), (1,))), preferred_element_type=F32
    )
    contrib = jnp.transpose(products, (0, 1, 3, 2)).reshape(2 * ENT, NC)
    outgoing = pl.pallas_call(
        pack_kernel,
        in_specs=[vmem, vmem, hbm],
        out_shape=shape((SLOTS, NC), BF16),
        compiler_params=params(),
        name="pack",
    )(contrib, send_map, folded)
    incoming = lax.all_to_all(
        outgoing.reshape(TILES, CAP, 2, NC), ("gx", "gy"), split_axis=0, concat_axis=0, tiled=True
    ).reshape(SLOTS, NC)

    ocean_mid, first_level = pl.pallas_call(
        ocean_kernel,
        in_specs=[smem, smem, hbm] + [vmem] * 11,
        out_specs=[hbm, vmem],
        out_shape=[pltpu.HBM(ocean_state.shape, F32), shape((2, NR, NC))],
        scratch_shapes=[
            pltpu.VMEM((LO // OB, 2, OB, NR, NC), F32),
            pltpu.VMEM((4, 128, NC), F32),
            pltpu.VMEM((4, NR, NC), F32),
            pltpu.SemaphoreType.DMA((2 * (LO // OB),)),
        ],
        compiler_params=params(16),
        cost_estimate=pl.CostEstimate(flops=30000000, bytes_accessed=8000000, transcendentals=0),
        name="ocean",
    )(
        at[1:], kappa, ocean_in, land_mask, kappa, send_prev, send_next, send_south, send_north,
        from_prev, from_next, from_south, from_north, folded,
    )

    take, give = pl.pallas_call(
        receive_map_kernel,
        in_specs=[smem, vmem],
        out_shape=[shape((128, SLOTS), BF16), shape((SLOTS, 128), BF16)],
        compiler_params=params(),
        cost_estimate=pl.CostEstimate(flops=4000000, bytes_accessed=4200000, transcendentals=0),
        name="receive_map",
    )(at, ids)

    new_level, back_out = pl.pallas_call(
        ocean_surface_kernel,
        out_shape=[shape((2, NR, NC)), shape((SLOTS, NC), BF16)],
        compiler_params=params(),
        name="ocean_surface",
    )(incoming, take, give, land_mask, first_level)

    back_in = lax.all_to_all(
        back_out.reshape(TILES, CAP, 2, NC), ("gx", "gy"), split_axis=0, concat_axis=0, tiled=True
    ).reshape(SLOTS, NC)

    atm_next, ocean_next = pl.pallas_call(
        finish_kernel,
        in_specs=[hbm] + [vmem] * 5 + [hbm],
        out_specs=[hbm, hbm],
        out_shape=[pltpu.HBM(atm_state.shape, F32), pltpu.HBM(ocean_state.shape, F32)],
        input_output_aliases={6: 1},
        scratch_shapes=[
            pltpu.VMEM((LEV // FB, 2, FB, NR, NC), F32),
            pltpu.VMEM((LEV // FB, 2, FB, NR, NC), F32),
            pltpu.VMEM((4, 144, NC), F32),
            pltpu.SemaphoreType.DMA((2 * (LEV // FB),)),
            pltpu.SemaphoreType.DMA(()),
        ],
        compiler_params=params(16),
        cost_estimate=pl.CostEstimate(flops=20000000, bytes_accessed=9400000, transcendentals=0),
        name="finish",
    )(pinned(z), from_prev, from_next, from_south, from_north, new_level, ocean_mid)

    returned = pl.pallas_call(
        return_kernel,
        in_specs=[vmem, vmem, hbm],
        out_specs=vmem,
        out_shape=shape((2, NR, NC)),
        scratch_shapes=[
            pltpu.VMEM((NR // WB, WB, TOP, NC, NC), BF16),
            pltpu.VMEM((512, 512), F32),
            pltpu.VMEM((512, NC), F32),
            pltpu.SemaphoreType.DMA((NR // WB,)),
        ],
        compiler_params=params(16),
        name="returned",
    )(back_in, slot_col, weights_in)
    return atm_next, ocean_next, returned


def solution(mesh):
    placed = (
        P(None, None, "gx", "gy"),
        P(None, None, "gx", "gy"),
        P("gx", "gy"),
        P(),
        P(),
        P(),
        P("gx", "gy", None, None, None),
        P(),
    )
    return jax.shard_map(
        per_device,
        mesh=mesh,
        in_specs=placed,
        out_specs=(P(None, None, "gx", "gy"), P(None, None, "gx", "gy"), P(None, "gx", "gy")),
        check_vma=False,
    )
```

```python
import jax
import jax.numpy as jnp
from jax import lax
from jax.experimental import pallas as pl
from jax.experimental.pallas import tpu as pltpu
from jax.sharding import PartitionSpec as P

F32, BF16 = jnp.float32, jnp.bfloat16
LEV, LO, NR, NC = 72, 60, 64, 128
AT, O1, O2, MK, PAY = 0, 144, 272, 400, 416
OL = 2 * LO
TOP, CAP, TILES = 4, 5, 128
ENT = NR * TOP
SLOTS = TILES * CAP * 2
MIB = 1024 * 1024


def iota(shape, dim):
    return lax.broadcasted_iota(jnp.int32, shape, dim)


def dot(a, b):
    return jnp.dot(a, b, preferred_element_type=F32)


def params(mib=6):
    return pltpu.CompilerParams(vmem_limit_bytes=mib * MIB)


def whole(shape):
    return pl.BlockSpec(shape, lambda *_: (0,) * len(shape))


def mask_rows(first, second):
    place = iota((16, NC), 0)
    return jnp.where(place == 0, first, jnp.where(place == 1, second, 0.0)).astype(BF16)


def element_rows(x_s, mix, b):
    fields = [jnp.swapaxes(x_s[f], 0, 1) for f in range(2)]
    ys = []
    for big in range(2):
        for f in range(2):
            x = jnp.concatenate([fields[f][big * 4 + k] for k in range(4)], 1)
            ys.append(x + dot(mix, x.astype(BF16)))
    y = jnp.concatenate(ys, 0)
    z = y + dot(y.astype(BF16), b)
    pieces = [[], []]
    for r in range(8):
        for f in range(2):
            at = ((r // 4) * 2 + f) * LEV
            pieces[f].append(z[at : at + LEV, (r % 4) * NC : (r % 4 + 1) * NC])
    return pieces


def store_rows(z_ref, pieces, at):
    for f in range(2):
        z_ref[f, :, pl.ds(at, 8), :] = jnp.swapaxes(jnp.stack(pieces[f], 0), 0, 1)


def atm_rim_kernel(
    x_hbm, o_hbm, m_hbm, mix_hbm, elem_hbm, z_hbm, sn_ref, sp_ref, b_ref, x_s, o_s, m_s, mix_s, elem_s, z_s, sems
):
    sources = (elem_hbm, mix_hbm, x_hbm.at[:, :, pl.ds(0, 8), :], x_hbm.at[:, :, pl.ds(NR - 8, 8), :], m_hbm) + tuple(
        o_hbm.at[:, :, pl.ds(at, 8), :] for at in (0, NR - 8)
    )
    targets = (elem_s, mix_s, x_s.at[0], x_s.at[1], m_s, o_s.at[0], o_s.at[1])
    copies = [pltpu.make_async_copy(a, b, sems.at[k]) for k, (a, b) in enumerate(zip(sources, targets))]
    outs = [
        pltpu.make_async_copy(z_s.at[k], z_hbm.at[:, :, pl.ds(k * (NR - 8), 8), :], sems.at[7 + k]) for k in range(2)
    ]
    for copy in copies:
        copy.start()
    copies[0].wait()
    row = iota((512, 16), 0)
    spread_in = (iota((512, 16), 1) == (row // 128) * 4 + row % 4).astype(BF16)
    col = iota((16, 512), 1)
    spread_out = (iota((16, 512), 0) == (col // 128) * 4 + col % 4).astype(BF16)
    elem = (0.5 * elem_s[...]).astype(BF16)
    half = lax.dot_general(spread_in, elem, (((1,), (1,)), ((), ())), preferred_element_type=F32)
    spread = dot(half.astype(BF16), spread_out)
    same = (iota((512, 512), 0) % 128) // 4 == (iota((512, 512), 1) % 128) // 4
    b = jnp.where(same, spread, 0.0).astype(BF16)
    b_ref[...] = b
    copies[1].wait()
    mix = (0.5 * mix_s[...]).astype(BF16)
    for k, ref in ((0, sp_ref), (1, sn_ref)):
        copies[2 + k].wait()
        pieces = element_rows(x_s.at[k], mix, b)
        store_rows(z_s.at[k], pieces, 0)
        outs[k].start()
        ref[AT:O1, :] = jnp.concatenate([pieces[f][7 * k] for f in range(2)], 0).astype(BF16)
    for k in (4, 5, 6):
        copies[k].wait()
    m = m_s[...].astype(F32)
    for ref, k, first in ((sp_ref, 0, 0), (sn_ref, 1, 6)):
        rows = jnp.swapaxes(o_s[k].reshape(OL, 8, NC), 0, 1)
        at = k * (NR - 8) + first
        for j, base in ((0, O1), (1, O2)):
            u = rows[first + j] * m[at + j : at + j + 1]
            ref[base : base + 128, :] = jnp.concatenate([u, jnp.zeros((8, NC), F32)], 0).astype(BF16)
        ref[MK:PAY, :] = mask_rows(m[at : at + 1], m[at + 1 : at + 2])
    for copy in outs:
        copy.wait()


INNER = NR // 8 - 2


def pick_columns(columns):
    k, at = iota((8 * len(columns), 8 * NC), 0), iota((8 * len(columns), 8 * NC), 1)
    wanted = jnp.zeros_like(k)
    for j, c in enumerate(columns):
        wanted = jnp.where(k // 8 == j, c, wanted)
    return ((at // NC == k % 8) & (at % NC == wanted)).astype(BF16)


def take_columns(pick, tiles):
    side = jnp.concatenate([t.astype(BF16) for t in tiles], 1)
    got = lax.dot_general(pick, side, (((1,), (1,)), ((), ())), preferred_element_type=F32)
    return jnp.concatenate([got, jnp.zeros_like(got)], 1)


def inner_kernel(
    x_hbm, mix_hbm, o_hbm, b_ref, m_ref, rim_hbm, w_hbm, z_hbm, top_ref, zc_ref, oc_ref, w_ref,
    x_s, z_s, o_s, mix_s, sems, rest,
):
    mix_copy = pltpu.make_async_copy(mix_hbm, mix_s, rest.at[0])
    ocean_copy = pltpu.make_async_copy(o_hbm, o_s, rest.at[1])
    rims = [
        pltpu.make_async_copy(
            rim_hbm.at[:, :, pl.ds(at, 8), :], z_s.at[:, :, pl.ds(at, 8), :], rest.at[2 + k]
        )
        for k, at in enumerate((0, NR - 8))
    ]

    def chunk(i):
        return pltpu.make_async_copy(x_hbm.at[:, :, pl.ds(i * 8 + 8, 8), :], x_s.at[i], sems.at[i])

    def leave(i):
        rows = pl.ds(pl.multiple_of(i * 8 + 8, 8), 8)
        return pltpu.make_async_copy(z_s.at[:, :, rows, :], z_hbm.at[:, :, rows, :], sems.at[INNER + i])

    mix_copy.start()
    for i in range(INNER):
        chunk(i).start()
    for copy in rims:
        copy.start()
    ocean_copy.start()
    weight_copy = pltpu.make_async_copy(w_hbm, w_ref, rest.at[4])
    weight_copy.start()
    mix_copy.wait()
    mix = (0.5 * mix_s[...]).astype(BF16)

    def step(i, carry):
        chunk(i).wait()
        store_rows(z_s, element_rows(x_s.at[i], mix, b_ref[...]), pl.multiple_of(i * 8 + 8, 8))
        leave(i).start()
        return carry

    lax.fori_loop(0, INNER, step, 0)
    for copy in rims:
        copy.wait()
    pick = pick_columns((0, NC - 1))

    def atm(i, carry):
        for f in range(2):
            got = take_columns(pick, [z_s[f, i * 8 + l] for l in range(8)])
            at = pl.multiple_of(f * LEV + i * 8, 8)
            for k in range(2):
                zc_ref[k, pl.ds(at, 8), :] = got[k * 8 : k * 8 + 8]
        return carry

    lax.fori_loop(0, LEV // 8, atm, 0, unroll=3)
    for f in range(2):
        top_ref[f] = z_s[f, LEV - 1]
    ocean_copy.wait()
    wet = m_ref[...].astype(F32)
    pick = pick_columns((0, 1, NC - 2, NC - 1))

    def ocean(i, carry):
        tiles = [i * 8 + l for l in range(8)]
        got = take_columns(pick, [wet * o_s[t // LO, t % LO] for t in tiles])
        for k in range(4):
            oc_ref[k, pl.ds(pl.multiple_of(i * 8, 8), 8), :] = got[k * 8 : k * 8 + 8]
        return carry

    lax.fori_loop(0, OL // 8, ocean, 0, unroll=3)
    oc_ref[:, OL:, :] = jnp.zeros((4, 8, NC), F32)
    for i in range(INNER):
        leave(i).wait()
    weight_copy.wait()


def cols_kernel(zc_ref, oc_ref, m_ref, rp_ref, rn_ref, ss_ref, sn_ref):
    lane = iota((144, NC), 1)
    place = lane % 4
    rp_at, rn_at = rp_ref[AT:O1, :].astype(F32), rn_ref[AT:O1, :].astype(F32)
    before, after = rp_ref[O2:MK, :].astype(F32), rn_ref[O1:O2, :].astype(F32)
    olane = iota((128, NC), 1)
    row = iota((64, NC), 0)
    m_before, m_after = rp_ref[MK:PAY, :].astype(F32)[1:2], rn_ref[MK:PAY, :].astype(F32)[0:1]
    tail = jnp.where(row == 0, m_before, jnp.where(row == 1, m_after, 0.0))
    m_t = jnp.transpose(jnp.concatenate([m_ref[...].astype(F32), tail], 0))
    for ref, c_at, ocs in ((ss_ref, 0, (0, 1)), (sn_ref, 127, (126, 127))):
        z = zc_ref[0 if c_at == 0 else 1]
        nxt = jnp.where(lane == 63, rn_at[:, c_at : c_at + 1], pltpu.roll(z, 127, 1))
        prv = jnp.where(lane == 0, rp_at[:, c_at : c_at + 1], pltpu.roll(z, 1, 1))
        z = jnp.where(place == 3, (z + nxt) * 0.5, jnp.where(place == 0, (z + prv) * 0.5, z))
        ref[AT:O1, :] = z.astype(BF16)
        for k, c in enumerate(ocs):
            source = c if c < 2 else c - 124
            u = jnp.where(
                olane < 64,
                oc_ref[source],
                jnp.where(olane == 64, before[:, c : c + 1], jnp.where(olane == 65, after[:, c : c + 1], 0.0)),
            )
            base = (O1, O2)[k]
            ref[base : base + 128, :] = u.astype(BF16)
        ref[MK:PAY, :] = mask_rows(m_t[ocs[0] : ocs[0] + 1], m_t[ocs[1] : ocs[1] + 1])


def averaged(z, nxt, prv, place):
    return jnp.where(place == 3, (z + nxt) * 0.5, jnp.where(place == 0, (z + prv) * 0.5, z))


def stiffness(z, h_prev, h_next, c_south, c_north):
    row, lane = iota((NR, NC), 0), iota((NR, NC), 1)
    nxt = jnp.where(row == NR - 1, h_next, pltpu.roll(z, NR - 1, 0))
    prv = jnp.where(row == 0, h_prev, pltpu.roll(z, 1, 0))
    z = averaged(z, nxt, prv, row % 4)
    nxt = jnp.where(lane == NC - 1, c_north, pltpu.roll(z, NC - 1, 1))
    prv = jnp.where(lane == 0, c_south, pltpu.roll(z, 1, 1))
    return averaged(z, nxt, prv, lane % 4)


def surface_kernel(z_ref, rp_ref, rn_ref, cs_ref, cn_ref, s_ref):
    rp, rn = rp_ref[AT:O1, :].astype(F32), rn_ref[AT:O1, :].astype(F32)
    cs, cn = cs_ref[AT:O1, :].astype(F32), cn_ref[AT:O1, :].astype(F32)
    for f in range(2):
        top = f * LEV + LEV - 8
        south = jnp.transpose(cs[top : top + 8])[:NR, 7:8]
        north = jnp.transpose(cn[top : top + 8])[:NR, 7:8]
        last = top + 7
        s = stiffness(z_ref[f], rp[last : last + 1], rn[last : last + 1], south, north)
        s_ref[f] = s.astype(BF16)


def edge_spread(tiles, scale):
    k, c = iota((2 * tiles, tiles * NC), 0), iota((2 * tiles, tiles * NC), 1)
    mine = k % tiles == c // NC
    end = c % NC == jnp.where(k < tiles, 0, NC - 1)
    return jnp.where(mine & end, scale, 0.0).astype(BF16)


def add_ends(x, first, last):
    row = iota((8, NC), 0)
    return jnp.concatenate(
        [
            x[0:8] + jnp.where(row == 0, first, 0.0),
            x[8 : NR - 8],
            x[NR - 8 :] + jnp.where(row == 7, last, 0.0),
        ],
        0,
    )


def column_halo(columns, spread):
    return lax.dot_general(columns, spread, (((0,), (0,)), ((), ())), preferred_element_type=F32)[:NR]


FB = 8
KEPT = 16


def finish_kernel(
    z_hbm, rp_ref, rn_ref, cs_ref, cn_ref, new_ref, w_hbm, mid_hbm, o_hbm, ocean_hbm, w_ref,
    z_s, o_s, h_ref, sems, level_sem, weight_sem,
):
    del mid_hbm
    weight_copy = pltpu.make_async_copy(w_hbm.at[pl.ds(NR - KEPT, KEPT)], w_ref, weight_sem)
    level = pltpu.make_async_copy(new_ref, ocean_hbm.at[:, 0], level_sem)
    level.start()

    def enter(i):
        return pltpu.make_async_copy(z_hbm.at[:, pl.ds(i * FB, FB)], z_s.at[i], sems.at[LEV // FB + i])

    for i in range(LEV // FB):
        enter(i).start()
    weight_copy.start()
    for k, ref in enumerate((rp_ref, rn_ref, cs_ref, cn_ref)):
        h_ref[k] = ref[AT:O1, :].astype(F32)
    spread = edge_spread(2 * FB, 0.5)
    row, lane = iota((NR, NC), 0), iota((NR, NC), 1)

    def weights(place, at, end):
        low = jnp.where((place == 0) & (at != 0), 0.5, 0.0)
        high = jnp.where((place == 3) & (at != end), 0.5, 0.0)
        return jnp.where((place == 0) | (place == 3), 0.5, 1.0), low, high

    own_r, low_r, high_r = weights(row % 4, row, NR - 1)
    own_c, low_c, high_c = weights(lane % 4, lane, NC - 1)

    def chunk(i):
        return pltpu.make_async_copy(o_s.at[i], o_hbm.at[:, pl.ds(i * FB, FB)], sems.at[i])

    def step(i, carry):
        enter(i).wait()

        def halo(k, f):
            return h_ref[k, pl.ds(pl.multiple_of(f * LEV + i * FB, 8), FB), :]

        columns = jnp.concatenate([halo(2, 0), halo(2, 1), halo(3, 0), halo(3, 1)], 0).astype(BF16)
        edges = column_halo(columns, spread)
        for f in range(2):
            first, last = 0.5 * halo(0, f), 0.5 * halo(1, f)
            for l in range(FB):
                t = z_s[i, f, l]
                t = own_r * t + high_r * pltpu.roll(t, NR - 1, 0) + low_r * pltpu.roll(t, 1, 0)
                t = add_ends(t, first[l : l + 1], last[l : l + 1])
                t = own_c * t + high_c * pltpu.roll(t, NC - 1, 1) + low_c * pltpu.roll(t, 1, 1)
                tile = f * FB + l
                o_s[i, f, l] = t + edges[:, tile * NC : (tile + 1) * NC]
        chunk(i).start()
        return carry

    lax.fori_loop(0, LEV // FB, step, 0)
    level.wait()
    weight_copy.wait()
    for i in range(LEV // FB):
        chunk(i).wait()


OB = 12


def ocean_kernel(
    at_ref, k_ref, o_hbm, m_ref, kc_ref, sp_ref, sn_ref, ss_ref, st_ref, rp_ref, rn_ref, cs_ref, cn_ref, fo_ref,
    out_hbm, first_ref, out_s, row_ref, col_ref, sems,
):
    def enter(i):
        return pltpu.make_async_copy(o_hbm.at[:, pl.ds(i * OB, OB)], out_s.at[i], sems.at[LO // OB + i])

    for i in range(LO // OB):
        enter(i).start()
    is_top, is_low = at_ref[0] == 7, at_ref[0] == 0
    lane = iota((128, NC), 1)

    def part(ref, base):
        return ref[base : base + 128, :].astype(F32)

    def masks(ref):
        m = ref[MK:PAY, :].astype(F32)
        return m[0:1], m[1:2]

    fr, fc = iota((NC, NC), 0), iota((NC, NC), 1)
    flip = (((fr < 64) & (fc == 63 - fr)) | ((fr == 64) & (fc == 65)) | ((fr == 65) & (fc == 64))).astype(BF16)
    turned = dot(fo_ref[...], flip)
    n0 = jnp.where(is_top, turned[O2:MK], part(cn_ref, O1))
    n1 = jnp.where(is_top, turned[O1:O2], part(cn_ref, O2))
    mc0, mc1 = masks(cn_ref)
    mn0 = jnp.where(is_top, turned[MK + 1 : MK + 2], mc0)
    mn1 = jnp.where(is_top, turned[MK : MK + 1], mc1)
    keep = jnp.where(is_low, 0.0, 1.0)
    s2, s1 = part(cs_ref, O1) * keep, part(cs_ref, O2) * keep
    ms2, ms1 = masks(cs_ref)
    ms2, ms1 = ms2 * keep, ms1 * keep
    um2, um1 = part(rp_ref, O1), part(rp_ref, O2)
    mm2, mm1 = masks(rp_ref)
    u64, u65 = part(rn_ref, O1), part(rn_ref, O2)
    m64, m65 = masks(rn_ref)
    own0, own63 = part(sp_ref, O1), part(sn_ref, O2)
    mo0, mo63 = masks(sp_ref)[0], masks(sn_ref)[1]
    west0, east127 = part(ss_ref, O1), part(st_ref, O2)
    mw0, me127 = masks(ss_ref)[0], masks(st_ref)[1]
    at, l60 = iota((128, LO), 0), iota((128, LO), 1)
    kap = sum(
        jnp.sum(jnp.where(at - f * LO == l60, kc_ref[f : f + 1, :], 0.0), 1, keepdims=True) for f in range(2)
    )

    def along(u, low, high, end):
        where = lane[: u.shape[0]]
        return jnp.where(where == end, high, pltpu.roll(u, 127, 1)) + jnp.where(
            where == 0, low, pltpu.roll(u, 1, 1)
        )

    def advance(u, wet, inner, outer, m_inner, m_outer, low, high, m_low, m_high, end):
        total = inner + outer + along(u, low, high, end)
        m8 = jnp.broadcast_to(wet, (8, NC))
        count = m_inner + m_outer + along(m8, m_low, m_high, end)[0:1]
        return u + kap * (wet * total - count * u)

    def corner(x, at):
        return x[:, at : at + 1]

    row_ref[0] = um1
    row_ref[1] = u64
    row_ref[2] = advance(
        um1, mm1, own0, um2, mo0, mm2, corner(s1, 64), corner(n0, 64), corner(ms1, 64), corner(mn0, 64), 127
    )
    row_ref[3] = advance(
        u64, m64, own63, u65, mo63, m65, corner(s1, 65), corner(n0, 65), corner(ms1, 65), corner(mn0, 65), 127
    )
    west = advance(
        s1, ms1, west0, s2, mw0, ms2, corner(s1, 64), corner(s1, 65), corner(ms1, 64), corner(ms1, 65), 63
    )
    east = advance(
        n0, mn0, east127, n1, me127, mn1, corner(n0, 64), corner(n0, 65), corner(mn0, 64), corner(mn0, 65), 63
    )
    here = iota((NR, NC), 1)
    for sub, (low, high) in enumerate(((s1, n0), (west, east))):
        low, high = jnp.transpose(low)[:NR], jnp.transpose(high)[:NR]
        for f in range(2):
            col_ref[2 * sub + f] = jnp.where(
                here < 64, pltpu.roll(low, (NC - LO * f) % NC, 1), pltpu.roll(high, (NC + 64 - LO * f) % NC, 1)
            )
    a, b = iota((NC, NC), 0), iota((NC, NC), 1)
    ends = ((a == 0) & (b == 0)) | ((a == 64) & (b == NC - 1))
    ns = jnp.concatenate([(jnp.abs(a - b) == 1).astype(BF16), ends.astype(BF16)], 0)
    wet = m_ref[...].astype(F32)
    r, c = iota((NR, NC), 0), iota((NR, NC), 1)
    m_north = jnp.transpose(jnp.broadcast_to(mn0, (8, NC)))[:NR, 0:1]
    m_south = jnp.transpose(jnp.broadcast_to(ms1, (8, NC)))[:NR, 0:1]
    count = jnp.where(r == NR - 1, m64, pltpu.roll(wet, NR - 1, 0)) + jnp.where(
        r == 0, mm1, pltpu.roll(wet, 1, 0)
    )
    count = count + jnp.where(c == NC - 1, m_north, pltpu.roll(wet, NC - 1, 1))
    count = count + jnp.where(c == 0, m_south, pltpu.roll(wet, 1, 1))

    places = [(f, l) for f in range(2) for l in range(OB)]

    def chunk(i):
        return pltpu.make_async_copy(out_s.at[i], out_hbm.at[:, pl.ds(i * OB, OB)], sems.at[i])

    def step(i, carry):
        enter(i).wait()
        ts = [out_s[i, f, l] for f, l in places]
        for sub in range(2):
            us = [wet * t for t in ts]
            halos = [pltpu.roll(col_ref[2 * sub + f], (NC - i * OB - l) % NC, 1) for f, l in places]
            side = jnp.concatenate([jnp.concatenate(us, 0), jnp.concatenate(halos, 0)], 1)
            cols = dot(side.astype(BF16), ns)
            for j, (f, l) in enumerate(places):
                level = i * OB + l
                here = pl.ds(f * LO + level, 1)
                u = us[j]
                total = pltpu.roll(u, NR - 1, 0) + pltpu.roll(u, 1, 0) + cols[j * NR : (j + 1) * NR]
                total = add_ends(
                    total, row_ref[2 * sub, here, :] - u[NR - 1 :], row_ref[2 * sub + 1, here, :] - u[0:1]
                )
                ts[j] = ts[j] + (k_ref[f, level] * wet) * (total - count * ts[j])
        for j, (f, l) in enumerate(places):
            out_s[i, f, l] = ts[j]
        chunk(i).start()
        return carry

    lax.fori_loop(0, LO // OB, step, 0)
    for f in range(2):
        first_ref[f] = out_s[0, f, 0]
    for i in range(LO // OB):
        chunk(i).wait()


def send_map_kernel(at_ref, ids_ref, pass_hbm, out_ref, scol_ref, through_hbm):
    del pass_hbm, through_hbm
    gx, gy = at_ref[0], at_ref[1]
    block = ids_ref[:, pl.ds(pl.multiple_of((gx // 2) * 128, 128), 128)]
    block = pltpu.roll(block, (gx % 2) * 64, 1)
    rows = iota((32, 128), 0)
    tile_row, lane = iota((128, 128), 0), iota((128, 128), 1)
    before = (tile_row < lane).astype(BF16)
    ones = jnp.ones((128, 128), BF16)
    earlier = jnp.zeros((128, 128), F32)
    tiles, ranks = [], []
    for t in range(TOP):
        ids = jnp.sum(jnp.where(rows == gy * 4 + t, block, 0), 0, keepdims=True)
        hit = (ids // 64 == tile_row) & (lane < 64)
        hot = hit.astype(BF16)
        rank = dot(hot, before) + earlier
        earlier = earlier + dot(hot, ones)
        ranks.append(jnp.sum(jnp.where(hit, rank, 0.0), 0, keepdims=True))
        tiles.append((ids // 64).astype(F32))
    place = iota((8, 128), 0)
    stack = jnp.zeros((8, 128), F32)
    for t in range(TOP):
        stack = jnp.where(place == t, tiles[t], jnp.where(place == t + 4, ranks[t], stack))
    spread = (iota((128, 512), 1) // 8 == iota((128, 512), 0)).astype(BF16)
    wide = dot(stack.astype(BF16), spread)
    col, row8 = iota((8, 512), 1), iota((8, 512), 0)
    wide = jnp.where(row8 % 4 == (col // 2) % 4, wide * jnp.where(row8 < 4, 10.0, 2.0), 0.0)
    slot = jnp.sum(wide, 0, keepdims=True) + (iota((1, 512), 1) % 2).astype(F32)
    out_ref[...] = jnp.where(slot.astype(jnp.int32) == iota((SLOTS, 512), 0), 1.0, 0.0).astype(BF16)
    scol_ref[...] = jnp.transpose(jnp.broadcast_to(slot, (128, 512)))


def receive_map_kernel(at_ref, ids_ref, take_ref, give_ref):
    own_tile = at_ref[0] * 8 + at_ref[1]
    blocks = 8
    row, lane = iota((128, 128), 0), iota((128, 128), 1)
    halves = (row // 64) == (lane // 64)
    before = jnp.concatenate([(halves & (row < lane)).astype(BF16), halves.astype(BF16)], 1)
    r, c = iota((256, 256), 0), iota((256, 256), 1)
    lower = ((r // 4 == c // 4) & (c % 4 < r % 4)).astype(BF16)
    sr, sc = iota((160, 160), 0), iota((160, 160), 1)
    pick = (((sr // 10) % 8 == (sc % 32) // 4) & ((sr % 10) // 2 == sc // 32)).astype(BF16)
    side = iota((160, NC), 0) // 80 == iota((160, NC), 1) // 64
    ids = jnp.concatenate([ids_ref[:, b * NC : (b + 1) * NC] for b in range(blocks)], 0)
    hit = ids // 64 == own_tile
    counts = dot(hit.astype(BF16), before)
    rank = counts[:, 0:NC] + dot(lower, counts[:, NC:].astype(BF16))
    value = (ids % 64 + 1).astype(F32)
    held = [jnp.where(hit & (rank == float(k)), value, 0.0) for k in range(CAP)]
    stacked = jnp.concatenate(
        [jnp.concatenate([h[b * 32 : (b + 1) * 32] for h in held], 0) for b in range(blocks)], 1
    )
    found = dot(pick, stacked.astype(BF16))
    found = jnp.concatenate(
        [jnp.where(side, found[:, b * NC : (b + 1) * NC], 0.0) for b in range(blocks)], 0
    )
    local = dot(found.astype(BF16), jnp.ones((NC, NC), BF16)).astype(jnp.int32)
    row, col = iota((SLOTS, NC), 0), iota((SLOTS, NC), 1)
    give = jnp.where((local - 1 == col % 64) & (row % 2 == col // 64), 1.0, 0.0)
    give_ref[...] = give.astype(BF16)
    for b in range(SLOTS // NC):
        take_ref[:, b * NC : (b + 1) * NC] = jnp.transpose(give[b * NC : (b + 1) * NC]).astype(BF16)


def pack_kernel(c_ref, map_ref, fold_ref, out_ref):
    del fold_ref
    out_ref[...] = dot(map_ref[...], c_ref[...].astype(BF16)).astype(BF16)


def ocean_surface_kernel(in_ref, take_ref, give_ref, m_ref, first_ref, new_ref, back_ref):
    forcing = dot(take_ref[...], in_ref[...])
    wet = 0.25 * m_ref[...].astype(F32)
    news = []
    for f in range(2):
        new = first_ref[f] + wet * forcing[f * NR : (f + 1) * NR]
        new_ref[f] = new
        news.append(new)
    sea = jnp.concatenate(news, 0).astype(BF16)
    back_ref[...] = dot(give_ref[...], sea).astype(BF16)


WB = 8


def return_kernel(in_ref, scol_ref, w_hbm, kept_ref, out_ref, w_s, e_s, p_s, sems):
    def chunk(i):
        return pltpu.make_async_copy(w_hbm.at[pl.ds(i * WB, WB)], w_s.at[i], sems.at[i])

    far = (NR - KEPT) // WB
    for i in range(far):
        chunk(i).start()
    total = jnp.zeros((512, 128), F32)
    slot = scol_ref[...].astype(jnp.int32)
    for b in range(SLOTS // 128):
        hot = jnp.where(slot == iota((512, 128), 1) + b * 128, 1.0, 0.0).astype(BF16)
        total = total + dot(hot, in_ref[b * 128 : (b + 1) * 128, :])
    term = (iota((512, 128), 0) % 8) // 2
    e_s[...] = jnp.concatenate([jnp.where(term == t, total, 0.0) for t in range(TOP)], 1)

    def apply(x, weight):
        rows = pl.ds(pl.multiple_of(x * 8, 8), 8)
        p_s[rows, :] = dot(e_s[rows, :].astype(BF16), weight.reshape(TOP * NC, NC))

    def near_step(i, carry):
        for k in range(WB):
            apply(NR - KEPT + i * WB + k, kept_ref[i * WB + k])
        return carry

    def far_step(i, carry):
        chunk(i).wait()
        for k in range(WB):
            apply(i * WB + k, w_s[i, k])
        return carry

    lax.fori_loop(0, KEPT // WB, near_step, 0)
    lax.fori_loop(0, far, far_step, 0)
    r, c = iota((128, 512), 0), iota((128, 512), 1)
    gather = jnp.where((c // 8 == r % NR) & (c % 2 == r // NR), 1.0, 0.0).astype(BF16)
    parts = p_s[...]
    high = parts.astype(BF16)
    low = (parts - high.astype(F32)).astype(BF16)
    done = dot(jnp.concatenate([gather, gather], 1), jnp.concatenate([high, low], 0))
    for f in range(2):
        out_ref[f] = done[f * NR : (f + 1) * NR]


def shape(dims, dtype=F32):
    return jax.ShapeDtypeStruct(dims, dtype)


def shifted(x, axis, by):
    count = lax.axis_size(axis)
    return lax.ppermute(x, axis, [(i, (i + by) % count) for i in range(count)])


def per_device(atm_state, ocean_state, land_mask, elem_op, column_mix, kappa, remap_weight, intersection):
    gx, gy = lax.axis_index("gx"), lax.axis_index("gy")
    at = jnp.stack([gx, gy]).astype(jnp.int32)
    smem = pl.BlockSpec(memory_space=pltpu.SMEM)
    full = whole((PAY, NC))

    vmem = pl.BlockSpec(memory_space=pltpu.VMEM)
    hbm = pl.BlockSpec(memory_space=pl.ANY)

    def pinned(x):
        return pltpu.with_memory_space_constraint(x, pltpu.HBM)

    atm_in, ocean_in, mask_in = pinned(atm_state), pinned(ocean_state), pinned(land_mask)
    mix_in, elem_in = pinned(column_mix), pinned(elem_op)
    payload = shape((PAY, NC), BF16)
    rim, send_next, send_prev, element = pl.pallas_call(
        atm_rim_kernel,
        in_specs=[hbm] * 5,
        out_specs=[hbm] + [vmem] * 3,
        out_shape=[pltpu.HBM(atm_state.shape, F32), payload, payload, shape((512, 512), BF16)],
        scratch_shapes=[
            pltpu.VMEM((2, 2, LEV, 8, NC), F32),
            pltpu.VMEM((2, 2, LO, 8, NC), F32),
            pltpu.VMEM((NR, NC), jnp.int32),
            pltpu.VMEM((LEV, LEV), F32),
            pltpu.VMEM((16, 16), F32),
            pltpu.VMEM((2, 2, LEV, 8, NC), F32),
            pltpu.SemaphoreType.DMA((9,)),
        ],
        compiler_params=params(16),
        name="atm_rim",
    )(atm_in, ocean_in, mask_in, mix_in, elem_in)

    from_prev = shifted(send_next, "gx", 1)
    from_next = shifted(send_prev, "gx", -1)

    weights = remap_weight[:, 0]
    weights_in = pinned(weights)
    z, top_level, z_cols, ocean_cols, near_weights = pl.pallas_call(
        inner_kernel,
        in_specs=[hbm, hbm, hbm, vmem, vmem, hbm, hbm],
        out_specs=[hbm] + [vmem] * 4,
        out_shape=[
            pltpu.HBM(atm_state.shape, F32),
            shape((2, NR, NC)),
            shape((2, 144, NC)),
            shape((4, 128, NC)),
            pltpu.VMEM(weights.shape, BF16),
        ],
        scratch_shapes=[
            pltpu.VMEM((INNER, 2, LEV, 8, NC), F32),
            pltpu.VMEM(atm_state.shape, F32),
            pltpu.VMEM(ocean_state.shape, F32),
            pltpu.VMEM((LEV, LEV), F32),
            pltpu.SemaphoreType.DMA((2 * INNER,)),
            pltpu.SemaphoreType.DMA((5,)),
        ],
        input_output_aliases={5: 0},
        compiler_params=params(14),
        cost_estimate=pl.CostEstimate(flops=1000000000, bytes_accessed=14000000, transcendentals=0),
        name="inner",
    )(atm_in, mix_in, ocean_in, element, land_mask, rim, weights_in)

    send_south, send_north = pl.pallas_call(
        cols_kernel,
        out_shape=[shape((PAY, NC), BF16)] * 2,
        compiler_params=params(),
        name="cols",
    )(z_cols, ocean_cols, land_mask, from_prev, from_next)

    from_south = shifted(send_north, "gy", 1)
    from_north = shifted(send_south, "gy", -1)
    gx_count, gy_count = lax.axis_size("gx"), lax.axis_size("gy")
    top = gy_count - 1
    folded = lax.ppermute(
        send_north, ("gx", "gy"), [(i * gy_count + top, (gx_count - 1 - i) * gy_count + top) for i in range(gx_count)]
    )

    ids = jnp.transpose(intersection, (1, 2, 0)).reshape(32, 1024)
    send_map, slot_col, from_north = pl.pallas_call(
        send_map_kernel,
        in_specs=[smem, vmem, hbm],
        out_specs=[vmem, vmem, hbm],
        out_shape=[shape((SLOTS, 512), BF16), shape((512, 128)), payload],
        input_output_aliases={2: 2},
        compiler_params=params(),
        cost_estimate=pl.CostEstimate(flops=4000000, bytes_accessed=4200000, transcendentals=0),
        name="send_map",
    )(at, ids, from_north)

    surface = pl.pallas_call(
        surface_kernel,
        in_specs=[vmem] * 5,
        out_shape=shape((2, NR, NC), BF16),
        compiler_params=params(),
        name="surface",
    )(top_level, from_prev, from_next, from_south, from_north)

    products = lax.dot_general(
        near_weights, surface, (((3,), (2,)), ((0,), (1,))), preferred_element_type=F32
    )
    contrib = jnp.transpose(products, (0, 1, 3, 2)).reshape(2 * ENT, NC)
    outgoing = pl.pallas_call(
        pack_kernel,
        in_specs=[vmem, vmem, hbm],
        out_shape=shape((SLOTS, NC), BF16),
        compiler_params=params(),
        name="pack",
    )(contrib, send_map, folded)
    incoming = lax.all_to_all(
        outgoing.reshape(TILES, CAP, 2, NC), ("gx", "gy"), split_axis=0, concat_axis=0, tiled=True
    ).reshape(SLOTS, NC)

    ocean_mid, first_level = pl.pallas_call(
        ocean_kernel,
        in_specs=[smem, smem, hbm] + [vmem] * 11,
        out_specs=[hbm, vmem],
        out_shape=[pltpu.HBM(ocean_state.shape, F32), shape((2, NR, NC))],
        scratch_shapes=[
            pltpu.VMEM((LO // OB, 2, OB, NR, NC), F32),
            pltpu.VMEM((4, 128, NC), F32),
            pltpu.VMEM((4, NR, NC), F32),
            pltpu.SemaphoreType.DMA((2 * (LO // OB),)),
        ],
        compiler_params=params(16),
        cost_estimate=pl.CostEstimate(flops=30000000, bytes_accessed=8000000, transcendentals=0),
        name="ocean",
    )(
        at[1:], kappa, ocean_in, land_mask, kappa, send_prev, send_next, send_south, send_north,
        from_prev, from_next, from_south, from_north, folded,
    )

    take, give = pl.pallas_call(
        receive_map_kernel,
        in_specs=[smem, vmem],
        out_shape=[shape((128, SLOTS), BF16), shape((SLOTS, 128), BF16)],
        compiler_params=params(),
        cost_estimate=pl.CostEstimate(flops=4000000, bytes_accessed=4200000, transcendentals=0),
        name="receive_map",
    )(at, ids)

    new_level, back_out = pl.pallas_call(
        ocean_surface_kernel,
        out_shape=[shape((2, NR, NC)), shape((SLOTS, NC), BF16)],
        compiler_params=params(),
        name="ocean_surface",
    )(incoming, take, give, land_mask, first_level)

    back_in = lax.all_to_all(
        back_out.reshape(TILES, CAP, 2, NC), ("gx", "gy"), split_axis=0, concat_axis=0, tiled=True
    ).reshape(SLOTS, NC)

    atm_next, ocean_next, kept_weights = pl.pallas_call(
        finish_kernel,
        in_specs=[hbm] + [vmem] * 5 + [hbm] * 2,
        out_specs=[hbm, hbm, vmem],
        out_shape=[
            pltpu.HBM(atm_state.shape, F32),
            pltpu.HBM(ocean_state.shape, F32),
            shape((KEPT, TOP, NC, NC), BF16),
        ],
        input_output_aliases={7: 1},
        scratch_shapes=[
            pltpu.VMEM((LEV // FB, 2, FB, NR, NC), F32),
            pltpu.VMEM((LEV // FB, 2, FB, NR, NC), F32),
            pltpu.VMEM((4, 144, NC), F32),
            pltpu.SemaphoreType.DMA((2 * (LEV // FB),)),
            pltpu.SemaphoreType.DMA(()),
            pltpu.SemaphoreType.DMA(()),
        ],
        compiler_params=params(16),
        cost_estimate=pl.CostEstimate(flops=20000000, bytes_accessed=9400000, transcendentals=0),
        name="finish",
    )(pinned(z), from_prev, from_next, from_south, from_north, new_level, weights_in, ocean_mid)

    returned = pl.pallas_call(
        return_kernel,
        in_specs=[vmem, vmem, hbm, vmem],
        out_specs=vmem,
        out_shape=shape((2, NR, NC)),
        scratch_shapes=[
            pltpu.VMEM(((NR - KEPT) // WB, WB, TOP, NC, NC), BF16),
            pltpu.VMEM((512, 512), F32),
            pltpu.VMEM((512, NC), F32),
            pltpu.SemaphoreType.DMA((NR // WB,)),
        ],
        compiler_params=params(16),
        name="returned",
    )(back_in, slot_col, weights_in, kept_weights)
    return atm_next, ocean_next, returned


def solution(mesh):
    placed = (
        P(None, None, "gx", "gy"),
        P(None, None, "gx", "gy"),
        P("gx", "gy"),
        P(),
        P(),
        P(),
        P("gx", "gy", None, None, None),
        P(),
    )
    return jax.shard_map(
        per_device,
        mesh=mesh,
        in_specs=placed,
        out_specs=(P(None, None, "gx", "gy"), P(None, None, "gx", "gy"), P(None, "gx", "gy")),
        check_vma=False,
    )
```

```python
import jax
import jax.numpy as jnp
from jax import lax
from jax.experimental import pallas as pl
from jax.experimental.pallas import tpu as pltpu
from jax.sharding import PartitionSpec as P

F32, BF16 = jnp.float32, jnp.bfloat16
LEV, LO, NR, NC = 72, 60, 64, 128
AT, O1, O2, MK, PAY = 0, 144, 272, 400, 416
OL = 2 * LO
TOP, CAP, TILES = 4, 5, 128
ENT = NR * TOP
SLOTS = TILES * CAP * 2
MIB = 1024 * 1024


def iota(shape, dim):
    return lax.broadcasted_iota(jnp.int32, shape, dim)


def dot(a, b):
    return jnp.dot(a, b, preferred_element_type=F32)


def params(mib=6):
    return pltpu.CompilerParams(vmem_limit_bytes=mib * MIB)


def whole(shape):
    return pl.BlockSpec(shape, lambda *_: (0,) * len(shape))


def mask_rows(first, second):
    place = iota((16, NC), 0)
    return jnp.where(place == 0, first, jnp.where(place == 1, second, 0.0)).astype(BF16)


def element_rows(x_s, mix, b):
    fields = [jnp.swapaxes(x_s[f], 0, 1) for f in range(2)]
    ys = []
    for big in range(2):
        for f in range(2):
            x = jnp.concatenate([fields[f][big * 4 + k] for k in range(4)], 1)
            ys.append(x + dot(mix, x.astype(BF16)))
    y = jnp.concatenate(ys, 0)
    z = y + dot(y.astype(BF16), b)
    pieces = [[], []]
    for r in range(8):
        for f in range(2):
            at = ((r // 4) * 2 + f) * LEV
            pieces[f].append(z[at : at + LEV, (r % 4) * NC : (r % 4 + 1) * NC])
    return pieces


def store_rows(z_ref, pieces, at):
    for f in range(2):
        z_ref[f, :, pl.ds(at, 8), :] = jnp.swapaxes(jnp.stack(pieces[f], 0), 0, 1)


def atm_rim_kernel(
    x_hbm, o_hbm, m_hbm, mix_hbm, elem_hbm, z_hbm, sn_ref, sp_ref, b_ref, x_s, o_s, m_s, mix_s, elem_s, z_s, sems
):
    sources = (elem_hbm, mix_hbm, x_hbm.at[:, :, pl.ds(0, 8), :], x_hbm.at[:, :, pl.ds(NR - 8, 8), :], m_hbm) + tuple(
        o_hbm.at[:, :, pl.ds(at, 8), :] for at in (0, NR - 8)
    )
    targets = (elem_s, mix_s, x_s.at[0], x_s.at[1], m_s, o_s.at[0], o_s.at[1])
    copies = [pltpu.make_async_copy(a, b, sems.at[k]) for k, (a, b) in enumerate(zip(sources, targets))]
    outs = [
        pltpu.make_async_copy(z_s.at[k], z_hbm.at[:, :, pl.ds(k * (NR - 8), 8), :], sems.at[7 + k]) for k in range(2)
    ]
    for copy in copies:
        copy.start()
    copies[0].wait()
    row = iota((512, 16), 0)
    spread_in = (iota((512, 16), 1) == (row // 128) * 4 + row % 4).astype(BF16)
    col = iota((16, 512), 1)
    spread_out = (iota((16, 512), 0) == (col // 128) * 4 + col % 4).astype(BF16)
    elem = (0.5 * elem_s[...]).astype(BF16)
    half = lax.dot_general(spread_in, elem, (((1,), (1,)), ((), ())), preferred_element_type=F32)
    spread = dot(half.astype(BF16), spread_out)
    same = (iota((512, 512), 0) % 128) // 4 == (iota((512, 512), 1) % 128) // 4
    b = jnp.where(same, spread, 0.0).astype(BF16)
    b_ref[...] = b
    copies[1].wait()
    mix = (0.5 * mix_s[...]).astype(BF16)
    for k, ref in ((0, sp_ref), (1, sn_ref)):
        copies[2 + k].wait()
        pieces = element_rows(x_s.at[k], mix, b)
        store_rows(z_s.at[k], pieces, 0)
        outs[k].start()
        ref[AT:O1, :] = jnp.concatenate([pieces[f][7 * k] for f in range(2)], 0).astype(BF16)
    for k in (4, 5, 6):
        copies[k].wait()
    m = m_s[...].astype(F32)
    for ref, k, first in ((sp_ref, 0, 0), (sn_ref, 1, 6)):
        rows = jnp.swapaxes(o_s[k].reshape(OL, 8, NC), 0, 1)
        at = k * (NR - 8) + first
        for j, base in ((0, O1), (1, O2)):
            u = rows[first + j] * m[at + j : at + j + 1]
            ref[base : base + 128, :] = jnp.concatenate([u, jnp.zeros((8, NC), F32)], 0).astype(BF16)
        ref[MK:PAY, :] = mask_rows(m[at : at + 1], m[at + 1 : at + 2])
    for copy in outs:
        copy.wait()


INNER = NR // 8 - 2


def pick_columns(columns):
    k, at = iota((8 * len(columns), 8 * NC), 0), iota((8 * len(columns), 8 * NC), 1)
    wanted = jnp.zeros_like(k)
    for j, c in enumerate(columns):
        wanted = jnp.where(k // 8 == j, c, wanted)
    return ((at // NC == k % 8) & (at % NC == wanted)).astype(BF16)


def take_columns(pick, tiles):
    side = jnp.concatenate([t.astype(BF16) for t in tiles], 1)
    got = lax.dot_general(pick, side, (((1,), (1,)), ((), ())), preferred_element_type=F32)
    return jnp.concatenate([got, jnp.zeros_like(got)], 1)


def inner_kernel(
    x_hbm, mix_hbm, o_hbm, b_ref, m_ref, rim_hbm, w_hbm, z_hbm, top_ref, zc_ref, oc_ref, w_ref,
    x_s, z_s, o_s, mix_s, sems, rest,
):
    mix_copy = pltpu.make_async_copy(mix_hbm, mix_s, rest.at[0])
    ocean_copy = pltpu.make_async_copy(o_hbm, o_s, rest.at[1])
    rims = [
        pltpu.make_async_copy(
            rim_hbm.at[:, :, pl.ds(at, 8), :], z_s.at[:, :, pl.ds(at, 8), :], rest.at[2 + k]
        )
        for k, at in enumerate((0, NR - 8))
    ]

    def chunk(i):
        return pltpu.make_async_copy(x_hbm.at[:, :, pl.ds(i * 8 + 8, 8), :], x_s.at[i], sems.at[i])

    def leave(i):
        rows = pl.ds(pl.multiple_of(i * 8 + 8, 8), 8)
        return pltpu.make_async_copy(z_s.at[:, :, rows, :], z_hbm.at[:, :, rows, :], sems.at[INNER + i])

    mix_copy.start()
    for i in range(INNER):
        chunk(i).start()
    for copy in rims:
        copy.start()
    ocean_copy.start()
    weight_copy = pltpu.make_async_copy(w_hbm, w_ref, rest.at[4])
    weight_copy.start()
    mix_copy.wait()
    mix = (0.5 * mix_s[...]).astype(BF16)

    def step(i, carry):
        chunk(i).wait()
        store_rows(z_s, element_rows(x_s.at[i], mix, b_ref[...]), pl.multiple_of(i * 8 + 8, 8))
        leave(i).start()
        return carry

    lax.fori_loop(0, INNER, step, 0)
    for copy in rims:
        copy.wait()
    pick = pick_columns((0, NC - 1))

    def atm(i, carry):
        for f in range(2):
            got = take_columns(pick, [z_s[f, i * 8 + l] for l in range(8)])
            at = pl.multiple_of(f * LEV + i * 8, 8)
            for k in range(2):
                zc_ref[k, pl.ds(at, 8), :] = got[k * 8 : k * 8 + 8]
        return carry

    lax.fori_loop(0, LEV // 8, atm, 0, unroll=3)
    for f in range(2):
        top_ref[f] = z_s[f, LEV - 1]
    ocean_copy.wait()
    wet = m_ref[...].astype(F32)
    pick = pick_columns((0, 1, NC - 2, NC - 1))

    def ocean(i, carry):
        tiles = [i * 8 + l for l in range(8)]
        got = take_columns(pick, [wet * o_s[t // LO, t % LO] for t in tiles])
        for k in range(4):
            oc_ref[k, pl.ds(pl.multiple_of(i * 8, 8), 8), :] = got[k * 8 : k * 8 + 8]
        return carry

    lax.fori_loop(0, OL // 8, ocean, 0, unroll=3)
    oc_ref[:, OL:, :] = jnp.zeros((4, 8, NC), F32)
    for i in range(INNER):
        leave(i).wait()
    weight_copy.wait()


def cols_kernel(zc_ref, oc_ref, m_ref, rp_ref, rn_ref, ss_ref, sn_ref):
    lane = iota((144, NC), 1)
    place = lane % 4
    rp_at, rn_at = rp_ref[AT:O1, :].astype(F32), rn_ref[AT:O1, :].astype(F32)
    before, after = rp_ref[O2:MK, :].astype(F32), rn_ref[O1:O2, :].astype(F32)
    olane = iota((128, NC), 1)
    row = iota((64, NC), 0)
    m_before, m_after = rp_ref[MK:PAY, :].astype(F32)[1:2], rn_ref[MK:PAY, :].astype(F32)[0:1]
    tail = jnp.where(row == 0, m_before, jnp.where(row == 1, m_after, 0.0))
    m_t = jnp.transpose(jnp.concatenate([m_ref[...].astype(F32), tail], 0))
    for ref, c_at, ocs in ((ss_ref, 0, (0, 1)), (sn_ref, 127, (126, 127))):
        z = zc_ref[0 if c_at == 0 else 1]
        nxt = jnp.where(lane == 63, rn_at[:, c_at : c_at + 1], pltpu.roll(z, 127, 1))
        prv = jnp.where(lane == 0, rp_at[:, c_at : c_at + 1], pltpu.roll(z, 1, 1))
        z = jnp.where(place == 3, (z + nxt) * 0.5, jnp.where(place == 0, (z + prv) * 0.5, z))
        ref[AT:O1, :] = z.astype(BF16)
        for k, c in enumerate(ocs):
            source = c if c < 2 else c - 124
            u = jnp.where(
                olane < 64,
                oc_ref[source],
                jnp.where(olane == 64, before[:, c : c + 1], jnp.where(olane == 65, after[:, c : c + 1], 0.0)),
            )
            base = (O1, O2)[k]
            ref[base : base + 128, :] = u.astype(BF16)
        ref[MK:PAY, :] = mask_rows(m_t[ocs[0] : ocs[0] + 1], m_t[ocs[1] : ocs[1] + 1])


def averaged(z, nxt, prv, place):
    return jnp.where(place == 3, (z + nxt) * 0.5, jnp.where(place == 0, (z + prv) * 0.5, z))


def stiffness(z, h_prev, h_next, c_south, c_north):
    row, lane = iota((NR, NC), 0), iota((NR, NC), 1)
    nxt = jnp.where(row == NR - 1, h_next, pltpu.roll(z, NR - 1, 0))
    prv = jnp.where(row == 0, h_prev, pltpu.roll(z, 1, 0))
    z = averaged(z, nxt, prv, row % 4)
    nxt = jnp.where(lane == NC - 1, c_north, pltpu.roll(z, NC - 1, 1))
    prv = jnp.where(lane == 0, c_south, pltpu.roll(z, 1, 1))
    return averaged(z, nxt, prv, lane % 4)


def surface_kernel(z_ref, rp_ref, rn_ref, cs_ref, cn_ref, s_ref):
    rp, rn = rp_ref[AT:O1, :].astype(F32), rn_ref[AT:O1, :].astype(F32)
    cs, cn = cs_ref[AT:O1, :].astype(F32), cn_ref[AT:O1, :].astype(F32)
    for f in range(2):
        top = f * LEV + LEV - 8
        south = jnp.transpose(cs[top : top + 8])[:NR, 7:8]
        north = jnp.transpose(cn[top : top + 8])[:NR, 7:8]
        last = top + 7
        s = stiffness(z_ref[f], rp[last : last + 1], rn[last : last + 1], south, north)
        s_ref[f] = s.astype(BF16)


def edge_spread(tiles, scale):
    k, c = iota((2 * tiles, tiles * NC), 0), iota((2 * tiles, tiles * NC), 1)
    mine = k % tiles == c // NC
    end = c % NC == jnp.where(k < tiles, 0, NC - 1)
    return jnp.where(mine & end, scale, 0.0).astype(BF16)


def add_ends(x, first, last):
    row = iota((8, NC), 0)
    return jnp.concatenate(
        [
            x[0:8] + jnp.where(row == 0, first, 0.0),
            x[8 : NR - 8],
            x[NR - 8 :] + jnp.where(row == 7, last, 0.0),
        ],
        0,
    )


def column_halo(columns, spread):
    return lax.dot_general(columns, spread, (((0,), (0,)), ((), ())), preferred_element_type=F32)[:NR]


FB = 8
KEPT = 16


def finish_kernel(
    z_hbm, rp_ref, rn_ref, cs_ref, cn_ref, w_hbm, o_hbm, w_ref, z_s, o_s, h_ref, sems, weight_sem
):
    weight_copy = pltpu.make_async_copy(w_hbm.at[pl.ds(NR - KEPT, KEPT)], w_ref, weight_sem)

    def enter(i):
        return pltpu.make_async_copy(z_hbm.at[:, pl.ds(i * FB, FB)], z_s.at[i], sems.at[LEV // FB + i])

    for i in range(LEV // FB):
        enter(i).start()
    weight_copy.start()
    for k, ref in enumerate((rp_ref, rn_ref, cs_ref, cn_ref)):
        h_ref[k] = ref[AT:O1, :].astype(F32)
    spread = edge_spread(2 * FB, 0.5)
    row, lane = iota((NR, NC), 0), iota((NR, NC), 1)

    def weights(place, at, end):
        low = jnp.where((place == 0) & (at != 0), 0.5, 0.0)
        high = jnp.where((place == 3) & (at != end), 0.5, 0.0)
        return jnp.where((place == 0) | (place == 3), 0.5, 1.0), low, high

    own_r, low_r, high_r = weights(row % 4, row, NR - 1)
    own_c, low_c, high_c = weights(lane % 4, lane, NC - 1)

    def chunk(i):
        return pltpu.make_async_copy(o_s.at[i], o_hbm.at[:, pl.ds(i * FB, FB)], sems.at[i])

    def step(i, carry):
        enter(i).wait()

        def halo(k, f):
            return h_ref[k, pl.ds(pl.multiple_of(f * LEV + i * FB, 8), FB), :]

        columns = jnp.concatenate([halo(2, 0), halo(2, 1), halo(3, 0), halo(3, 1)], 0).astype(BF16)
        edges = column_halo(columns, spread)
        for f in range(2):
            first, last = 0.5 * halo(0, f), 0.5 * halo(1, f)
            for l in range(FB):
                t = z_s[i, f, l]
                t = own_r * t + high_r * pltpu.roll(t, NR - 1, 0) + low_r * pltpu.roll(t, 1, 0)
                t = add_ends(t, first[l : l + 1], last[l : l + 1])
                t = own_c * t + high_c * pltpu.roll(t, NC - 1, 1) + low_c * pltpu.roll(t, 1, 1)
                tile = f * FB + l
                o_s[i, f, l] = t + edges[:, tile * NC : (tile + 1) * NC]
        chunk(i).start()
        return carry

    lax.fori_loop(0, LEV // FB, step, 0)
    weight_copy.wait()
    for i in range(LEV // FB):
        chunk(i).wait()


OB = 12
HEAD = 1


def ocean_levels(
    begin, count_, out_hbm, out_s, row_ref, col_ref, sems,
    at_ref, k_ref, o_hbm, m_ref, kc_ref, sp_ref, sn_ref, ss_ref, st_ref, rp_ref, rn_ref, cs_ref, cn_ref, fo_ref,
):
    def enter(i):
        return pltpu.make_async_copy(o_hbm.at[:, pl.ds((begin + i) * OB, OB)], out_s.at[i], sems.at[count_ + i])

    for i in range(count_):
        enter(i).start()
    is_top, is_low = at_ref[0] == 7, at_ref[0] == 0
    lane = iota((128, NC), 1)

    def part(ref, base):
        return ref[base : base + 128, :].astype(F32)

    def masks(ref):
        m = ref[MK:PAY, :].astype(F32)
        return m[0:1], m[1:2]

    fr, fc = iota((NC, NC), 0), iota((NC, NC), 1)
    flip = (((fr < 64) & (fc == 63 - fr)) | ((fr == 64) & (fc == 65)) | ((fr == 65) & (fc == 64))).astype(BF16)
    turned = dot(fo_ref[...], flip)
    n0 = jnp.where(is_top, turned[O2:MK], part(cn_ref, O1))
    n1 = jnp.where(is_top, turned[O1:O2], part(cn_ref, O2))
    mc0, mc1 = masks(cn_ref)
    mn0 = jnp.where(is_top, turned[MK + 1 : MK + 2], mc0)
    mn1 = jnp.where(is_top, turned[MK : MK + 1], mc1)
    keep = jnp.where(is_low, 0.0, 1.0)
    s2, s1 = part(cs_ref, O1) * keep, part(cs_ref, O2) * keep
    ms2, ms1 = masks(cs_ref)
    ms2, ms1 = ms2 * keep, ms1 * keep
    um2, um1 = part(rp_ref, O1), part(rp_ref, O2)
    mm2, mm1 = masks(rp_ref)
    u64, u65 = part(rn_ref, O1), part(rn_ref, O2)
    m64, m65 = masks(rn_ref)
    own0, own63 = part(sp_ref, O1), part(sn_ref, O2)
    mo0, mo63 = masks(sp_ref)[0], masks(sn_ref)[1]
    west0, east127 = part(ss_ref, O1), part(st_ref, O2)
    mw0, me127 = masks(ss_ref)[0], masks(st_ref)[1]
    at, l60 = iota((128, LO), 0), iota((128, LO), 1)
    kap = sum(
        jnp.sum(jnp.where(at - f * LO == l60, kc_ref[f : f + 1, :], 0.0), 1, keepdims=True) for f in range(2)
    )

    def along(u, low, high, end):
        where = lane[: u.shape[0]]
        return jnp.where(where == end, high, pltpu.roll(u, 127, 1)) + jnp.where(
            where == 0, low, pltpu.roll(u, 1, 1)
        )

    def advance(u, wet, inner, outer, m_inner, m_outer, low, high, m_low, m_high, end):
        total = inner + outer + along(u, low, high, end)
        m8 = jnp.broadcast_to(wet, (8, NC))
        count = m_inner + m_outer + along(m8, m_low, m_high, end)[0:1]
        return u + kap * (wet * total - count * u)

    def corner(x, at):
        return x[:, at : at + 1]

    row_ref[0] = um1
    row_ref[1] = u64
    row_ref[2] = advance(
        um1, mm1, own0, um2, mo0, mm2, corner(s1, 64), corner(n0, 64), corner(ms1, 64), corner(mn0, 64), 127
    )
    row_ref[3] = advance(
        u64, m64, own63, u65, mo63, m65, corner(s1, 65), corner(n0, 65), corner(ms1, 65), corner(mn0, 65), 127
    )
    west = advance(
        s1, ms1, west0, s2, mw0, ms2, corner(s1, 64), corner(s1, 65), corner(ms1, 64), corner(ms1, 65), 63
    )
    east = advance(
        n0, mn0, east127, n1, me127, mn1, corner(n0, 64), corner(n0, 65), corner(mn0, 64), corner(mn0, 65), 63
    )
    here = iota((NR, NC), 1)
    for sub, (low, high) in enumerate(((s1, n0), (west, east))):
        low, high = jnp.transpose(low)[:NR], jnp.transpose(high)[:NR]
        for f in range(2):
            col_ref[2 * sub + f] = jnp.where(
                here < 64, pltpu.roll(low, (NC - LO * f) % NC, 1), pltpu.roll(high, (NC + 64 - LO * f) % NC, 1)
            )
    a, b = iota((NC, NC), 0), iota((NC, NC), 1)
    ends = ((a == 0) & (b == 0)) | ((a == 64) & (b == NC - 1))
    ns = jnp.concatenate([(jnp.abs(a - b) == 1).astype(BF16), ends.astype(BF16)], 0)
    wet = m_ref[...].astype(F32)
    r, c = iota((NR, NC), 0), iota((NR, NC), 1)
    m_north = jnp.transpose(jnp.broadcast_to(mn0, (8, NC)))[:NR, 0:1]
    m_south = jnp.transpose(jnp.broadcast_to(ms1, (8, NC)))[:NR, 0:1]
    count = jnp.where(r == NR - 1, m64, pltpu.roll(wet, NR - 1, 0)) + jnp.where(
        r == 0, mm1, pltpu.roll(wet, 1, 0)
    )
    count = count + jnp.where(c == NC - 1, m_north, pltpu.roll(wet, NC - 1, 1))
    count = count + jnp.where(c == 0, m_south, pltpu.roll(wet, 1, 1))

    places = [(f, l) for f in range(2) for l in range(OB)]

    def chunk(i):
        return pltpu.make_async_copy(out_s.at[i], out_hbm.at[:, pl.ds((begin + i) * OB, OB)], sems.at[i])

    def step(i, carry):
        enter(i).wait()
        ts = [out_s[i, f, l] for f, l in places]
        for sub in range(2):
            us = [wet * t for t in ts]
            halos = [pltpu.roll(col_ref[2 * sub + f], (NC - (begin + i) * OB - l) % NC, 1) for f, l in places]
            side = jnp.concatenate([jnp.concatenate(us, 0), jnp.concatenate(halos, 0)], 1)
            cols = dot(side.astype(BF16), ns)
            for j, (f, l) in enumerate(places):
                level = (begin + i) * OB + l
                here = pl.ds(f * LO + level, 1)
                u = us[j]
                total = pltpu.roll(u, NR - 1, 0) + pltpu.roll(u, 1, 0) + cols[j * NR : (j + 1) * NR]
                total = add_ends(
                    total, row_ref[2 * sub, here, :] - u[NR - 1 :], row_ref[2 * sub + 1, here, :] - u[0:1]
                )
                ts[j] = ts[j] + (k_ref[f, level] * wet) * (total - count * ts[j])
        for j, (f, l) in enumerate(places):
            out_s[i, f, l] = ts[j]
        chunk(i).start()
        return carry

    lax.fori_loop(0, count_, step, 0)
    for i in range(count_):
        chunk(i).wait()


def ocean_head_kernel(*refs):
    out_hbm, first_ref, out_s, row_ref, col_ref, sems = refs[14:]
    ocean_levels(0, HEAD, out_hbm, out_s, row_ref, col_ref, sems, *refs[:14])
    for f in range(2):
        first_ref[f] = out_s[0, f, 0]


def ocean_rest_kernel(*refs):
    new_ref, _, out_hbm, out_s, row_ref, col_ref, sems, level_sem = refs[14:]
    level = pltpu.make_async_copy(new_ref, out_hbm.at[:, 0], level_sem)
    level.start()
    ocean_levels(HEAD, LO // OB - HEAD, out_hbm, out_s, row_ref, col_ref, sems, *refs[:14])
    level.wait()


def send_map_kernel(at_ref, ids_ref, pass_hbm, out_ref, slot_ref, through_hbm):
    del pass_hbm, through_hbm
    gx, gy = at_ref[0], at_ref[1]
    block = ids_ref[:, pl.ds(pl.multiple_of((gx // 2) * 128, 128), 128)]
    block = pltpu.roll(block, (gx % 2) * 64, 1)
    rows = iota((32, 128), 0)
    tile_row, lane = iota((128, 128), 0), iota((128, 128), 1)
    before = (tile_row < lane).astype(BF16)
    ones = jnp.ones((128, 128), BF16)
    earlier = jnp.zeros((128, 128), F32)
    tiles, ranks = [], []
    for t in range(TOP):
        ids = jnp.sum(jnp.where(rows == gy * 4 + t, block, 0), 0, keepdims=True)
        hit = (ids // 64 == tile_row) & (lane < 64)
        hot = hit.astype(BF16)
        rank = dot(hot, before) + earlier
        earlier = earlier + dot(hot, ones)
        ranks.append(jnp.sum(jnp.where(hit, rank, 0.0), 0, keepdims=True))
        tiles.append((ids // 64).astype(F32))
    place = iota((8, 128), 0)
    stack = jnp.zeros((8, 128), F32)
    for t in range(TOP):
        stack = jnp.where(place == t, tiles[t], jnp.where(place == t + 4, ranks[t], stack))
    spread = (iota((128, 512), 1) // 8 == iota((128, 512), 0)).astype(BF16)
    wide = dot(stack.astype(BF16), spread)
    col, row8 = iota((8, 512), 1), iota((8, 512), 0)
    wide = jnp.where(row8 % 4 == (col // 2) % 4, wide * jnp.where(row8 < 4, 10.0, 2.0), 0.0)
    slot = jnp.sum(wide, 0, keepdims=True) + (iota((1, 512), 1) % 2).astype(F32)
    out_ref[...] = jnp.where(slot.astype(jnp.int32) == iota((SLOTS, 512), 0), 1.0, 0.0).astype(BF16)
    slot_ref[...] = jnp.broadcast_to(slot, (8, 512))


def receive_map_kernel(at_ref, ids_ref, take_ref, give_ref):
    own_tile = at_ref[0] * 8 + at_ref[1]
    blocks = 8
    row, lane = iota((128, 128), 0), iota((128, 128), 1)
    halves = (row // 64) == (lane // 64)
    before = jnp.concatenate([(halves & (row < lane)).astype(BF16), halves.astype(BF16)], 1)
    r, c = iota((256, 256), 0), iota((256, 256), 1)
    lower = ((r // 4 == c // 4) & (c % 4 < r % 4)).astype(BF16)
    sr, sc = iota((160, 160), 0), iota((160, 160), 1)
    pick = (((sr // 10) % 8 == (sc % 32) // 4) & ((sr % 10) // 2 == sc // 32)).astype(BF16)
    side = iota((160, NC), 0) // 80 == iota((160, NC), 1) // 64
    ids = jnp.concatenate([ids_ref[:, b * NC : (b + 1) * NC] for b in range(blocks)], 0)
    hit = ids // 64 == own_tile
    counts = dot(hit.astype(BF16), before)
    rank = counts[:, 0:NC] + dot(lower, counts[:, NC:].astype(BF16))
    value = (ids % 64 + 1).astype(F32)
    held = [jnp.where(hit & (rank == float(k)), value, 0.0) for k in range(CAP)]
    stacked = jnp.concatenate(
        [jnp.concatenate([h[b * 32 : (b + 1) * 32] for h in held], 0) for b in range(blocks)], 1
    )
    found = dot(pick, stacked.astype(BF16))
    found = jnp.concatenate(
        [jnp.where(side, found[:, b * NC : (b + 1) * NC], 0.0) for b in range(blocks)], 0
    )
    local = dot(found.astype(BF16), jnp.ones((NC, NC), BF16)).astype(jnp.int32)
    row, col = iota((SLOTS, NC), 0), iota((SLOTS, NC), 1)
    give = jnp.where((local - 1 == col % 64) & (row % 2 == col // 64), 1.0, 0.0)
    give_ref[...] = give.astype(BF16)
    for b in range(SLOTS // NC):
        take_ref[:, b * NC : (b + 1) * NC] = jnp.transpose(give[b * NC : (b + 1) * NC]).astype(BF16)


def pack_kernel(c_ref, map_ref, out_ref):
    out_ref[...] = dot(map_ref[...], c_ref[...].astype(BF16)).astype(BF16)


def ocean_surface_kernel(in_ref, take_ref, give_ref, m_ref, first_ref, new_ref, back_ref):
    forcing = dot(take_ref[...], in_ref[...])
    wet = 0.25 * m_ref[...].astype(F32)
    news = []
    for f in range(2):
        new = first_ref[f] + wet * forcing[f * NR : (f + 1) * NR]
        new_ref[f] = new
        news.append(new)
    sea = jnp.concatenate(news, 0).astype(BF16)
    back_ref[...] = dot(give_ref[...], sea).astype(BF16)


WB = 8


def return_kernel(in_ref, slot_ref, w_hbm, kept_ref, out_ref, w_s, e_s, p_s, sems):
    def chunk(i):
        return pltpu.make_async_copy(w_hbm.at[pl.ds(i * WB, WB)], w_s.at[i], sems.at[i])

    far = (NR - KEPT) // WB
    for i in range(far):
        chunk(i).start()
    total = jnp.zeros((512, 128), F32)
    slot = jnp.transpose(jnp.broadcast_to(slot_ref[0:1, :], (NC, 512))).astype(jnp.int32)
    for b in range(SLOTS // 128):
        hot = jnp.where(slot == iota((512, 128), 1) + b * 128, 1.0, 0.0).astype(BF16)
        total = total + dot(hot, in_ref[b * 128 : (b + 1) * 128, :])
    term = (iota((512, 128), 0) % 8) // 2
    e_s[...] = jnp.concatenate([jnp.where(term == t, total, 0.0) for t in range(TOP)], 1)

    def apply(x, weight):
        rows = pl.ds(pl.multiple_of(x * 8, 8), 8)
        p_s[rows, :] = dot(e_s[rows, :].astype(BF16), weight.reshape(TOP * NC, NC))

    def near_step(i, carry):
        for k in range(WB):
            apply(NR - KEPT + i * WB + k, kept_ref[i * WB + k])
        return carry

    def far_step(i, carry):
        chunk(i).wait()
        for k in range(WB):
            apply(i * WB + k, w_s[i, k])
        return carry

    lax.fori_loop(0, KEPT // WB, near_step, 0)
    lax.fori_loop(0, far, far_step, 0)
    r, c = iota((128, 512), 0), iota((128, 512), 1)
    gather = jnp.where((c // 8 == r % NR) & (c % 2 == r // NR), 1.0, 0.0).astype(BF16)
    parts = p_s[...]
    high = parts.astype(BF16)
    low = (parts - high.astype(F32)).astype(BF16)
    done = dot(jnp.concatenate([gather, gather], 1), jnp.concatenate([high, low], 0))
    for f in range(2):
        out_ref[f] = done[f * NR : (f + 1) * NR]


def shape(dims, dtype=F32):
    return jax.ShapeDtypeStruct(dims, dtype)


def shifted(x, axis, by):
    count = lax.axis_size(axis)
    return lax.ppermute(x, axis, [(i, (i + by) % count) for i in range(count)])


def per_device(atm_state, ocean_state, land_mask, elem_op, column_mix, kappa, remap_weight, intersection):
    gx, gy = lax.axis_index("gx"), lax.axis_index("gy")
    at = jnp.stack([gx, gy]).astype(jnp.int32)
    smem = pl.BlockSpec(memory_space=pltpu.SMEM)
    full = whole((PAY, NC))

    vmem = pl.BlockSpec(memory_space=pltpu.VMEM)
    hbm = pl.BlockSpec(memory_space=pl.ANY)

    def pinned(x):
        return pltpu.with_memory_space_constraint(x, pltpu.HBM)

    atm_in, ocean_in, mask_in = pinned(atm_state), pinned(ocean_state), pinned(land_mask)
    mix_in, elem_in = pinned(column_mix), pinned(elem_op)
    payload = shape((PAY, NC), BF16)
    rim, send_next, send_prev, element = pl.pallas_call(
        atm_rim_kernel,
        in_specs=[hbm] * 5,
        out_specs=[hbm] + [vmem] * 3,
        out_shape=[pltpu.HBM(atm_state.shape, F32), payload, payload, shape((512, 512), BF16)],
        scratch_shapes=[
            pltpu.VMEM((2, 2, LEV, 8, NC), F32),
            pltpu.VMEM((2, 2, LO, 8, NC), F32),
            pltpu.VMEM((NR, NC), jnp.int32),
            pltpu.VMEM((LEV, LEV), F32),
            pltpu.VMEM((16, 16), F32),
            pltpu.VMEM((2, 2, LEV, 8, NC), F32),
            pltpu.SemaphoreType.DMA((9,)),
        ],
        compiler_params=params(16),
        name="atm_rim",
    )(atm_in, ocean_in, mask_in, mix_in, elem_in)

    from_prev = shifted(send_next, "gx", 1)
    from_next = shifted(send_prev, "gx", -1)

    weights = remap_weight[:, 0]
    weights_in = pinned(weights)
    z, top_level, z_cols, ocean_cols, near_weights = pl.pallas_call(
        inner_kernel,
        in_specs=[hbm, hbm, hbm, vmem, vmem, hbm, hbm],
        out_specs=[hbm] + [vmem] * 4,
        out_shape=[
            pltpu.HBM(atm_state.shape, F32),
            shape((2, NR, NC)),
            shape((2, 144, NC)),
            shape((4, 128, NC)),
            pltpu.VMEM(weights.shape, BF16),
        ],
        scratch_shapes=[
            pltpu.VMEM((INNER, 2, LEV, 8, NC), F32),
            pltpu.VMEM(atm_state.shape, F32),
            pltpu.VMEM(ocean_state.shape, F32),
            pltpu.VMEM((LEV, LEV), F32),
            pltpu.SemaphoreType.DMA((2 * INNER,)),
            pltpu.SemaphoreType.DMA((5,)),
        ],
        input_output_aliases={5: 0},
        compiler_params=params(14),
        cost_estimate=pl.CostEstimate(flops=1000000000, bytes_accessed=14000000, transcendentals=0),
        name="inner",
    )(atm_in, mix_in, ocean_in, element, land_mask, rim, weights_in)

    send_south, send_north = pl.pallas_call(
        cols_kernel,
        out_shape=[shape((PAY, NC), BF16)] * 2,
        compiler_params=params(),
        name="cols",
    )(z_cols, ocean_cols, land_mask, from_prev, from_next)

    from_south = shifted(send_north, "gy", 1)
    from_north = shifted(send_south, "gy", -1)
    gx_count, gy_count = lax.axis_size("gx"), lax.axis_size("gy")
    top = gy_count - 1
    folded = lax.ppermute(
        send_north, ("gx", "gy"), [(i * gy_count + top, (gx_count - 1 - i) * gy_count + top) for i in range(gx_count)]
    )

    ids = jnp.transpose(intersection, (1, 2, 0)).reshape(32, 1024)
    send_map, slot_row, from_north = pl.pallas_call(
        send_map_kernel,
        in_specs=[smem, vmem, hbm],
        out_specs=[vmem, vmem, hbm],
        out_shape=[shape((SLOTS, 512), BF16), shape((8, 512)), payload],
        input_output_aliases={2: 2},
        compiler_params=params(),
        cost_estimate=pl.CostEstimate(flops=4000000, bytes_accessed=4200000, transcendentals=0),
        name="send_map",
    )(at, ids, from_north)

    surface = pl.pallas_call(
        surface_kernel,
        in_specs=[vmem] * 5,
        out_shape=shape((2, NR, NC), BF16),
        compiler_params=params(),
        name="surface",
    )(top_level, from_prev, from_next, from_south, from_north)

    products = lax.dot_general(
        near_weights, surface, (((3,), (2,)), ((0,), (1,))), preferred_element_type=F32
    )
    contrib = jnp.transpose(products, (0, 1, 3, 2)).reshape(2 * ENT, NC)
    outgoing = pl.pallas_call(
        pack_kernel,
        out_shape=shape((SLOTS, NC), BF16),
        compiler_params=params(),
        name="pack",
    )(contrib, send_map)
    incoming = lax.all_to_all(
        outgoing.reshape(TILES, CAP, 2, NC), ("gx", "gy"), split_axis=0, concat_axis=0, tiled=True
    ).reshape(SLOTS, NC)

    halos = (
        send_prev, send_next, send_south, send_north, from_prev, from_next, from_south, from_north, folded
    )
    ocean_args = (at[1:], kappa, ocean_in, land_mask, kappa) + halos
    ocean_specs = [smem, smem, hbm] + [vmem] * 11

    def ocean_scratch(blocks):
        return [
            pltpu.VMEM((blocks, 2, OB, NR, NC), F32),
            pltpu.VMEM((4, 128, NC), F32),
            pltpu.VMEM((4, NR, NC), F32),
            pltpu.SemaphoreType.DMA((2 * blocks,)),
        ]

    ocean_mid, first_level = pl.pallas_call(
        ocean_head_kernel,
        in_specs=ocean_specs,
        out_specs=[hbm, vmem],
        out_shape=[pltpu.HBM(ocean_state.shape, F32), shape((2, NR, NC))],
        scratch_shapes=ocean_scratch(HEAD),
        compiler_params=params(16),
        cost_estimate=pl.CostEstimate(flops=6000000, bytes_accessed=2000000, transcendentals=0),
        name="ocean_head",
    )(*ocean_args)

    take, give = pl.pallas_call(
        receive_map_kernel,
        in_specs=[smem, vmem],
        out_shape=[shape((128, SLOTS), BF16), shape((SLOTS, 128), BF16)],
        compiler_params=params(),
        cost_estimate=pl.CostEstimate(flops=4000000, bytes_accessed=4200000, transcendentals=0),
        name="receive_map",
    )(at, ids)

    new_level, back_out = pl.pallas_call(
        ocean_surface_kernel,
        out_shape=[shape((2, NR, NC)), shape((SLOTS, NC), BF16)],
        compiler_params=params(),
        name="ocean_surface",
    )(incoming, take, give, land_mask, first_level)

    back_in = lax.all_to_all(
        back_out.reshape(TILES, CAP, 2, NC), ("gx", "gy"), split_axis=0, concat_axis=0, tiled=True
    ).reshape(SLOTS, NC)

    ocean_next = pl.pallas_call(
        ocean_rest_kernel,
        in_specs=ocean_specs + [vmem, hbm],
        out_specs=hbm,
        out_shape=pltpu.HBM(ocean_state.shape, F32),
        scratch_shapes=ocean_scratch(LO // OB - HEAD) + [pltpu.SemaphoreType.DMA(())],
        input_output_aliases={15: 0},
        compiler_params=params(16),
        cost_estimate=pl.CostEstimate(flops=24000000, bytes_accessed=6000000, transcendentals=0),
        name="ocean_rest",
    )(*ocean_args, new_level, ocean_mid)

    atm_next, kept_weights = pl.pallas_call(
        finish_kernel,
        in_specs=[hbm] + [vmem] * 4 + [hbm],
        out_specs=[hbm, vmem],
        out_shape=[
            pltpu.HBM(atm_state.shape, F32),
            shape((KEPT, TOP, NC, NC), BF16),
        ],
        scratch_shapes=[
            pltpu.VMEM((LEV // FB, 2, FB, NR, NC), F32),
            pltpu.VMEM((LEV // FB, 2, FB, NR, NC), F32),
            pltpu.VMEM((4, 144, NC), F32),
            pltpu.SemaphoreType.DMA((2 * (LEV // FB),)),
            pltpu.SemaphoreType.DMA(()),
        ],
        compiler_params=params(16),
        cost_estimate=pl.CostEstimate(flops=20000000, bytes_accessed=9400000, transcendentals=0),
        name="finish",
    )(pinned(z), from_prev, from_next, from_south, from_north, weights_in)

    returned = pl.pallas_call(
        return_kernel,
        in_specs=[vmem, vmem, hbm, vmem],
        out_specs=vmem,
        out_shape=shape((2, NR, NC)),
        scratch_shapes=[
            pltpu.VMEM(((NR - KEPT) // WB, WB, TOP, NC, NC), BF16),
            pltpu.VMEM((512, 512), F32),
            pltpu.VMEM((512, NC), F32),
            pltpu.SemaphoreType.DMA((NR // WB,)),
        ],
        compiler_params=params(16),
        name="returned",
    )(back_in, slot_row, weights_in, kept_weights)
    return atm_next, ocean_next, returned


def solution(mesh):
    placed = (
        P(None, None, "gx", "gy"),
        P(None, None, "gx", "gy"),
        P("gx", "gy"),
        P(),
        P(),
        P(),
        P("gx", "gy", None, None, None),
        P(),
    )
    return jax.shard_map(
        per_device,
        mesh=mesh,
        in_specs=placed,
        out_specs=(P(None, None, "gx", "gy"), P(None, None, "gx", "gy"), P(None, "gx", "gy")),
        check_vma=False,
    )
```

```python
import jax
import jax.numpy as jnp
from jax import lax
from jax.experimental import pallas as pl
from jax.experimental.pallas import tpu as pltpu
from jax.sharding import PartitionSpec as P

F32, BF16 = jnp.float32, jnp.bfloat16
LEV, LO, NR, NC = 72, 60, 64, 128
AT, O1, O2, MK, PAY = 0, 144, 272, 400, 416
OL = 2 * LO
TOP, CAP, TILES = 4, 5, 128
ENT = NR * TOP
SLOTS = TILES * CAP * 2
MIB = 1024 * 1024


def iota(shape, dim):
    return lax.broadcasted_iota(jnp.int32, shape, dim)


def dot(a, b):
    return jnp.dot(a, b, preferred_element_type=F32)


def params(mib=6):
    return pltpu.CompilerParams(vmem_limit_bytes=mib * MIB)


def whole(shape):
    return pl.BlockSpec(shape, lambda *_: (0,) * len(shape))


def mask_rows(first, second):
    place = iota((16, NC), 0)
    return jnp.where(place == 0, first, jnp.where(place == 1, second, 0.0)).astype(BF16)


def element_rows(x_s, mix, b):
    fields = [jnp.swapaxes(x_s[f], 0, 1) for f in range(2)]
    ys = []
    for big in range(2):
        for f in range(2):
            x = jnp.concatenate([fields[f][big * 4 + k] for k in range(4)], 1)
            ys.append(x + dot(mix, x.astype(BF16)))
    y = jnp.concatenate(ys, 0)
    z = y + dot(y.astype(BF16), b)
    pieces = [[], []]
    for r in range(8):
        for f in range(2):
            at = ((r // 4) * 2 + f) * LEV
            pieces[f].append(z[at : at + LEV, (r % 4) * NC : (r % 4 + 1) * NC])
    return pieces


def store_rows(z_ref, pieces, at):
    for f in range(2):
        z_ref[f, :, pl.ds(at, 8), :] = jnp.swapaxes(jnp.stack(pieces[f], 0), 0, 1)


def atm_rim_kernel(
    x_hbm, o_hbm, m_hbm, mix_hbm, elem_hbm, z_hbm, sn_ref, sp_ref, b_ref, x_s, o_s, m_s, mix_s, elem_s, z_s, sems
):
    sources = (elem_hbm, mix_hbm, x_hbm.at[:, :, pl.ds(0, 8), :], x_hbm.at[:, :, pl.ds(NR - 8, 8), :], m_hbm) + tuple(
        o_hbm.at[:, :, pl.ds(at, 8), :] for at in (0, NR - 8)
    )
    targets = (elem_s, mix_s, x_s.at[0], x_s.at[1], m_s, o_s.at[0], o_s.at[1])
    copies = [pltpu.make_async_copy(a, b, sems.at[k]) for k, (a, b) in enumerate(zip(sources, targets))]
    outs = [
        pltpu.make_async_copy(z_s.at[k], z_hbm.at[:, :, pl.ds(k * (NR - 8), 8), :], sems.at[7 + k]) for k in range(2)
    ]
    for copy in copies:
        copy.start()
    copies[0].wait()
    row = iota((512, 16), 0)
    spread_in = (iota((512, 16), 1) == (row // 128) * 4 + row % 4).astype(BF16)
    col = iota((16, 512), 1)
    spread_out = (iota((16, 512), 0) == (col // 128) * 4 + col % 4).astype(BF16)
    elem = (0.5 * elem_s[...]).astype(BF16)
    half = lax.dot_general(spread_in, elem, (((1,), (1,)), ((), ())), preferred_element_type=F32)
    spread = dot(half.astype(BF16), spread_out)
    same = (iota((512, 512), 0) % 128) // 4 == (iota((512, 512), 1) % 128) // 4
    b = jnp.where(same, spread, 0.0).astype(BF16)
    b_ref[...] = b
    copies[1].wait()
    mix = (0.5 * mix_s[...]).astype(BF16)
    for k, ref in ((0, sp_ref), (1, sn_ref)):
        copies[2 + k].wait()
        pieces = element_rows(x_s.at[k], mix, b)
        store_rows(z_s.at[k], pieces, 0)
        outs[k].start()
        ref[AT:O1, :] = jnp.concatenate([pieces[f][7 * k] for f in range(2)], 0).astype(BF16)
    for k in (4, 5, 6):
        copies[k].wait()
    m = m_s[...].astype(F32)
    for ref, k, first in ((sp_ref, 0, 0), (sn_ref, 1, 6)):
        rows = jnp.swapaxes(o_s[k].reshape(OL, 8, NC), 0, 1)
        at = k * (NR - 8) + first
        for j, base in ((0, O1), (1, O2)):
            u = rows[first + j] * m[at + j : at + j + 1]
            ref[base : base + 128, :] = jnp.concatenate([u, jnp.zeros((8, NC), F32)], 0).astype(BF16)
        ref[MK:PAY, :] = mask_rows(m[at : at + 1], m[at + 1 : at + 2])
    for copy in outs:
        copy.wait()


INNER = NR // 8 - 2
EARLY = 32


def pick_columns(columns):
    k, at = iota((8 * len(columns), 8 * NC), 0), iota((8 * len(columns), 8 * NC), 1)
    wanted = jnp.zeros_like(k)
    for j, c in enumerate(columns):
        wanted = jnp.where(k // 8 == j, c, wanted)
    return ((at // NC == k % 8) & (at % NC == wanted)).astype(BF16)


def take_columns(pick, tiles):
    side = jnp.concatenate([t.astype(BF16) for t in tiles], 1)
    got = lax.dot_general(pick, side, (((1,), (1,)), ((), ())), preferred_element_type=F32)
    return jnp.concatenate([got, jnp.zeros_like(got)], 1)


def inner_kernel(
    x_hbm, mix_hbm, o_hbm, b_ref, rim_hbm, w_hbm, z_hbm, top_ref, zc_ref, oc_ref, w_ref,
    x_s, z_s, o_s, mix_s, sems, rest,
):
    mix_copy = pltpu.make_async_copy(mix_hbm, mix_s, rest.at[0])
    ocean_copy = pltpu.make_async_copy(o_hbm, o_s, rest.at[1])
    rims = [
        pltpu.make_async_copy(
            rim_hbm.at[:, :, pl.ds(at, 8), :], z_s.at[:, :, pl.ds(at, 8), :], rest.at[2 + k]
        )
        for k, at in enumerate((0, NR - 8))
    ]

    def chunk(i):
        return pltpu.make_async_copy(x_hbm.at[:, :, pl.ds(i * 8 + 8, 8), :], x_s.at[i], sems.at[i])

    def leave(i):
        rows = pl.ds(pl.multiple_of(i * 8 + 8, 8), 8)
        return pltpu.make_async_copy(z_s.at[:, :, rows, :], z_hbm.at[:, :, rows, :], sems.at[INNER + i])

    mix_copy.start()
    for i in range(INNER):
        chunk(i).start()
    for copy in rims:
        copy.start()
    ocean_copy.start()
    early = pl.ds(0, EARLY)
    weight_copy = pltpu.make_async_copy(w_hbm.at[early], w_ref.at[early], rest.at[4])
    weight_copy.start()
    mix_copy.wait()
    mix = (0.5 * mix_s[...]).astype(BF16)

    def step(i, carry):
        chunk(i).wait()
        store_rows(z_s, element_rows(x_s.at[i], mix, b_ref[...]), pl.multiple_of(i * 8 + 8, 8))
        leave(i).start()
        return carry

    lax.fori_loop(0, INNER, step, 0)
    for copy in rims:
        copy.wait()
    pick = pick_columns((0, NC - 1))

    def atm(i, carry):
        for f in range(2):
            got = take_columns(pick, [z_s[f, i * 8 + l] for l in range(8)])
            at = pl.multiple_of(f * LEV + i * 8, 8)
            for k in range(2):
                zc_ref[k, pl.ds(at, 8), :] = got[k * 8 : k * 8 + 8]
        return carry

    lax.fori_loop(0, LEV // 8, atm, 0, unroll=3)
    for f in range(2):
        top_ref[f] = z_s[f, LEV - 1]
    ocean_copy.wait()
    pick = pick_columns((0, 1, NC - 2, NC - 1))

    def ocean(i, carry):
        tiles = [i * 8 + l for l in range(8)]
        got = take_columns(pick, [o_s[t // LO, t % LO] for t in tiles])
        for k in range(4):
            oc_ref[k, pl.ds(pl.multiple_of(i * 8, 8), 8), :] = got[k * 8 : k * 8 + 8]
        return carry

    lax.fori_loop(0, OL // 8, ocean, 0, unroll=5)
    oc_ref[:, OL:, :] = jnp.zeros((4, 8, NC), F32)
    for i in range(INNER):
        leave(i).wait()
    weight_copy.wait()


def cols_kernel(zc_ref, oc_ref, m_ref, rp_ref, rn_ref, ss_ref, sn_ref):
    lane = iota((144, NC), 1)
    place = lane % 4
    rp_at, rn_at = rp_ref[AT:O1, :].astype(F32), rn_ref[AT:O1, :].astype(F32)
    before, after = rp_ref[O2:MK, :].astype(F32), rn_ref[O1:O2, :].astype(F32)
    olane = iota((128, NC), 1)
    row = iota((64, NC), 0)
    m_before, m_after = rp_ref[MK:PAY, :].astype(F32)[1:2], rn_ref[MK:PAY, :].astype(F32)[0:1]
    tail = jnp.where(row == 0, m_before, jnp.where(row == 1, m_after, 0.0))
    m_t = jnp.transpose(jnp.concatenate([m_ref[...].astype(F32), tail], 0))
    for ref, c_at, ocs in ((ss_ref, 0, (0, 1)), (sn_ref, 127, (126, 127))):
        z = zc_ref[0 if c_at == 0 else 1]
        nxt = jnp.where(lane == 63, rn_at[:, c_at : c_at + 1], pltpu.roll(z, 127, 1))
        prv = jnp.where(lane == 0, rp_at[:, c_at : c_at + 1], pltpu.roll(z, 1, 1))
        z = jnp.where(place == 3, (z + nxt) * 0.5, jnp.where(place == 0, (z + prv) * 0.5, z))
        ref[AT:O1, :] = z.astype(BF16)
        for k, c in enumerate(ocs):
            source = c if c < 2 else c - 124
            u = jnp.where(
                olane < 64,
                oc_ref[source] * m_t[c : c + 1],
                jnp.where(olane == 64, before[:, c : c + 1], jnp.where(olane == 65, after[:, c : c + 1], 0.0)),
            )
            base = (O1, O2)[k]
            ref[base : base + 128, :] = u.astype(BF16)
        ref[MK:PAY, :] = mask_rows(m_t[ocs[0] : ocs[0] + 1], m_t[ocs[1] : ocs[1] + 1])


def averaged(z, nxt, prv, place):
    return jnp.where(place == 3, (z + nxt) * 0.5, jnp.where(place == 0, (z + prv) * 0.5, z))


def stiffness(z, h_prev, h_next, c_south, c_north):
    row, lane = iota((NR, NC), 0), iota((NR, NC), 1)
    nxt = jnp.where(row == NR - 1, h_next, pltpu.roll(z, NR - 1, 0))
    prv = jnp.where(row == 0, h_prev, pltpu.roll(z, 1, 0))
    z = averaged(z, nxt, prv, row % 4)
    nxt = jnp.where(lane == NC - 1, c_north, pltpu.roll(z, NC - 1, 1))
    prv = jnp.where(lane == 0, c_south, pltpu.roll(z, 1, 1))
    return averaged(z, nxt, prv, lane % 4)


def surface_kernel(z_ref, rp_ref, rn_ref, cs_ref, cn_ref, s_ref):
    rp, rn = rp_ref[AT:O1, :].astype(F32), rn_ref[AT:O1, :].astype(F32)
    cs, cn = cs_ref[AT:O1, :].astype(F32), cn_ref[AT:O1, :].astype(F32)
    for f in range(2):
        top = f * LEV + LEV - 8
        south = jnp.transpose(cs[top : top + 8])[:NR, 7:8]
        north = jnp.transpose(cn[top : top + 8])[:NR, 7:8]
        last = top + 7
        s = stiffness(z_ref[f], rp[last : last + 1], rn[last : last + 1], south, north)
        s_ref[f] = s.astype(BF16)


def edge_spread(tiles, scale):
    k, c = iota((2 * tiles, tiles * NC), 0), iota((2 * tiles, tiles * NC), 1)
    mine = k % tiles == c // NC
    end = c % NC == jnp.where(k < tiles, 0, NC - 1)
    return jnp.where(mine & end, scale, 0.0).astype(BF16)


def add_ends(x, first, last):
    row = iota((8, NC), 0)
    return jnp.concatenate(
        [
            x[0:8] + jnp.where(row == 0, first, 0.0),
            x[8 : NR - 8],
            x[NR - 8 :] + jnp.where(row == 7, last, 0.0),
        ],
        0,
    )


def column_halo(columns, spread):
    return lax.dot_general(columns, spread, (((0,), (0,)), ((), ())), preferred_element_type=F32)[:NR]


FB = 8
KEPT = 16


def finish_kernel(
    z_hbm, rp_ref, rn_ref, cs_ref, cn_ref, new_ref, w_hbm, mid_hbm, o_hbm, ocean_hbm, w_ref,
    z_s, o_s, h_ref, sems, level_sem, weight_sem,
):
    del mid_hbm
    weight_copy = pltpu.make_async_copy(w_hbm.at[pl.ds(NR - KEPT, KEPT)], w_ref, weight_sem)
    level = pltpu.make_async_copy(new_ref, ocean_hbm.at[:, 0], level_sem)
    level.start()

    def enter(i):
        return pltpu.make_async_copy(z_hbm.at[:, pl.ds(i * FB, FB)], z_s.at[i], sems.at[LEV // FB + i])

    for i in range(LEV // FB):
        enter(i).start()
    weight_copy.start()
    for k, ref in enumerate((rp_ref, rn_ref, cs_ref, cn_ref)):
        h_ref[k] = ref[AT:O1, :].astype(F32)
    spread = edge_spread(2 * FB, 0.5)
    row, lane = iota((NR, NC), 0), iota((NR, NC), 1)

    def weights(place, at, end):
        low = jnp.where((place == 0) & (at != 0), 0.5, 0.0)
        high = jnp.where((place == 3) & (at != end), 0.5, 0.0)
        return jnp.where((place == 0) | (place == 3), 0.5, 1.0), low, high

    own_r, low_r, high_r = weights(row % 4, row, NR - 1)
    own_c, low_c, high_c = weights(lane % 4, lane, NC - 1)

    def chunk(i):
        return pltpu.make_async_copy(o_s.at[i], o_hbm.at[:, pl.ds(i * FB, FB)], sems.at[i])

    def step(i, carry):
        enter(i).wait()

        def halo(k, f):
            return h_ref[k, pl.ds(pl.multiple_of(f * LEV + i * FB, 8), FB), :]

        columns = jnp.concatenate([halo(2, 0), halo(2, 1), halo(3, 0), halo(3, 1)], 0).astype(BF16)
        edges = column_halo(columns, spread)
        for f in range(2):
            first, last = 0.5 * halo(0, f), 0.5 * halo(1, f)
            for l in range(FB):
                t = z_s[i, f, l]
                t = own_r * t + high_r * pltpu.roll(t, NR - 1, 0) + low_r * pltpu.roll(t, 1, 0)
                t = add_ends(t, first[l : l + 1], last[l : l + 1])
                t = own_c * t + high_c * pltpu.roll(t, NC - 1, 1) + low_c * pltpu.roll(t, 1, 1)
                tile = f * FB + l
                o_s[i, f, l] = t + edges[:, tile * NC : (tile + 1) * NC]
        chunk(i).start()
        return carry

    lax.fori_loop(0, LEV // FB, step, 0)
    level.wait()
    weight_copy.wait()
    for i in range(LEV // FB):
        chunk(i).wait()


OB = 12


def ocean_kernel(
    at_ref, k_ref, o_hbm, m_ref, kc_ref, sp_ref, sn_ref, ss_ref, st_ref, rp_ref, rn_ref, cs_ref, cn_ref, fo_ref,
    out_hbm, first_ref, out_s, row_ref, col_ref, sems,
):
    def enter(i):
        return pltpu.make_async_copy(o_hbm.at[:, pl.ds(i * OB, OB)], out_s.at[i], sems.at[LO // OB + i])

    for i in range(LO // OB):
        enter(i).start()
    is_top, is_low = at_ref[0] == 7, at_ref[0] == 0
    lane = iota((128, NC), 1)

    def part(ref, base):
        return ref[base : base + 128, :].astype(F32)

    def masks(ref):
        m = ref[MK:PAY, :].astype(F32)
        return m[0:1], m[1:2]

    fr, fc = iota((NC, NC), 0), iota((NC, NC), 1)
    flip = (((fr < 64) & (fc == 63 - fr)) | ((fr == 64) & (fc == 65)) | ((fr == 65) & (fc == 64))).astype(BF16)
    turned = dot(fo_ref[...], flip)
    n0 = jnp.where(is_top, turned[O2:MK], part(cn_ref, O1))
    n1 = jnp.where(is_top, turned[O1:O2], part(cn_ref, O2))
    mc0, mc1 = masks(cn_ref)
    mn0 = jnp.where(is_top, turned[MK + 1 : MK + 2], mc0)
    mn1 = jnp.where(is_top, turned[MK : MK + 1], mc1)
    keep = jnp.where(is_low, 0.0, 1.0)
    s2, s1 = part(cs_ref, O1) * keep, part(cs_ref, O2) * keep
    ms2, ms1 = masks(cs_ref)
    ms2, ms1 = ms2 * keep, ms1 * keep
    um2, um1 = part(rp_ref, O1), part(rp_ref, O2)
    mm2, mm1 = masks(rp_ref)
    u64, u65 = part(rn_ref, O1), part(rn_ref, O2)
    m64, m65 = masks(rn_ref)
    own0, own63 = part(sp_ref, O1), part(sn_ref, O2)
    mo0, mo63 = masks(sp_ref)[0], masks(sn_ref)[1]
    west0, east127 = part(ss_ref, O1), part(st_ref, O2)
    mw0, me127 = masks(ss_ref)[0], masks(st_ref)[1]
    at, l60 = iota((128, LO), 0), iota((128, LO), 1)
    kap = sum(
        jnp.sum(jnp.where(at - f * LO == l60, kc_ref[f : f + 1, :], 0.0), 1, keepdims=True) for f in range(2)
    )

    def along(u, low, high, end):
        where = lane[: u.shape[0]]
        return jnp.where(where == end, high, pltpu.roll(u, 127, 1)) + jnp.where(
            where == 0, low, pltpu.roll(u, 1, 1)
        )

    def advance(u, wet, inner, outer, m_inner, m_outer, low, high, m_low, m_high, end):
        total = inner + outer + along(u, low, high, end)
        m8 = jnp.broadcast_to(wet, (8, NC))
        count = m_inner + m_outer + along(m8, m_low, m_high, end)[0:1]
        return u + kap * (wet * total - count * u)

    def corner(x, at):
        return x[:, at : at + 1]

    row_ref[0] = um1
    row_ref[1] = u64
    row_ref[2] = advance(
        um1, mm1, own0, um2, mo0, mm2, corner(s1, 64), corner(n0, 64), corner(ms1, 64), corner(mn0, 64), 127
    )
    row_ref[3] = advance(
        u64, m64, own63, u65, mo63, m65, corner(s1, 65), corner(n0, 65), corner(ms1, 65), corner(mn0, 65), 127
    )
    west = advance(
        s1, ms1, west0, s2, mw0, ms2, corner(s1, 64), corner(s1, 65), corner(ms1, 64), corner(ms1, 65), 63
    )
    east = advance(
        n0, mn0, east127, n1, me127, mn1, corner(n0, 64), corner(n0, 65), corner(mn0, 64), corner(mn0, 65), 63
    )
    here = iota((NR, NC), 1)
    for sub, (low, high) in enumerate(((s1, n0), (west, east))):
        low, high = jnp.transpose(low)[:NR], jnp.transpose(high)[:NR]
        for f in range(2):
            col_ref[2 * sub + f] = jnp.where(
                here < 64, pltpu.roll(low, (NC - LO * f) % NC, 1), pltpu.roll(high, (NC + 64 - LO * f) % NC, 1)
            )
    a, b = iota((NC, NC), 0), iota((NC, NC), 1)
    ends = ((a == 0) & (b == 0)) | ((a == 64) & (b == NC - 1))
    ns = jnp.concatenate([(jnp.abs(a - b) == 1).astype(BF16), ends.astype(BF16)], 0)
    wet = m_ref[...].astype(F32)
    r, c = iota((NR, NC), 0), iota((NR, NC), 1)
    m_north = jnp.transpose(jnp.broadcast_to(mn0, (8, NC)))[:NR, 0:1]
    m_south = jnp.transpose(jnp.broadcast_to(ms1, (8, NC)))[:NR, 0:1]
    count = jnp.where(r == NR - 1, m64, pltpu.roll(wet, NR - 1, 0)) + jnp.where(
        r == 0, mm1, pltpu.roll(wet, 1, 0)
    )
    count = count + jnp.where(c == NC - 1, m_north, pltpu.roll(wet, NC - 1, 1))
    count = count + jnp.where(c == 0, m_south, pltpu.roll(wet, 1, 1))

    places = [(f, l) for f in range(2) for l in range(OB)]

    def chunk(i):
        return pltpu.make_async_copy(out_s.at[i], out_hbm.at[:, pl.ds(i * OB, OB)], sems.at[i])

    def step(i, carry):
        enter(i).wait()
        ts = [out_s[i, f, l] for f, l in places]
        for sub in range(2):
            us = [wet * t for t in ts]
            halos = [pltpu.roll(col_ref[2 * sub + f], (NC - i * OB - l) % NC, 1) for f, l in places]
            side = jnp.concatenate([jnp.concatenate(us, 0), jnp.concatenate(halos, 0)], 1)
            cols = dot(side.astype(BF16), ns)
            for j, (f, l) in enumerate(places):
                level = i * OB + l
                here = pl.ds(f * LO + level, 1)
                u = us[j]
                total = pltpu.roll(u, NR - 1, 0) + pltpu.roll(u, 1, 0) + cols[j * NR : (j + 1) * NR]
                total = add_ends(
                    total, row_ref[2 * sub, here, :] - u[NR - 1 :], row_ref[2 * sub + 1, here, :] - u[0:1]
                )
                ts[j] = ts[j] + (k_ref[f, level] * wet) * (total - count * ts[j])
        for j, (f, l) in enumerate(places):
            out_s[i, f, l] = ts[j]
        chunk(i).start()
        return carry

    lax.fori_loop(0, LO // OB, step, 0)
    for f in range(2):
        first_ref[f] = out_s[0, f, 0]
    for i in range(LO // OB):
        chunk(i).wait()


def send_map_kernel(
    at_ref, ids_ref, pass_hbm, w_hbm, near_ref, out_ref, slot_ref, through_hbm, w_ref, weight_sem
):
    del pass_hbm, through_hbm, near_ref
    rows = pl.ds(EARLY, NR - EARLY)
    weight_copy = pltpu.make_async_copy(w_hbm.at[rows], w_ref.at[rows], weight_sem)
    weight_copy.start()
    gx, gy = at_ref[0], at_ref[1]
    block = ids_ref[:, pl.ds(pl.multiple_of((gx // 2) * 128, 128), 128)]
    block = pltpu.roll(block, (gx % 2) * 64, 1)
    rows = iota((32, 128), 0)
    tile_row, lane = iota((128, 128), 0), iota((128, 128), 1)
    before = (tile_row < lane).astype(BF16)
    ones = jnp.ones((128, 128), BF16)
    earlier = jnp.zeros((128, 128), F32)
    tiles, ranks = [], []
    for t in range(TOP):
        ids = jnp.sum(jnp.where(rows == gy * 4 + t, block, 0), 0, keepdims=True)
        hit = (ids // 64 == tile_row) & (lane < 64)
        hot = hit.astype(BF16)
        rank = dot(hot, before) + earlier
        earlier = earlier + dot(hot, ones)
        ranks.append(jnp.sum(jnp.where(hit, rank, 0.0), 0, keepdims=True))
        tiles.append((ids // 64).astype(F32))
    place = iota((8, 128), 0)
    stack = jnp.zeros((8, 128), F32)
    for t in range(TOP):
        stack = jnp.where(place == t, tiles[t], jnp.where(place == t + 4, ranks[t], stack))
    spread = (iota((128, 512), 1) // 8 == iota((128, 512), 0)).astype(BF16)
    wide = dot(stack.astype(BF16), spread)
    col, row8 = iota((8, 512), 1), iota((8, 512), 0)
    wide = jnp.where(row8 % 4 == (col // 2) % 4, wide * jnp.where(row8 < 4, 10.0, 2.0), 0.0)
    slot = jnp.sum(wide, 0, keepdims=True) + (iota((1, 512), 1) % 2).astype(F32)
    out_ref[...] = jnp.where(slot.astype(jnp.int32) == iota((SLOTS, 512), 0), 1.0, 0.0).astype(BF16)
    slot_ref[...] = jnp.broadcast_to(slot, (8, 512))
    weight_copy.wait()


def receive_map_kernel(at_ref, ids_ref, take_ref, give_ref):
    own_tile = at_ref[0] * 8 + at_ref[1]
    blocks = 8
    row, lane = iota((128, 128), 0), iota((128, 128), 1)
    halves = (row // 64) == (lane // 64)
    before = jnp.concatenate([(halves & (row < lane)).astype(BF16), halves.astype(BF16)], 1)
    r, c = iota((256, 256), 0), iota((256, 256), 1)
    lower = ((r // 4 == c // 4) & (c % 4 < r % 4)).astype(BF16)
    sr, sc = iota((160, 160), 0), iota((160, 160), 1)
    pick = (((sr // 10) % 8 == (sc % 32) // 4) & ((sr % 10) // 2 == sc // 32)).astype(BF16)
    side = iota((160, NC), 0) // 80 == iota((160, NC), 1) // 64
    ids = jnp.concatenate([ids_ref[:, b * NC : (b + 1) * NC] for b in range(blocks)], 0)
    hit = ids // 64 == own_tile
    counts = dot(hit.astype(BF16), before)
    rank = counts[:, 0:NC] + dot(lower, counts[:, NC:].astype(BF16))
    value = (ids % 64 + 1).astype(F32)
    held = [jnp.where(hit & (rank == float(k)), value, 0.0) for k in range(CAP)]
    stacked = jnp.concatenate(
        [jnp.concatenate([h[b * 32 : (b + 1) * 32] for h in held], 0) for b in range(blocks)], 1
    )
    found = dot(pick, stacked.astype(BF16))
    found = jnp.concatenate(
        [jnp.where(side, found[:, b * NC : (b + 1) * NC], 0.0) for b in range(blocks)], 0
    )
    local = dot(found.astype(BF16), jnp.ones((NC, NC), BF16)).astype(jnp.int32)
    row, col = iota((SLOTS, NC), 0), iota((SLOTS, NC), 1)
    give = jnp.where((local - 1 == col % 64) & (row % 2 == col // 64), 1.0, 0.0)
    give_ref[...] = give.astype(BF16)
    for b in range(SLOTS // NC):
        take_ref[:, b * NC : (b + 1) * NC] = jnp.transpose(give[b * NC : (b + 1) * NC]).astype(BF16)


def pack_kernel(c_ref, map_ref, fold_ref, out_ref):
    del fold_ref
    out_ref[...] = dot(map_ref[...], c_ref[...].astype(BF16)).astype(BF16)


def ocean_surface_kernel(in_ref, take_ref, give_ref, m_ref, first_ref, new_ref, back_ref):
    forcing = dot(take_ref[...], in_ref[...])
    wet = 0.25 * m_ref[...].astype(F32)
    news = []
    for f in range(2):
        new = first_ref[f] + wet * forcing[f * NR : (f + 1) * NR]
        new_ref[f] = new
        news.append(new)
    sea = jnp.concatenate(news, 0).astype(BF16)
    back_ref[...] = dot(give_ref[...], sea).astype(BF16)


WB = 8


def return_kernel(in_ref, slot_ref, w_hbm, kept_ref, out_ref, w_s, e_s, p_s, sems):
    def chunk(i):
        return pltpu.make_async_copy(w_hbm.at[pl.ds(i * WB, WB)], w_s.at[i], sems.at[i])

    far = (NR - KEPT) // WB
    for i in range(far):
        chunk(i).start()
    total = jnp.zeros((512, 128), F32)
    slot = jnp.transpose(jnp.broadcast_to(slot_ref[0:1, :], (NC, 512))).astype(jnp.int32)
    for b in range(SLOTS // 128):
        hot = jnp.where(slot == iota((512, 128), 1) + b * 128, 1.0, 0.0).astype(BF16)
        total = total + dot(hot, in_ref[b * 128 : (b + 1) * 128, :])
    term = (iota((512, 128), 0) % 8) // 2
    e_s[...] = jnp.concatenate([jnp.where(term == t, total, 0.0) for t in range(TOP)], 1)

    def apply(x, weight):
        rows = pl.ds(pl.multiple_of(x * 8, 8), 8)
        p_s[rows, :] = dot(e_s[rows, :].astype(BF16), weight.reshape(TOP * NC, NC))

    def near_step(i, carry):
        for k in range(WB):
            apply(NR - KEPT + i * WB + k, kept_ref[i * WB + k])
        return carry

    def far_step(i, carry):
        chunk(i).wait()
        for k in range(WB):
            apply(i * WB + k, w_s[i, k])
        return carry

    lax.fori_loop(0, KEPT // WB, near_step, 0)
    lax.fori_loop(0, far, far_step, 0)
    r, c = iota((128, 512), 0), iota((128, 512), 1)
    gather = jnp.where((c // 8 == r % NR) & (c % 2 == r // NR), 1.0, 0.0).astype(BF16)
    parts = p_s[...]
    high = parts.astype(BF16)
    low = (parts - high.astype(F32)).astype(BF16)
    done = dot(jnp.concatenate([gather, gather], 1), jnp.concatenate([high, low], 0))
    for f in range(2):
        out_ref[f] = done[f * NR : (f + 1) * NR]


def shape(dims, dtype=F32):
    return jax.ShapeDtypeStruct(dims, dtype)


def shifted(x, axis, by):
    count = lax.axis_size(axis)
    return lax.ppermute(x, axis, [(i, (i + by) % count) for i in range(count)])


def per_device(atm_state, ocean_state, land_mask, elem_op, column_mix, kappa, remap_weight, intersection):
    gx, gy = lax.axis_index("gx"), lax.axis_index("gy")
    at = jnp.stack([gx, gy]).astype(jnp.int32)
    smem = pl.BlockSpec(memory_space=pltpu.SMEM)
    full = whole((PAY, NC))

    vmem = pl.BlockSpec(memory_space=pltpu.VMEM)
    hbm = pl.BlockSpec(memory_space=pl.ANY)

    def pinned(x):
        return pltpu.with_memory_space_constraint(x, pltpu.HBM)

    atm_in, ocean_in, mask_in = pinned(atm_state), pinned(ocean_state), pinned(land_mask)
    mix_in, elem_in = pinned(column_mix), pinned(elem_op)
    payload = shape((PAY, NC), BF16)
    rim, send_next, send_prev, element = pl.pallas_call(
        atm_rim_kernel,
        in_specs=[hbm] * 5,
        out_specs=[hbm] + [vmem] * 3,
        out_shape=[pltpu.HBM(atm_state.shape, F32), payload, payload, shape((512, 512), BF16)],
        scratch_shapes=[
            pltpu.VMEM((2, 2, LEV, 8, NC), F32),
            pltpu.VMEM((2, 2, LO, 8, NC), F32),
            pltpu.VMEM((NR, NC), jnp.int32),
            pltpu.VMEM((LEV, LEV), F32),
            pltpu.VMEM((16, 16), F32),
            pltpu.VMEM((2, 2, LEV, 8, NC), F32),
            pltpu.SemaphoreType.DMA((9,)),
        ],
        compiler_params=params(16),
        name="atm_rim",
    )(atm_in, ocean_in, mask_in, mix_in, elem_in)

    from_prev = shifted(send_next, "gx", 1)
    from_next = shifted(send_prev, "gx", -1)

    weights = remap_weight[:, 0]
    weights_in = pinned(weights)
    z, top_level, z_cols, ocean_cols, near_weights = pl.pallas_call(
        inner_kernel,
        in_specs=[hbm, hbm, hbm, vmem, hbm, hbm],
        out_specs=[hbm] + [vmem] * 4,
        out_shape=[
            pltpu.HBM(atm_state.shape, F32),
            shape((2, NR, NC)),
            shape((2, 144, NC)),
            shape((4, 128, NC)),
            pltpu.VMEM(weights.shape, BF16),
        ],
        scratch_shapes=[
            pltpu.VMEM((INNER, 2, LEV, 8, NC), F32),
            pltpu.VMEM(atm_state.shape, F32),
            pltpu.VMEM(ocean_state.shape, F32),
            pltpu.VMEM((LEV, LEV), F32),
            pltpu.SemaphoreType.DMA((2 * INNER,)),
            pltpu.SemaphoreType.DMA((5,)),
        ],
        input_output_aliases={4: 0},
        compiler_params=params(14),
        cost_estimate=pl.CostEstimate(flops=1000000000, bytes_accessed=14000000, transcendentals=0),
        name="inner",
    )(atm_in, mix_in, ocean_in, element, rim, weights_in)

    send_south, send_north = pl.pallas_call(
        cols_kernel,
        out_shape=[shape((PAY, NC), BF16)] * 2,
        compiler_params=params(),
        name="cols",
    )(z_cols, ocean_cols, land_mask, from_prev, from_next)

    from_south = shifted(send_north, "gy", 1)
    from_north = shifted(send_south, "gy", -1)
    gx_count, gy_count = lax.axis_size("gx"), lax.axis_size("gy")
    top = gy_count - 1
    folded = lax.ppermute(
        send_north, ("gx", "gy"), [(i * gy_count + top, (gx_count - 1 - i) * gy_count + top) for i in range(gx_count)]
    )

    ids = jnp.transpose(intersection, (1, 2, 0)).reshape(32, 1024)
    send_map, slot_row, from_north, near_weights = pl.pallas_call(
        send_map_kernel,
        in_specs=[smem, vmem, hbm, hbm, vmem],
        out_specs=[vmem, vmem, hbm, vmem],
        out_shape=[
            shape((SLOTS, 512), BF16), shape((8, 512)), payload, pltpu.VMEM(weights.shape, BF16)
        ],
        scratch_shapes=[pltpu.SemaphoreType.DMA(())],
        input_output_aliases={2: 2, 4: 3},
        compiler_params=params(),
        cost_estimate=pl.CostEstimate(flops=4000000, bytes_accessed=4200000, transcendentals=0),
        name="send_map",
    )(at, ids, from_north, weights_in, near_weights)

    surface = pl.pallas_call(
        surface_kernel,
        in_specs=[vmem] * 5,
        out_shape=shape((2, NR, NC), BF16),
        compiler_params=params(),
        name="surface",
    )(top_level, from_prev, from_next, from_south, from_north)

    products = lax.dot_general(
        near_weights, surface, (((3,), (2,)), ((0,), (1,))), preferred_element_type=F32
    )
    contrib = jnp.transpose(products, (0, 1, 3, 2)).reshape(2 * ENT, NC)
    outgoing = pl.pallas_call(
        pack_kernel,
        in_specs=[vmem, vmem, hbm],
        out_shape=shape((SLOTS, NC), BF16),
        compiler_params=params(),
        name="pack",
    )(contrib, send_map, folded)
    incoming = lax.all_to_all(
        outgoing.reshape(TILES, CAP, 2, NC), ("gx", "gy"), split_axis=0, concat_axis=0, tiled=True
    ).reshape(SLOTS, NC)

    ocean_mid, first_level = pl.pallas_call(
        ocean_kernel,
        in_specs=[smem, smem, hbm] + [vmem] * 11,
        out_specs=[hbm, vmem],
        out_shape=[pltpu.HBM(ocean_state.shape, F32), shape((2, NR, NC))],
        scratch_shapes=[
            pltpu.VMEM((LO // OB, 2, OB, NR, NC), F32),
            pltpu.VMEM((4, 128, NC), F32),
            pltpu.VMEM((4, NR, NC), F32),
            pltpu.SemaphoreType.DMA((2 * (LO // OB),)),
        ],
        compiler_params=params(16),
        cost_estimate=pl.CostEstimate(flops=30000000, bytes_accessed=8000000, transcendentals=0),
        name="ocean",
    )(
        at[1:], kappa, ocean_in, land_mask, kappa, send_prev, send_next, send_south, send_north,
        from_prev, from_next, from_south, from_north, folded,
    )

    take, give = pl.pallas_call(
        receive_map_kernel,
        in_specs=[smem, vmem],
        out_shape=[shape((128, SLOTS), BF16), shape((SLOTS, 128), BF16)],
        compiler_params=params(),
        cost_estimate=pl.CostEstimate(flops=4000000, bytes_accessed=4200000, transcendentals=0),
        name="receive_map",
    )(at, ids)

    new_level, back_out = pl.pallas_call(
        ocean_surface_kernel,
        out_shape=[shape((2, NR, NC)), shape((SLOTS, NC), BF16)],
        compiler_params=params(),
        name="ocean_surface",
    )(incoming, take, give, land_mask, first_level)

    back_in = lax.all_to_all(
        back_out.reshape(TILES, CAP, 2, NC), ("gx", "gy"), split_axis=0, concat_axis=0, tiled=True
    ).reshape(SLOTS, NC)

    atm_next, ocean_next, kept_weights = pl.pallas_call(
        finish_kernel,
        in_specs=[hbm] + [vmem] * 5 + [hbm] * 2,
        out_specs=[hbm, hbm, vmem],
        out_shape=[
            pltpu.HBM(atm_state.shape, F32),
            pltpu.HBM(ocean_state.shape, F32),
            shape((KEPT, TOP, NC, NC), BF16),
        ],
        input_output_aliases={7: 1},
        scratch_shapes=[
            pltpu.VMEM((LEV // FB, 2, FB, NR, NC), F32),
            pltpu.VMEM((LEV // FB, 2, FB, NR, NC), F32),
            pltpu.VMEM((4, 144, NC), F32),
            pltpu.SemaphoreType.DMA((2 * (LEV // FB),)),
            pltpu.SemaphoreType.DMA(()),
            pltpu.SemaphoreType.DMA(()),
        ],
        compiler_params=params(16),
        cost_estimate=pl.CostEstimate(flops=20000000, bytes_accessed=9400000, transcendentals=0),
        name="finish",
    )(pinned(z), from_prev, from_next, from_south, from_north, new_level, weights_in, ocean_mid)

    returned = pl.pallas_call(
        return_kernel,
        in_specs=[vmem, vmem, hbm, vmem],
        out_specs=vmem,
        out_shape=shape((2, NR, NC)),
        scratch_shapes=[
            pltpu.VMEM(((NR - KEPT) // WB, WB, TOP, NC, NC), BF16),
            pltpu.VMEM((512, 512), F32),
            pltpu.VMEM((512, NC), F32),
            pltpu.SemaphoreType.DMA((NR // WB,)),
        ],
        compiler_params=params(16),
        name="returned",
    )(back_in, slot_row, weights_in, kept_weights)
    return atm_next, ocean_next, returned


def solution(mesh):
    placed = (
        P(None, None, "gx", "gy"),
        P(None, None, "gx", "gy"),
        P("gx", "gy"),
        P(),
        P(),
        P(),
        P("gx", "gy", None, None, None),
        P(),
    )
    return jax.shard_map(
        per_device,
        mesh=mesh,
        in_specs=placed,
        out_specs=(P(None, None, "gx", "gy"), P(None, None, "gx", "gy"), P(None, "gx", "gy")),
        check_vma=False,
    )
```

```python
import jax
import jax.numpy as jnp
from jax import lax
from jax.experimental import pallas as pl
from jax.experimental.pallas import tpu as pltpu
from jax.sharding import PartitionSpec as P

F32, BF16 = jnp.float32, jnp.bfloat16
LEV, LO, NR, NC = 72, 60, 64, 128
AT, O1, O2, MK, PAY = 0, 144, 272, 400, 416
OL = 2 * LO
TOP, CAP, TILES = 4, 5, 128
ENT = NR * TOP
SLOTS = TILES * CAP * 2
MIB = 1024 * 1024


def iota(shape, dim):
    return lax.broadcasted_iota(jnp.int32, shape, dim)


def dot(a, b):
    return jnp.dot(a, b, preferred_element_type=F32)


def params(mib=6):
    return pltpu.CompilerParams(vmem_limit_bytes=mib * MIB)


def whole(shape):
    return pl.BlockSpec(shape, lambda *_: (0,) * len(shape))


def mask_rows(first, second):
    place = iota((16, NC), 0)
    return jnp.where(place == 0, first, jnp.where(place == 1, second, 0.0)).astype(BF16)


def element_rows(x_s, mix, b):
    fields = [jnp.swapaxes(x_s[f], 0, 1) for f in range(2)]
    ys = []
    for big in range(2):
        for f in range(2):
            x = jnp.concatenate([fields[f][big * 4 + k] for k in range(4)], 1)
            ys.append(x + dot(mix, x.astype(BF16)))
    y = jnp.concatenate(ys, 0)
    z = y + dot(y.astype(BF16), b)
    pieces = [[], []]
    for r in range(8):
        for f in range(2):
            at = ((r // 4) * 2 + f) * LEV
            pieces[f].append(z[at : at + LEV, (r % 4) * NC : (r % 4 + 1) * NC])
    return pieces


def store_rows(z_ref, pieces, at):
    for f in range(2):
        z_ref[f, :, pl.ds(at, 8), :] = jnp.swapaxes(jnp.stack(pieces[f], 0), 0, 1)


def atm_rim_kernel(
    x_hbm, o_hbm, m_hbm, mix_hbm, elem_hbm, z_hbm, sn_ref, sp_ref, b_ref, x_s, o_s, m_s, mix_s, elem_s, z_s, sems
):
    sources = (elem_hbm, mix_hbm, x_hbm.at[:, :, pl.ds(0, 8), :], x_hbm.at[:, :, pl.ds(NR - 8, 8), :], m_hbm) + tuple(
        o_hbm.at[:, :, pl.ds(at, 8), :] for at in (0, NR - 8)
    )
    targets = (elem_s, mix_s, x_s.at[0], x_s.at[1], m_s, o_s.at[0], o_s.at[1])
    copies = [pltpu.make_async_copy(a, b, sems.at[k]) for k, (a, b) in enumerate(zip(sources, targets))]
    outs = [
        pltpu.make_async_copy(z_s.at[k], z_hbm.at[:, :, pl.ds(k * (NR - 8), 8), :], sems.at[7 + k]) for k in range(2)
    ]
    for copy in copies:
        copy.start()
    copies[0].wait()
    row = iota((512, 16), 0)
    spread_in = (iota((512, 16), 1) == (row // 128) * 4 + row % 4).astype(BF16)
    col = iota((16, 512), 1)
    spread_out = (iota((16, 512), 0) == (col // 128) * 4 + col % 4).astype(BF16)
    elem = (0.5 * elem_s[...]).astype(BF16)
    half = lax.dot_general(spread_in, elem, (((1,), (1,)), ((), ())), preferred_element_type=F32)
    spread = dot(half.astype(BF16), spread_out)
    same = (iota((512, 512), 0) % 128) // 4 == (iota((512, 512), 1) % 128) // 4
    b = jnp.where(same, spread, 0.0).astype(BF16)
    b_ref[...] = b
    copies[1].wait()
    mix = (0.5 * mix_s[...]).astype(BF16)
    for k, ref in ((0, sp_ref), (1, sn_ref)):
        copies[2 + k].wait()
        pieces = element_rows(x_s.at[k], mix, b)
        store_rows(z_s.at[k], pieces, 0)
        outs[k].start()
        ref[AT:O1, :] = jnp.concatenate([pieces[f][7 * k] for f in range(2)], 0).astype(BF16)
    for k in (4, 5, 6):
        copies[k].wait()
    m = m_s[...].astype(F32)
    for ref, k, first in ((sp_ref, 0, 0), (sn_ref, 1, 6)):
        rows = jnp.swapaxes(o_s[k].reshape(OL, 8, NC), 0, 1)
        at = k * (NR - 8) + first
        for j, base in ((0, O1), (1, O2)):
            u = rows[first + j] * m[at + j : at + j + 1]
            ref[base : base + 128, :] = jnp.concatenate([u, jnp.zeros((8, NC), F32)], 0).astype(BF16)
        ref[MK:PAY, :] = mask_rows(m[at : at + 1], m[at + 1 : at + 2])
    for copy in outs:
        copy.wait()


INNER = NR // 8 - 2


def pick_columns(columns):
    k, at = iota((8 * len(columns), 8 * NC), 0), iota((8 * len(columns), 8 * NC), 1)
    wanted = jnp.zeros_like(k)
    for j, c in enumerate(columns):
        wanted = jnp.where(k // 8 == j, c, wanted)
    return ((at // NC == k % 8) & (at % NC == wanted)).astype(BF16)


def take_columns(pick, tiles):
    side = jnp.concatenate([t.astype(BF16) for t in tiles], 1)
    got = lax.dot_general(pick, side, (((1,), (1,)), ((), ())), preferred_element_type=F32)
    return jnp.concatenate([got, jnp.zeros_like(got)], 1)


def inner_kernel(
    x_hbm, mix_hbm, o_hbm, b_ref, m_ref, rim_hbm, w_hbm, z_hbm, top_ref, zc_ref, oc_ref, w_ref,
    x_s, z_s, o_s, mix_s, sems, rest,
):
    mix_copy = pltpu.make_async_copy(mix_hbm, mix_s, rest.at[0])
    ocean_copy = pltpu.make_async_copy(o_hbm, o_s, rest.at[1])
    rims = [
        pltpu.make_async_copy(
            rim_hbm.at[:, :, pl.ds(at, 8), :], z_s.at[:, :, pl.ds(at, 8), :], rest.at[2 + k]
        )
        for k, at in enumerate((0, NR - 8))
    ]

    def chunk(i):
        return pltpu.make_async_copy(x_hbm.at[:, :, pl.ds(i * 8 + 8, 8), :], x_s.at[i], sems.at[i])

    def leave(i):
        rows = pl.ds(pl.multiple_of(i * 8 + 8, 8), 8)
        return pltpu.make_async_copy(z_s.at[:, :, rows, :], z_hbm.at[:, :, rows, :], sems.at[INNER + i])

    mix_copy.start()
    for i in range(INNER):
        chunk(i).start()
    for copy in rims:
        copy.start()
    ocean_copy.start()
    weight_copy = pltpu.make_async_copy(w_hbm, w_ref, rest.at[4])
    weight_copy.start()
    mix_copy.wait()
    mix = (0.5 * mix_s[...]).astype(BF16)

    def step(i, carry):
        chunk(i).wait()
        store_rows(z_s, element_rows(x_s.at[i], mix, b_ref[...]), pl.multiple_of(i * 8 + 8, 8))
        leave(i).start()
        return carry

    lax.fori_loop(0, INNER, step, 0)
    for copy in rims:
        copy.wait()
    pick = pick_columns((0, NC - 1))

    def atm(i, carry):
        for f in range(2):
            got = take_columns(pick, [z_s[f, i * 8 + l] for l in range(8)])
            at = pl.multiple_of(f * LEV + i * 8, 8)
            for k in range(2):
                zc_ref[k, pl.ds(at, 8), :] = got[k * 8 : k * 8 + 8]
        return carry

    lax.fori_loop(0, LEV // 8, atm, 0, unroll=3)
    for f in range(2):
        top_ref[f] = z_s[f, LEV - 1]
    ocean_copy.wait()
    wet = m_ref[...].astype(F32)
    pick = pick_columns((0, 1, NC - 2, NC - 1))

    def ocean(i, carry):
        tiles = [i * 8 + l for l in range(8)]
        got = take_columns(pick, [wet * o_s[t // LO, t % LO] for t in tiles])
        for k in range(4):
            oc_ref[k, pl.ds(pl.multiple_of(i * 8, 8), 8), :] = got[k * 8 : k * 8 + 8]
        return carry

    lax.fori_loop(0, OL // 8, ocean, 0, unroll=3)
    oc_ref[:, OL:, :] = jnp.zeros((4, 8, NC), F32)
    for i in range(INNER):
        leave(i).wait()
    weight_copy.wait()


def cols_kernel(zc_ref, oc_ref, m_ref, rp_ref, rn_ref, ss_ref, sn_ref):
    lane = iota((144, NC), 1)
    place = lane % 4
    rp_at, rn_at = rp_ref[AT:O1, :].astype(F32), rn_ref[AT:O1, :].astype(F32)
    before, after = rp_ref[O2:MK, :].astype(F32), rn_ref[O1:O2, :].astype(F32)
    olane = iota((128, NC), 1)
    row = iota((64, NC), 0)
    m_before, m_after = rp_ref[MK:PAY, :].astype(F32)[1:2], rn_ref[MK:PAY, :].astype(F32)[0:1]
    tail = jnp.where(row == 0, m_before, jnp.where(row == 1, m_after, 0.0))
    m_t = jnp.transpose(jnp.concatenate([m_ref[...].astype(F32), tail], 0))
    for ref, c_at, ocs in ((ss_ref, 0, (0, 1)), (sn_ref, 127, (126, 127))):
        z = zc_ref[0 if c_at == 0 else 1]
        nxt = jnp.where(lane == 63, rn_at[:, c_at : c_at + 1], pltpu.roll(z, 127, 1))
        prv = jnp.where(lane == 0, rp_at[:, c_at : c_at + 1], pltpu.roll(z, 1, 1))
        z = jnp.where(place == 3, (z + nxt) * 0.5, jnp.where(place == 0, (z + prv) * 0.5, z))
        ref[AT:O1, :] = z.astype(BF16)
        for k, c in enumerate(ocs):
            source = c if c < 2 else c - 124
            u = jnp.where(
                olane < 64,
                oc_ref[source],
                jnp.where(olane == 64, before[:, c : c + 1], jnp.where(olane == 65, after[:, c : c + 1], 0.0)),
            )
            base = (O1, O2)[k]
            ref[base : base + 128, :] = u.astype(BF16)
        ref[MK:PAY, :] = mask_rows(m_t[ocs[0] : ocs[0] + 1], m_t[ocs[1] : ocs[1] + 1])


def averaged(z, nxt, prv, place):
    return jnp.where(place == 3, (z + nxt) * 0.5, jnp.where(place == 0, (z + prv) * 0.5, z))


def stiffness(z, h_prev, h_next, c_south, c_north):
    row, lane = iota((NR, NC), 0), iota((NR, NC), 1)
    nxt = jnp.where(row == NR - 1, h_next, pltpu.roll(z, NR - 1, 0))
    prv = jnp.where(row == 0, h_prev, pltpu.roll(z, 1, 0))
    z = averaged(z, nxt, prv, row % 4)
    nxt = jnp.where(lane == NC - 1, c_north, pltpu.roll(z, NC - 1, 1))
    prv = jnp.where(lane == 0, c_south, pltpu.roll(z, 1, 1))
    return averaged(z, nxt, prv, lane % 4)


def surface_kernel(z_ref, rp_ref, rn_ref, cs_ref, cn_ref, s_ref):
    rp, rn = rp_ref[AT:O1, :].astype(F32), rn_ref[AT:O1, :].astype(F32)
    cs, cn = cs_ref[AT:O1, :].astype(F32), cn_ref[AT:O1, :].astype(F32)
    for f in range(2):
        top = f * LEV + LEV - 8
        south = jnp.transpose(cs[top : top + 8])[:NR, 7:8]
        north = jnp.transpose(cn[top : top + 8])[:NR, 7:8]
        last = top + 7
        s = stiffness(z_ref[f], rp[last : last + 1], rn[last : last + 1], south, north)
        s_ref[f] = s.astype(BF16)


def edge_spread(tiles, scale):
    k, c = iota((2 * tiles, tiles * NC), 0), iota((2 * tiles, tiles * NC), 1)
    mine = k % tiles == c // NC
    end = c % NC == jnp.where(k < tiles, 0, NC - 1)
    return jnp.where(mine & end, scale, 0.0).astype(BF16)


def add_ends(x, first, last):
    row = iota((8, NC), 0)
    return jnp.concatenate(
        [
            x[0:8] + jnp.where(row == 0, first, 0.0),
            x[8 : NR - 8],
            x[NR - 8 :] + jnp.where(row == 7, last, 0.0),
        ],
        0,
    )


def column_halo(columns, spread):
    return lax.dot_general(columns, spread, (((0,), (0,)), ((), ())), preferred_element_type=F32)[:NR]


FB = 8
KEPT = 16


def finish_kernel(
    z_hbm, rp_ref, rn_ref, cs_ref, cn_ref, new_ref, w_hbm, mid_hbm, o_hbm, ocean_hbm, w_ref,
    z_s, o_s, h_ref, sems, level_sem, weight_sem,
):
    del mid_hbm
    weight_copy = pltpu.make_async_copy(w_hbm.at[pl.ds(NR - KEPT, KEPT)], w_ref, weight_sem)
    level = pltpu.make_async_copy(new_ref, ocean_hbm.at[:, 0], level_sem)
    level.start()

    def enter(i):
        return pltpu.make_async_copy(z_hbm.at[:, pl.ds(i * FB, FB)], z_s.at[i], sems.at[LEV // FB + i])

    for i in range(LEV // FB):
        enter(i).start()
    weight_copy.start()
    for k, ref in enumerate((rp_ref, rn_ref, cs_ref, cn_ref)):
        h_ref[k] = ref[AT:O1, :].astype(F32)
    spread = edge_spread(2 * FB, 0.5)
    row, lane = iota((NR, NC), 0), iota((NR, NC), 1)

    def weights(place, at, end):
        low = jnp.where((place == 0) & (at != 0), 0.5, 0.0)
        high = jnp.where((place == 3) & (at != end), 0.5, 0.0)
        return jnp.where((place == 0) | (place == 3), 0.5, 1.0), low, high

    own_r, low_r, high_r = weights(row % 4, row, NR - 1)
    own_c, low_c, high_c = weights(lane % 4, lane, NC - 1)

    def chunk(i):
        return pltpu.make_async_copy(o_s.at[i], o_hbm.at[:, pl.ds(i * FB, FB)], sems.at[i])

    def step(i, carry):
        enter(i).wait()

        def halo(k, f):
            return h_ref[k, pl.ds(pl.multiple_of(f * LEV + i * FB, 8), FB), :]

        columns = jnp.concatenate([halo(2, 0), halo(2, 1), halo(3, 0), halo(3, 1)], 0).astype(BF16)
        edges = column_halo(columns, spread)
        for f in range(2):
            first, last = 0.5 * halo(0, f), 0.5 * halo(1, f)
            for l in range(FB):
                t = z_s[i, f, l]
                t = own_r * t + high_r * pltpu.roll(t, NR - 1, 0) + low_r * pltpu.roll(t, 1, 0)
                t = add_ends(t, first[l : l + 1], last[l : l + 1])
                t = own_c * t + high_c * pltpu.roll(t, NC - 1, 1) + low_c * pltpu.roll(t, 1, 1)
                tile = f * FB + l
                o_s[i, f, l] = t + edges[:, tile * NC : (tile + 1) * NC]
        chunk(i).start()
        return carry

    lax.fori_loop(0, LEV // FB, step, 0)
    level.wait()
    weight_copy.wait()
    for i in range(LEV // FB):
        chunk(i).wait()


OB = 12


def ocean_kernel(
    at_ref, k_ref, o_hbm, m_ref, kc_ref, sp_ref, sn_ref, ss_ref, st_ref, rp_ref, rn_ref, cs_ref, cn_ref, fo_ref,
    out_hbm, first_ref, out_s, row_ref, col_ref, sems,
):
    def enter(i):
        return pltpu.make_async_copy(o_hbm.at[:, pl.ds(i * OB, OB)], out_s.at[i], sems.at[LO // OB + i])

    for i in range(LO // OB):
        enter(i).start()
    is_top, is_low = at_ref[0] == 7, at_ref[0] == 0
    lane = iota((128, NC), 1)

    def part(ref, base):
        return ref[base : base + 128, :].astype(F32)

    def masks(ref):
        m = ref[MK:PAY, :].astype(F32)
        return m[0:1], m[1:2]

    fr, fc = iota((NC, NC), 0), iota((NC, NC), 1)
    flip = (((fr < 64) & (fc == 63 - fr)) | ((fr == 64) & (fc == 65)) | ((fr == 65) & (fc == 64))).astype(BF16)
    turned = dot(fo_ref[...], flip)
    n0 = jnp.where(is_top, turned[O2:MK], part(cn_ref, O1))
    n1 = jnp.where(is_top, turned[O1:O2], part(cn_ref, O2))
    mc0, mc1 = masks(cn_ref)
    mn0 = jnp.where(is_top, turned[MK + 1 : MK + 2], mc0)
    mn1 = jnp.where(is_top, turned[MK : MK + 1], mc1)
    keep = jnp.where(is_low, 0.0, 1.0)
    s2, s1 = part(cs_ref, O1) * keep, part(cs_ref, O2) * keep
    ms2, ms1 = masks(cs_ref)
    ms2, ms1 = ms2 * keep, ms1 * keep
    um2, um1 = part(rp_ref, O1), part(rp_ref, O2)
    mm2, mm1 = masks(rp_ref)
    u64, u65 = part(rn_ref, O1), part(rn_ref, O2)
    m64, m65 = masks(rn_ref)
    own0, own63 = part(sp_ref, O1), part(sn_ref, O2)
    mo0, mo63 = masks(sp_ref)[0], masks(sn_ref)[1]
    west0, east127 = part(ss_ref, O1), part(st_ref, O2)
    mw0, me127 = masks(ss_ref)[0], masks(st_ref)[1]
    at, l60 = iota((128, LO), 0), iota((128, LO), 1)
    kap = sum(
        jnp.sum(jnp.where(at - f * LO == l60, kc_ref[f : f + 1, :], 0.0), 1, keepdims=True) for f in range(2)
    )

    def along(u, low, high, end):
        where = lane[: u.shape[0]]
        return jnp.where(where == end, high, pltpu.roll(u, 127, 1)) + jnp.where(
            where == 0, low, pltpu.roll(u, 1, 1)
        )

    def advance(u, wet, inner, outer, m_inner, m_outer, low, high, m_low, m_high, end):
        total = inner + outer + along(u, low, high, end)
        m8 = jnp.broadcast_to(wet, (8, NC))
        count = m_inner + m_outer + along(m8, m_low, m_high, end)[0:1]
        return u + kap * (wet * total - count * u)

    def corner(x, at):
        return x[:, at : at + 1]

    row_ref[0] = um1
    row_ref[1] = u64
    row_ref[2] = advance(
        um1, mm1, own0, um2, mo0, mm2, corner(s1, 64), corner(n0, 64), corner(ms1, 64), corner(mn0, 64), 127
    )
    row_ref[3] = advance(
        u64, m64, own63, u65, mo63, m65, corner(s1, 65), corner(n0, 65), corner(ms1, 65), corner(mn0, 65), 127
    )
    west = advance(
        s1, ms1, west0, s2, mw0, ms2, corner(s1, 64), corner(s1, 65), corner(ms1, 64), corner(ms1, 65), 63
    )
    east = advance(
        n0, mn0, east127, n1, me127, mn1, corner(n0, 64), corner(n0, 65), corner(mn0, 64), corner(mn0, 65), 63
    )
    here = iota((NR, NC), 1)
    for sub, (low, high) in enumerate(((s1, n0), (west, east))):
        low, high = jnp.transpose(low)[:NR], jnp.transpose(high)[:NR]
        for f in range(2):
            col_ref[2 * sub + f] = jnp.where(
                here < 64, pltpu.roll(low, (NC - LO * f) % NC, 1), pltpu.roll(high, (NC + 64 - LO * f) % NC, 1)
            )
    a, b = iota((NC, NC), 0), iota((NC, NC), 1)
    ends = ((a == 0) & (b == 0)) | ((a == 64) & (b == NC - 1))
    ns = jnp.concatenate([(jnp.abs(a - b) == 1).astype(BF16), ends.astype(BF16)], 0)
    wet = m_ref[...].astype(F32)
    r, c = iota((NR, NC), 0), iota((NR, NC), 1)
    m_north = jnp.transpose(jnp.broadcast_to(mn0, (8, NC)))[:NR, 0:1]
    m_south = jnp.transpose(jnp.broadcast_to(ms1, (8, NC)))[:NR, 0:1]
    count = jnp.where(r == NR - 1, m64, pltpu.roll(wet, NR - 1, 0)) + jnp.where(
        r == 0, mm1, pltpu.roll(wet, 1, 0)
    )
    count = count + jnp.where(c == NC - 1, m_north, pltpu.roll(wet, NC - 1, 1))
    count = count + jnp.where(c == 0, m_south, pltpu.roll(wet, 1, 1))

    places = [(f, l) for f in range(2) for l in range(OB)]

    def chunk(i):
        return pltpu.make_async_copy(out_s.at[i], out_hbm.at[:, pl.ds(i * OB, OB)], sems.at[i])

    def step(i, carry):
        enter(i).wait()
        ts = [out_s[i, f, l] for f, l in places]
        for sub in range(2):
            us = [wet * t for t in ts]
            halos = [pltpu.roll(col_ref[2 * sub + f], (NC - i * OB - l) % NC, 1) for f, l in places]
            side = jnp.concatenate([jnp.concatenate(us, 0), jnp.concatenate(halos, 0)], 1)
            cols = dot(side.astype(BF16), ns)
            for j, (f, l) in enumerate(places):
                level = i * OB + l
                here = pl.ds(f * LO + level, 1)
                u = us[j]
                total = pltpu.roll(u, NR - 1, 0) + pltpu.roll(u, 1, 0) + cols[j * NR : (j + 1) * NR]
                total = add_ends(
                    total, row_ref[2 * sub, here, :] - u[NR - 1 :], row_ref[2 * sub + 1, here, :] - u[0:1]
                )
                ts[j] = ts[j] + (k_ref[f, level] * wet) * (total - count * ts[j])
        for j, (f, l) in enumerate(places):
            out_s[i, f, l] = ts[j]
        chunk(i).start()
        return carry

    lax.fori_loop(0, LO // OB, step, 0)
    for f in range(2):
        first_ref[f] = out_s[0, f, 0]
    for i in range(LO // OB):
        chunk(i).wait()


def send_map_kernel(at_ref, ids_ref, pass_hbm, out_ref, scol_ref, through_hbm):
    del pass_hbm, through_hbm
    gx, gy = at_ref[0], at_ref[1]
    block = ids_ref[:, pl.ds(pl.multiple_of((gx // 2) * 128, 128), 128)]
    block = pltpu.roll(block, (gx % 2) * 64, 1)
    rows = iota((32, 128), 0)
    tile_row, lane = iota((128, 128), 0), iota((128, 128), 1)
    sums = jnp.concatenate([(tile_row < lane).astype(BF16), jnp.ones((128, 128), BF16)], 1)
    ids = [jnp.sum(jnp.where(rows == gy * 4 + t, block, 0), 0, keepdims=True) for t in range(TOP)]
    hits = [(i // 64 == tile_row) & (lane < 64) for i in ids]
    counts = dot(jnp.concatenate([h.astype(BF16) for h in hits], 0), sums)
    earlier = jnp.zeros((128, 128), F32)
    tiles, ranks = [], []
    for t in range(TOP):
        count = counts[t * 128 : (t + 1) * 128]
        ranks.append(jnp.sum(jnp.where(hits[t], count[:, 0:128] + earlier, 0.0), 0, keepdims=True))
        earlier = earlier + count[:, 128:]
        tiles.append((ids[t] // 64).astype(F32))
    place = iota((8, 128), 0)
    stack = jnp.zeros((8, 128), F32)
    for t in range(TOP):
        stack = jnp.where(place == t, tiles[t], jnp.where(place == t + 4, ranks[t], stack))
    spread = (iota((128, 512), 1) // 8 == iota((128, 512), 0)).astype(BF16)
    wide = dot(stack.astype(BF16), spread)
    col, row8 = iota((8, 512), 1), iota((8, 512), 0)
    wide = jnp.where(row8 % 4 == (col // 2) % 4, wide * jnp.where(row8 < 4, 10.0, 2.0), 0.0)
    slot = jnp.sum(wide, 0, keepdims=True) + (iota((1, 512), 1) % 2).astype(F32)
    out_ref[...] = jnp.where(slot.astype(jnp.int32) == iota((SLOTS, 512), 0), 1.0, 0.0).astype(BF16)
    scol_ref[...] = jnp.transpose(jnp.broadcast_to(slot, (128, 512)))


def receive_map_kernel(at_ref, ids_ref, take_ref, give_ref):
    own_tile = at_ref[0] * 8 + at_ref[1]
    blocks = 8
    row, lane = iota((128, 128), 0), iota((128, 128), 1)
    halves = (row // 64) == (lane // 64)
    before = jnp.concatenate([(halves & (row < lane)).astype(BF16), halves.astype(BF16)], 1)
    r, c = iota((256, 256), 0), iota((256, 256), 1)
    lower = ((r // 4 == c // 4) & (c % 4 < r % 4)).astype(BF16)
    sr, sc = iota((160, 160), 0), iota((160, 160), 1)
    pick = (((sr // 10) % 8 == (sc % 32) // 4) & ((sr % 10) // 2 == sc // 32)).astype(BF16)
    side = iota((160, NC), 0) // 80 == iota((160, NC), 1) // 64
    ids = jnp.concatenate([ids_ref[:, b * NC : (b + 1) * NC] for b in range(blocks)], 0)
    hit = ids // 64 == own_tile
    counts = dot(hit.astype(BF16), before)
    rank = counts[:, 0:NC] + dot(lower, counts[:, NC:].astype(BF16))
    value = (ids % 64 + 1).astype(F32)
    held = [jnp.where(hit & (rank == float(k)), value, 0.0) for k in range(CAP)]
    stacked = jnp.concatenate(
        [jnp.concatenate([h[b * 32 : (b + 1) * 32] for h in held], 0) for b in range(blocks)], 1
    )
    found = dot(pick, stacked.astype(BF16))
    found = jnp.concatenate(
        [jnp.where(side, found[:, b * NC : (b + 1) * NC], 0.0) for b in range(blocks)], 0
    )
    local = dot(found.astype(BF16), jnp.ones((NC, NC), BF16)).astype(jnp.int32)
    row, col = iota((SLOTS, NC), 0), iota((SLOTS, NC), 1)
    give = jnp.where((local - 1 == col % 64) & (row % 2 == col // 64), 1.0, 0.0)
    give_ref[...] = give.astype(BF16)
    for b in range(SLOTS // NC):
        take_ref[:, b * NC : (b + 1) * NC] = jnp.transpose(give[b * NC : (b + 1) * NC]).astype(BF16)


PARTS = 4


def send_parts(make, out_hbm, stage, sems):
    size = SLOTS // PARTS
    copies = []
    for k in range(PARTS):
        rows = pl.ds(k * size, size)
        stage[rows, :] = make(rows).astype(BF16)
        copies.append(pltpu.make_async_copy(stage.at[rows], out_hbm.at[rows], sems.at[k]))
        copies[k].start()
    for copy in copies:
        copy.wait()


def pack_kernel(c_ref, map_ref, fold_ref, out_hbm, stage, sems):
    del fold_ref
    terms = c_ref[...].astype(BF16)
    send_parts(lambda rows: dot(map_ref[rows, :], terms), out_hbm, stage, sems)


def ocean_surface_kernel(in_ref, take_ref, give_ref, m_ref, first_ref, new_ref, back_hbm, stage, sems):
    forcing = dot(take_ref[...], in_ref[...])
    wet = 0.25 * m_ref[...].astype(F32)
    news = []
    for f in range(2):
        new = first_ref[f] + wet * forcing[f * NR : (f + 1) * NR]
        new_ref[f] = new
        news.append(new)
    sea = jnp.concatenate(news, 0).astype(BF16)
    send_parts(lambda rows: dot(give_ref[rows, :], sea), back_hbm, stage, sems)


WB = 8


def return_kernel(in_ref, scol_ref, w_hbm, kept_ref, out_ref, w_s, e_s, p_s, sems):
    def chunk(i):
        return pltpu.make_async_copy(w_hbm.at[pl.ds(i * WB, WB)], w_s.at[i], sems.at[i])

    far = (NR - KEPT) // WB
    for i in range(far):
        chunk(i).start()
    total = jnp.zeros((512, 128), F32)
    slot = scol_ref[...].astype(jnp.int32)
    for b in range(SLOTS // 128):
        hot = jnp.where(slot == iota((512, 128), 1) + b * 128, 1.0, 0.0).astype(BF16)
        total = total + dot(hot, in_ref[b * 128 : (b + 1) * 128, :])
    term = (iota((512, 128), 0) % 8) // 2
    e_s[...] = jnp.concatenate([jnp.where(term == t, total, 0.0) for t in range(TOP)], 1)

    def apply(x, weight):
        rows = pl.ds(pl.multiple_of(x * 8, 8), 8)
        p_s[rows, :] = dot(e_s[rows, :].astype(BF16), weight.reshape(TOP * NC, NC))

    def near_step(i, carry):
        for k in range(WB):
            apply(NR - KEPT + i * WB + k, kept_ref[i * WB + k])
        return carry

    def far_step(i, carry):
        chunk(i).wait()
        for k in range(WB):
            apply(i * WB + k, w_s[i, k])
        return carry

    lax.fori_loop(0, KEPT // WB, near_step, 0)
    lax.fori_loop(0, far, far_step, 0)
    r, c = iota((128, 512), 0), iota((128, 512), 1)
    gather = jnp.where((c // 8 == r % NR) & (c % 2 == r // NR), 1.0, 0.0).astype(BF16)
    parts = p_s[...]
    high = parts.astype(BF16)
    low = (parts - high.astype(F32)).astype(BF16)
    done = dot(jnp.concatenate([gather, gather], 1), jnp.concatenate([high, low], 0))
    for f in range(2):
        out_ref[f] = done[f * NR : (f + 1) * NR]


def shape(dims, dtype=F32):
    return jax.ShapeDtypeStruct(dims, dtype)


def shifted(x, axis, by):
    count = lax.axis_size(axis)
    return lax.ppermute(x, axis, [(i, (i + by) % count) for i in range(count)])


def per_device(atm_state, ocean_state, land_mask, elem_op, column_mix, kappa, remap_weight, intersection):
    gx, gy = lax.axis_index("gx"), lax.axis_index("gy")
    at = jnp.stack([gx, gy]).astype(jnp.int32)
    smem = pl.BlockSpec(memory_space=pltpu.SMEM)
    full = whole((PAY, NC))

    vmem = pl.BlockSpec(memory_space=pltpu.VMEM)
    hbm = pl.BlockSpec(memory_space=pl.ANY)

    def pinned(x):
        return pltpu.with_memory_space_constraint(x, pltpu.HBM)

    atm_in, ocean_in, mask_in = pinned(atm_state), pinned(ocean_state), pinned(land_mask)
    mix_in, elem_in = pinned(column_mix), pinned(elem_op)
    payload = shape((PAY, NC), BF16)
    rim, send_next, send_prev, element = pl.pallas_call(
        atm_rim_kernel,
        in_specs=[hbm] * 5,
        out_specs=[hbm] + [vmem] * 3,
        out_shape=[pltpu.HBM(atm_state.shape, F32), payload, payload, shape((512, 512), BF16)],
        scratch_shapes=[
            pltpu.VMEM((2, 2, LEV, 8, NC), F32),
            pltpu.VMEM((2, 2, LO, 8, NC), F32),
            pltpu.VMEM((NR, NC), jnp.int32),
            pltpu.VMEM((LEV, LEV), F32),
            pltpu.VMEM((16, 16), F32),
            pltpu.VMEM((2, 2, LEV, 8, NC), F32),
            pltpu.SemaphoreType.DMA((9,)),
        ],
        compiler_params=params(16),
        name="atm_rim",
    )(atm_in, ocean_in, mask_in, mix_in, elem_in)

    from_prev = shifted(send_next, "gx", 1)
    from_next = shifted(send_prev, "gx", -1)

    weights = remap_weight[:, 0]
    weights_in = pinned(weights)
    z, top_level, z_cols, ocean_cols, near_weights = pl.pallas_call(
        inner_kernel,
        in_specs=[hbm, hbm, hbm, vmem, vmem, hbm, hbm],
        out_specs=[hbm] + [vmem] * 4,
        out_shape=[
            pltpu.HBM(atm_state.shape, F32),
            shape((2, NR, NC)),
            shape((2, 144, NC)),
            shape((4, 128, NC)),
            pltpu.VMEM(weights.shape, BF16),
        ],
        scratch_shapes=[
            pltpu.VMEM((INNER, 2, LEV, 8, NC), F32),
            pltpu.VMEM(atm_state.shape, F32),
            pltpu.VMEM(ocean_state.shape, F32),
            pltpu.VMEM((LEV, LEV), F32),
            pltpu.SemaphoreType.DMA((2 * INNER,)),
            pltpu.SemaphoreType.DMA((5,)),
        ],
        input_output_aliases={5: 0},
        compiler_params=params(14),
        cost_estimate=pl.CostEstimate(flops=1000000000, bytes_accessed=14000000, transcendentals=0),
        name="inner",
    )(atm_in, mix_in, ocean_in, element, land_mask, rim, weights_in)

    send_south, send_north = pl.pallas_call(
        cols_kernel,
        out_shape=[shape((PAY, NC), BF16)] * 2,
        compiler_params=params(),
        name="cols",
    )(z_cols, ocean_cols, land_mask, from_prev, from_next)

    from_south = shifted(send_north, "gy", 1)
    from_north = shifted(send_south, "gy", -1)
    gx_count, gy_count = lax.axis_size("gx"), lax.axis_size("gy")
    top = gy_count - 1
    folded = lax.ppermute(
        send_north, ("gx", "gy"), [(i * gy_count + top, (gx_count - 1 - i) * gy_count + top) for i in range(gx_count)]
    )

    ids = jnp.transpose(intersection, (1, 2, 0)).reshape(32, 1024)
    send_map, slot_col, from_north = pl.pallas_call(
        send_map_kernel,
        in_specs=[smem, vmem, hbm],
        out_specs=[vmem, vmem, hbm],
        out_shape=[shape((SLOTS, 512), BF16), shape((512, 128)), payload],
        input_output_aliases={2: 2},
        compiler_params=params(),
        cost_estimate=pl.CostEstimate(flops=4000000, bytes_accessed=4200000, transcendentals=0),
        name="send_map",
    )(at, ids, from_north)

    surface = pl.pallas_call(
        surface_kernel,
        in_specs=[vmem] * 5,
        out_shape=shape((2, NR, NC), BF16),
        compiler_params=params(),
        name="surface",
    )(top_level, from_prev, from_next, from_south, from_north)

    products = lax.dot_general(
        near_weights, surface, (((3,), (2,)), ((0,), (1,))), preferred_element_type=F32
    )
    contrib = jnp.transpose(products, (0, 1, 3, 2)).reshape(2 * ENT, NC)
    outgoing = pl.pallas_call(
        pack_kernel,
        in_specs=[vmem, vmem, hbm],
        out_specs=hbm,
        out_shape=pltpu.HBM((SLOTS, NC), BF16),
        scratch_shapes=[pltpu.VMEM((SLOTS, NC), BF16), pltpu.SemaphoreType.DMA((PARTS,))],
        compiler_params=params(),
        name="pack",
    )(contrib, send_map, folded)
    incoming = lax.all_to_all(
        outgoing.reshape(TILES, CAP, 2, NC), ("gx", "gy"), split_axis=0, concat_axis=0, tiled=True
    ).reshape(SLOTS, NC)

    ocean_mid, first_level = pl.pallas_call(
        ocean_kernel,
        in_specs=[smem, smem, hbm] + [vmem] * 11,
        out_specs=[hbm, vmem],
        out_shape=[pltpu.HBM(ocean_state.shape, F32), shape((2, NR, NC))],
        scratch_shapes=[
            pltpu.VMEM((LO // OB, 2, OB, NR, NC), F32),
            pltpu.VMEM((4, 128, NC), F32),
            pltpu.VMEM((4, NR, NC), F32),
            pltpu.SemaphoreType.DMA((2 * (LO // OB),)),
        ],
        compiler_params=params(16),
        cost_estimate=pl.CostEstimate(flops=30000000, bytes_accessed=8000000, transcendentals=0),
        name="ocean",
    )(
        at[1:], kappa, ocean_in, land_mask, kappa, send_prev, send_next, send_south, send_north,
        from_prev, from_next, from_south, from_north, folded,
    )

    take, give = pl.pallas_call(
        receive_map_kernel,
        in_specs=[smem, vmem],
        out_shape=[shape((128, SLOTS), BF16), shape((SLOTS, 128), BF16)],
        compiler_params=params(),
        cost_estimate=pl.CostEstimate(flops=4000000, bytes_accessed=4200000, transcendentals=0),
        name="receive_map",
    )(at, ids)

    new_level, back_out = pl.pallas_call(
        ocean_surface_kernel,
        in_specs=[vmem] * 5,
        out_specs=[vmem, hbm],
        out_shape=[shape((2, NR, NC)), pltpu.HBM((SLOTS, NC), BF16)],
        scratch_shapes=[pltpu.VMEM((SLOTS, NC), BF16), pltpu.SemaphoreType.DMA((PARTS,))],
        compiler_params=params(),
        name="ocean_surface",
    )(incoming, take, give, land_mask, first_level)

    back_in = lax.all_to_all(
        back_out.reshape(TILES, CAP, 2, NC), ("gx", "gy"), split_axis=0, concat_axis=0, tiled=True
    ).reshape(SLOTS, NC)

    atm_next, ocean_next, kept_weights = pl.pallas_call(
        finish_kernel,
        in_specs=[hbm] + [vmem] * 5 + [hbm] * 2,
        out_specs=[hbm, hbm, vmem],
        out_shape=[
            pltpu.HBM(atm_state.shape, F32),
            pltpu.HBM(ocean_state.shape, F32),
            shape((KEPT, TOP, NC, NC), BF16),
        ],
        input_output_aliases={7: 1},
        scratch_shapes=[
            pltpu.VMEM((LEV // FB, 2, FB, NR, NC), F32),
            pltpu.VMEM((LEV // FB, 2, FB, NR, NC), F32),
            pltpu.VMEM((4, 144, NC), F32),
            pltpu.SemaphoreType.DMA((2 * (LEV // FB),)),
            pltpu.SemaphoreType.DMA(()),
            pltpu.SemaphoreType.DMA(()),
        ],
        compiler_params=params(16),
        cost_estimate=pl.CostEstimate(flops=20000000, bytes_accessed=9400000, transcendentals=0),
        name="finish",
    )(pinned(z), from_prev, from_next, from_south, from_north, new_level, weights_in, ocean_mid)

    returned = pl.pallas_call(
        return_kernel,
        in_specs=[vmem, vmem, hbm, vmem],
        out_specs=vmem,
        out_shape=shape((2, NR, NC)),
        scratch_shapes=[
            pltpu.VMEM(((NR - KEPT) // WB, WB, TOP, NC, NC), BF16),
            pltpu.VMEM((512, 512), F32),
            pltpu.VMEM((512, NC), F32),
            pltpu.SemaphoreType.DMA((NR // WB,)),
        ],
        compiler_params=params(16),
        name="returned",
    )(back_in, slot_col, weights_in, kept_weights)
    return atm_next, ocean_next, returned


def solution(mesh):
    placed = (
        P(None, None, "gx", "gy"),
        P(None, None, "gx", "gy"),
        P("gx", "gy"),
        P(),
        P(),
        P(),
        P("gx", "gy", None, None, None),
        P(),
    )
    return jax.shard_map(
        per_device,
        mesh=mesh,
        in_specs=placed,
        out_specs=(P(None, None, "gx", "gy"), P(None, None, "gx", "gy"), P(None, "gx", "gy")),
        check_vma=False,
    )
```

```python
import jax
import jax.numpy as jnp
from jax import lax
from jax.experimental import pallas as pl
from jax.experimental.pallas import tpu as pltpu
from jax.sharding import PartitionSpec as P

F32, BF16 = jnp.float32, jnp.bfloat16
LEV, LO, NR, NC = 72, 60, 64, 128
AT, O1, O2, MK, PAY = 0, 144, 272, 400, 416
OL = 2 * LO
TOP, CAP, TILES = 4, 5, 128
ENT = NR * TOP
SLOTS = TILES * CAP * 2
MIB = 1024 * 1024


def iota(shape, dim):
    return lax.broadcasted_iota(jnp.int32, shape, dim)


def dot(a, b):
    return jnp.dot(a, b, preferred_element_type=F32)


def params(mib=6):
    return pltpu.CompilerParams(vmem_limit_bytes=mib * MIB)


def whole(shape):
    return pl.BlockSpec(shape, lambda *_: (0,) * len(shape))


def mask_rows(first, second):
    place = iota((16, NC), 0)
    return jnp.where(place == 0, first, jnp.where(place == 1, second, 0.0)).astype(BF16)


def element_rows(x_s, mix, b):
    fields = [jnp.swapaxes(x_s[f], 0, 1) for f in range(2)]
    ys = []
    for big in range(2):
        for f in range(2):
            x = jnp.concatenate([fields[f][big * 4 + k] for k in range(4)], 1)
            ys.append(x + dot(mix, x.astype(BF16)))
    y = jnp.concatenate(ys, 0)
    z = y + dot(y.astype(BF16), b)
    pieces = [[], []]
    for r in range(8):
        for f in range(2):
            at = ((r // 4) * 2 + f) * LEV
            pieces[f].append(z[at : at + LEV, (r % 4) * NC : (r % 4 + 1) * NC])
    return pieces


def store_rows(z_ref, pieces, at):
    for f in range(2):
        z_ref[f, :, pl.ds(at, 8), :] = jnp.swapaxes(jnp.stack(pieces[f], 0), 0, 1)


def atm_rim_kernel(
    x_hbm, o_hbm, m_hbm, mix_hbm, elem_hbm, z_ref, sn_ref, sp_ref, b_ref, x_s, o_s, m_s, mix_s, elem_s, sems
):
    sources = (elem_hbm, mix_hbm, x_hbm.at[:, :, pl.ds(0, 8), :], x_hbm.at[:, :, pl.ds(NR - 8, 8), :], m_hbm) + tuple(
        o_hbm.at[:, :, pl.ds(at, 8), :] for at in (0, NR - 8)
    )
    targets = (elem_s, mix_s, x_s.at[0], x_s.at[1], m_s, o_s.at[0], o_s.at[1])
    copies = [pltpu.make_async_copy(a, b, sems.at[k]) for k, (a, b) in enumerate(zip(sources, targets))]
    for copy in copies:
        copy.start()
    copies[0].wait()
    row = iota((512, 16), 0)
    spread_in = (iota((512, 16), 1) == (row // 128) * 4 + row % 4).astype(BF16)
    col = iota((16, 512), 1)
    spread_out = (iota((16, 512), 0) == (col // 128) * 4 + col % 4).astype(BF16)
    elem = (0.5 * elem_s[...]).astype(BF16)
    half = lax.dot_general(spread_in, elem, (((1,), (1,)), ((), ())), preferred_element_type=F32)
    spread = dot(half.astype(BF16), spread_out)
    same = (iota((512, 512), 0) % 128) // 4 == (iota((512, 512), 1) % 128) // 4
    b = jnp.where(same, spread, 0.0).astype(BF16)
    b_ref[...] = b
    copies[1].wait()
    mix = (0.5 * mix_s[...]).astype(BF16)
    for k, ref in ((0, sp_ref), (1, sn_ref)):
        copies[2 + k].wait()
        pieces = element_rows(x_s.at[k], mix, b)
        store_rows(z_ref.at[k], pieces, 0)
        ref[AT:O1, :] = jnp.concatenate([pieces[f][7 * k] for f in range(2)], 0).astype(BF16)
    for k in (4, 5, 6):
        copies[k].wait()
    m = m_s[...].astype(F32)
    for ref, k, first in ((sp_ref, 0, 0), (sn_ref, 1, 6)):
        rows = jnp.swapaxes(o_s[k].reshape(OL, 8, NC), 0, 1)
        at = k * (NR - 8) + first
        for j, base in ((0, O1), (1, O2)):
            u = rows[first + j] * m[at + j : at + j + 1]
            ref[base : base + 128, :] = jnp.concatenate([u, jnp.zeros((8, NC), F32)], 0).astype(BF16)
        ref[MK:PAY, :] = mask_rows(m[at : at + 1], m[at + 1 : at + 2])


INNER = NR // 8 - 2


def pick_columns(columns):
    k, at = iota((8 * len(columns), 8 * NC), 0), iota((8 * len(columns), 8 * NC), 1)
    wanted = jnp.zeros_like(k)
    for j, c in enumerate(columns):
        wanted = jnp.where(k // 8 == j, c, wanted)
    return ((at // NC == k % 8) & (at % NC == wanted)).astype(BF16)


def take_columns(pick, tiles):
    side = jnp.concatenate([t.astype(BF16) for t in tiles], 1)
    got = lax.dot_general(pick, side, (((1,), (1,)), ((), ())), preferred_element_type=F32)
    return jnp.concatenate([got, jnp.zeros_like(got)], 1)


def inner_kernel(
    x_hbm, mix_hbm, o_hbm, b_ref, m_ref, rim_ref, w_hbm, z_hbm, top_ref, zc_ref, oc_ref, w_ref,
    x_s, z_s, o_s, mix_s, sems, rest,
):
    mix_copy = pltpu.make_async_copy(mix_hbm, mix_s, rest.at[0])
    ocean_copy = pltpu.make_async_copy(o_hbm, o_s, rest.at[1])
    rims = [
        pltpu.make_async_copy(
            z_s.at[:, :, pl.ds(at, 8), :], z_hbm.at[:, :, pl.ds(at, 8), :], rest.at[2 + k]
        )
        for k, at in enumerate((0, NR - 8))
    ]

    def chunk(i):
        return pltpu.make_async_copy(x_hbm.at[:, :, pl.ds(i * 8 + 8, 8), :], x_s.at[i], sems.at[i])

    def leave(i):
        rows = pl.ds(pl.multiple_of(i * 8 + 8, 8), 8)
        return pltpu.make_async_copy(z_s.at[:, :, rows, :], z_hbm.at[:, :, rows, :], sems.at[INNER + i])

    mix_copy.start()
    for i in range(INNER):
        chunk(i).start()
    ocean_copy.start()
    weight_copy = pltpu.make_async_copy(w_hbm, w_ref, rest.at[4])
    weight_copy.start()
    for k, copy in enumerate(rims):
        z_s[:, :, k * (NR - 8) : k * (NR - 8) + 8, :] = rim_ref[k]
        copy.start()
    mix_copy.wait()
    mix = (0.5 * mix_s[...]).astype(BF16)

    def step(i, carry):
        chunk(i).wait()
        store_rows(z_s, element_rows(x_s.at[i], mix, b_ref[...]), pl.multiple_of(i * 8 + 8, 8))
        leave(i).start()
        return carry

    lax.fori_loop(0, INNER, step, 0)
    pick = pick_columns((0, NC - 1))

    def atm(i, carry):
        for f in range(2):
            got = take_columns(pick, [z_s[f, i * 8 + l] for l in range(8)])
            at = pl.multiple_of(f * LEV + i * 8, 8)
            for k in range(2):
                zc_ref[k, pl.ds(at, 8), :] = got[k * 8 : k * 8 + 8]
        return carry

    lax.fori_loop(0, LEV // 8, atm, 0, unroll=3)
    for f in range(2):
        top_ref[f] = z_s[f, LEV - 1]
    ocean_copy.wait()
    wet = m_ref[...].astype(F32)
    pick = pick_columns((0, 1, NC - 2, NC - 1))

    def ocean(i, carry):
        tiles = [i * 8 + l for l in range(8)]
        got = take_columns(pick, [wet * o_s[t // LO, t % LO] for t in tiles])
        for k in range(4):
            oc_ref[k, pl.ds(pl.multiple_of(i * 8, 8), 8), :] = got[k * 8 : k * 8 + 8]
        return carry

    lax.fori_loop(0, OL // 8, ocean, 0, unroll=3)
    oc_ref[:, OL:, :] = jnp.zeros((4, 8, NC), F32)
    for i in range(INNER):
        leave(i).wait()
    for copy in rims:
        copy.wait()
    weight_copy.wait()


def cols_kernel(zc_ref, oc_ref, m_ref, rp_ref, rn_ref, ss_ref, sn_ref):
    lane = iota((144, NC), 1)
    place = lane % 4
    rp_at, rn_at = rp_ref[AT:O1, :].astype(F32), rn_ref[AT:O1, :].astype(F32)
    before, after = rp_ref[O2:MK, :].astype(F32), rn_ref[O1:O2, :].astype(F32)
    olane = iota((128, NC), 1)
    row = iota((64, NC), 0)
    m_before, m_after = rp_ref[MK:PAY, :].astype(F32)[1:2], rn_ref[MK:PAY, :].astype(F32)[0:1]
    tail = jnp.where(row == 0, m_before, jnp.where(row == 1, m_after, 0.0))
    m_t = jnp.transpose(jnp.concatenate([m_ref[...].astype(F32), tail], 0))
    for ref, c_at, ocs in ((ss_ref, 0, (0, 1)), (sn_ref, 127, (126, 127))):
        z = zc_ref[0 if c_at == 0 else 1]
        nxt = jnp.where(lane == 63, rn_at[:, c_at : c_at + 1], pltpu.roll(z, 127, 1))
        prv = jnp.where(lane == 0, rp_at[:, c_at : c_at + 1], pltpu.roll(z, 1, 1))
        z = jnp.where(place == 3, (z + nxt) * 0.5, jnp.where(place == 0, (z + prv) * 0.5, z))
        ref[AT:O1, :] = z.astype(BF16)
        for k, c in enumerate(ocs):
            source = c if c < 2 else c - 124
            u = jnp.where(
                olane < 64,
                oc_ref[source],
                jnp.where(olane == 64, before[:, c : c + 1], jnp.where(olane == 65, after[:, c : c + 1], 0.0)),
            )
            base = (O1, O2)[k]
            ref[base : base + 128, :] = u.astype(BF16)
        ref[MK:PAY, :] = mask_rows(m_t[ocs[0] : ocs[0] + 1], m_t[ocs[1] : ocs[1] + 1])


def averaged(z, nxt, prv, place):
    return jnp.where(place == 3, (z + nxt) * 0.5, jnp.where(place == 0, (z + prv) * 0.5, z))


def stiffness(z, h_prev, h_next, c_south, c_north):
    row, lane = iota((NR, NC), 0), iota((NR, NC), 1)
    nxt = jnp.where(row == NR - 1, h_next, pltpu.roll(z, NR - 1, 0))
    prv = jnp.where(row == 0, h_prev, pltpu.roll(z, 1, 0))
    z = averaged(z, nxt, prv, row % 4)
    nxt = jnp.where(lane == NC - 1, c_north, pltpu.roll(z, NC - 1, 1))
    prv = jnp.where(lane == 0, c_south, pltpu.roll(z, 1, 1))
    return averaged(z, nxt, prv, lane % 4)


def surface_kernel(z_ref, rp_ref, rn_ref, cs_ref, cn_ref, s_ref):
    rp, rn = rp_ref[AT:O1, :].astype(F32), rn_ref[AT:O1, :].astype(F32)
    cs, cn = cs_ref[AT:O1, :].astype(F32), cn_ref[AT:O1, :].astype(F32)
    for f in range(2):
        top = f * LEV + LEV - 8
        south = jnp.transpose(cs[top : top + 8])[:NR, 7:8]
        north = jnp.transpose(cn[top : top + 8])[:NR, 7:8]
        last = top + 7
        s = stiffness(z_ref[f], rp[last : last + 1], rn[last : last + 1], south, north)
        s_ref[f] = s.astype(BF16)


def edge_spread(tiles, scale):
    k, c = iota((2 * tiles, tiles * NC), 0), iota((2 * tiles, tiles * NC), 1)
    mine = k % tiles == c // NC
    end = c % NC == jnp.where(k < tiles, 0, NC - 1)
    return jnp.where(mine & end, scale, 0.0).astype(BF16)


def add_ends(x, first, last):
    row = iota((8, NC), 0)
    return jnp.concatenate(
        [
            x[0:8] + jnp.where(row == 0, first, 0.0),
            x[8 : NR - 8],
            x[NR - 8 :] + jnp.where(row == 7, last, 0.0),
        ],
        0,
    )


def column_halo(columns, spread):
    return lax.dot_general(columns, spread, (((0,), (0,)), ((), ())), preferred_element_type=F32)[:NR]


FB = 8
KEPT = 16


def finish_kernel(
    z_hbm, rp_ref, rn_ref, cs_ref, cn_ref, new_ref, w_hbm, mid_hbm, o_hbm, ocean_hbm, w_ref,
    z_s, o_s, h_ref, sems, level_sem, weight_sem,
):
    del mid_hbm
    weight_copy = pltpu.make_async_copy(w_hbm.at[pl.ds(NR - KEPT, KEPT)], w_ref, weight_sem)
    level = pltpu.make_async_copy(new_ref, ocean_hbm.at[:, 0], level_sem)
    level.start()

    def enter(i):
        return pltpu.make_async_copy(z_hbm.at[:, pl.ds(i * FB, FB)], z_s.at[i], sems.at[LEV // FB + i])

    for i in range(LEV // FB):
        enter(i).start()
    weight_copy.start()
    for k, ref in enumerate((rp_ref, rn_ref, cs_ref, cn_ref)):
        h_ref[k] = ref[AT:O1, :].astype(F32)
    spread = edge_spread(2 * FB, 0.5)
    row, lane = iota((NR, NC), 0), iota((NR, NC), 1)

    def weights(place, at, end):
        low = jnp.where((place == 0) & (at != 0), 0.5, 0.0)
        high = jnp.where((place == 3) & (at != end), 0.5, 0.0)
        return jnp.where((place == 0) | (place == 3), 0.5, 1.0), low, high

    own_r, low_r, high_r = weights(row % 4, row, NR - 1)
    own_c, low_c, high_c = weights(lane % 4, lane, NC - 1)

    def chunk(i):
        return pltpu.make_async_copy(o_s.at[i], o_hbm.at[:, pl.ds(i * FB, FB)], sems.at[i])

    def step(i, carry):
        enter(i).wait()

        def halo(k, f):
            return h_ref[k, pl.ds(pl.multiple_of(f * LEV + i * FB, 8), FB), :]

        columns = jnp.concatenate([halo(2, 0), halo(2, 1), halo(3, 0), halo(3, 1)], 0).astype(BF16)
        edges = column_halo(columns, spread)
        for f in range(2):
            first, last = 0.5 * halo(0, f), 0.5 * halo(1, f)
            for l in range(FB):
                t = z_s[i, f, l]
                t = own_r * t + high_r * pltpu.roll(t, NR - 1, 0) + low_r * pltpu.roll(t, 1, 0)
                t = add_ends(t, first[l : l + 1], last[l : l + 1])
                t = own_c * t + high_c * pltpu.roll(t, NC - 1, 1) + low_c * pltpu.roll(t, 1, 1)
                tile = f * FB + l
                o_s[i, f, l] = t + edges[:, tile * NC : (tile + 1) * NC]
        chunk(i).start()
        return carry

    lax.fori_loop(0, LEV // FB, step, 0)
    level.wait()
    weight_copy.wait()
    for i in range(LEV // FB):
        chunk(i).wait()


OB = 12


def ocean_kernel(
    at_ref, k_ref, o_hbm, m_ref, kc_ref, sp_ref, sn_ref, ss_ref, st_ref, rp_ref, rn_ref, cs_ref, cn_ref, fo_ref,
    out_hbm, first_ref, out_s, row_ref, col_ref, sems,
):
    def enter(i):
        return pltpu.make_async_copy(o_hbm.at[:, pl.ds(i * OB, OB)], out_s.at[i], sems.at[LO // OB + i])

    for i in range(LO // OB):
        enter(i).start()
    is_top, is_low = at_ref[0] == 7, at_ref[0] == 0
    lane = iota((128, NC), 1)

    def part(ref, base):
        return ref[base : base + 128, :].astype(F32)

    def masks(ref):
        m = ref[MK:PAY, :].astype(F32)
        return m[0:1], m[1:2]

    fr, fc = iota((NC, NC), 0), iota((NC, NC), 1)
    flip = (((fr < 64) & (fc == 63 - fr)) | ((fr == 64) & (fc == 65)) | ((fr == 65) & (fc == 64))).astype(BF16)
    turned = dot(fo_ref[...], flip)
    n0 = jnp.where(is_top, turned[O2:MK], part(cn_ref, O1))
    n1 = jnp.where(is_top, turned[O1:O2], part(cn_ref, O2))
    mc0, mc1 = masks(cn_ref)
    mn0 = jnp.where(is_top, turned[MK + 1 : MK + 2], mc0)
    mn1 = jnp.where(is_top, turned[MK : MK + 1], mc1)
    keep = jnp.where(is_low, 0.0, 1.0)
    s2, s1 = part(cs_ref, O1) * keep, part(cs_ref, O2) * keep
    ms2, ms1 = masks(cs_ref)
    ms2, ms1 = ms2 * keep, ms1 * keep
    um2, um1 = part(rp_ref, O1), part(rp_ref, O2)
    mm2, mm1 = masks(rp_ref)
    u64, u65 = part(rn_ref, O1), part(rn_ref, O2)
    m64, m65 = masks(rn_ref)
    own0, own63 = part(sp_ref, O1), part(sn_ref, O2)
    mo0, mo63 = masks(sp_ref)[0], masks(sn_ref)[1]
    west0, east127 = part(ss_ref, O1), part(st_ref, O2)
    mw0, me127 = masks(ss_ref)[0], masks(st_ref)[1]
    at, l60 = iota((128, LO), 0), iota((128, LO), 1)
    kap = sum(
        jnp.sum(jnp.where(at - f * LO == l60, kc_ref[f : f + 1, :], 0.0), 1, keepdims=True) for f in range(2)
    )

    def along(u, low, high, end):
        where = lane[: u.shape[0]]
        return jnp.where(where == end, high, pltpu.roll(u, 127, 1)) + jnp.where(
            where == 0, low, pltpu.roll(u, 1, 1)
        )

    def advance(u, wet, inner, outer, m_inner, m_outer, low, high, m_low, m_high, end):
        total = inner + outer + along(u, low, high, end)
        m8 = jnp.broadcast_to(wet, (8, NC))
        count = m_inner + m_outer + along(m8, m_low, m_high, end)[0:1]
        return u + kap * (wet * total - count * u)

    def corner(x, at):
        return x[:, at : at + 1]

    row_ref[0] = um1
    row_ref[1] = u64
    row_ref[2] = advance(
        um1, mm1, own0, um2, mo0, mm2, corner(s1, 64), corner(n0, 64), corner(ms1, 64), corner(mn0, 64), 127
    )
    row_ref[3] = advance(
        u64, m64, own63, u65, mo63, m65, corner(s1, 65), corner(n0, 65), corner(ms1, 65), corner(mn0, 65), 127
    )
    west = advance(
        s1, ms1, west0, s2, mw0, ms2, corner(s1, 64), corner(s1, 65), corner(ms1, 64), corner(ms1, 65), 63
    )
    east = advance(
        n0, mn0, east127, n1, me127, mn1, corner(n0, 64), corner(n0, 65), corner(mn0, 64), corner(mn0, 65), 63
    )
    here = iota((NR, NC), 1)
    for sub, (low, high) in enumerate(((s1, n0), (west, east))):
        low, high = jnp.transpose(low)[:NR], jnp.transpose(high)[:NR]
        for f in range(2):
            col_ref[2 * sub + f] = jnp.where(
                here < 64, pltpu.roll(low, (NC - LO * f) % NC, 1), pltpu.roll(high, (NC + 64 - LO * f) % NC, 1)
            )
    a, b = iota((NC, NC), 0), iota((NC, NC), 1)
    ends = ((a == 0) & (b == 0)) | ((a == 64) & (b == NC - 1))
    ns = jnp.concatenate([(jnp.abs(a - b) == 1).astype(BF16), ends.astype(BF16)], 0)
    wet = m_ref[...].astype(F32)
    r, c = iota((NR, NC), 0), iota((NR, NC), 1)
    m_north = jnp.transpose(jnp.broadcast_to(mn0, (8, NC)))[:NR, 0:1]
    m_south = jnp.transpose(jnp.broadcast_to(ms1, (8, NC)))[:NR, 0:1]
    count = jnp.where(r == NR - 1, m64, pltpu.roll(wet, NR - 1, 0)) + jnp.where(
        r == 0, mm1, pltpu.roll(wet, 1, 0)
    )
    count = count + jnp.where(c == NC - 1, m_north, pltpu.roll(wet, NC - 1, 1))
    count = count + jnp.where(c == 0, m_south, pltpu.roll(wet, 1, 1))

    places = [(f, l) for f in range(2) for l in range(OB)]

    def chunk(i):
        return pltpu.make_async_copy(out_s.at[i], out_hbm.at[:, pl.ds(i * OB, OB)], sems.at[i])

    def step(i, carry):
        enter(i).wait()
        ts = [out_s[i, f, l] for f, l in places]
        for sub in range(2):
            us = [wet * t for t in ts]
            halos = [pltpu.roll(col_ref[2 * sub + f], (NC - i * OB - l) % NC, 1) for f, l in places]
            side = jnp.concatenate([jnp.concatenate(us, 0), jnp.concatenate(halos, 0)], 1)
            cols = dot(side.astype(BF16), ns)
            for j, (f, l) in enumerate(places):
                level = i * OB + l
                here = pl.ds(f * LO + level, 1)
                u = us[j]
                total = pltpu.roll(u, NR - 1, 0) + pltpu.roll(u, 1, 0) + cols[j * NR : (j + 1) * NR]
                total = add_ends(
                    total, row_ref[2 * sub, here, :] - u[NR - 1 :], row_ref[2 * sub + 1, here, :] - u[0:1]
                )
                ts[j] = ts[j] + (k_ref[f, level] * wet) * (total - count * ts[j])
        for j, (f, l) in enumerate(places):
            out_s[i, f, l] = ts[j]
        chunk(i).start()
        return carry

    lax.fori_loop(0, LO // OB, step, 0)
    for f in range(2):
        first_ref[f] = out_s[0, f, 0]
    for i in range(LO // OB):
        chunk(i).wait()


def send_map_kernel(at_ref, ids_ref, pass_hbm, out_ref, scol_ref, through_hbm):
    del pass_hbm, through_hbm
    gx, gy = at_ref[0], at_ref[1]
    block = ids_ref[:, pl.ds(pl.multiple_of((gx // 2) * 128, 128), 128)]
    block = pltpu.roll(block, (gx % 2) * 64, 1)
    rows = iota((32, 128), 0)
    tile_row, lane = iota((128, 128), 0), iota((128, 128), 1)
    before = (tile_row < lane).astype(BF16)
    ones = jnp.ones((128, 128), BF16)
    earlier = jnp.zeros((128, 128), F32)
    tiles, ranks = [], []
    for t in range(TOP):
        ids = jnp.sum(jnp.where(rows == gy * 4 + t, block, 0), 0, keepdims=True)
        hit = (ids // 64 == tile_row) & (lane < 64)
        hot = hit.astype(BF16)
        rank = dot(hot, before) + earlier
        earlier = earlier + dot(hot, ones)
        ranks.append(jnp.sum(jnp.where(hit, rank, 0.0), 0, keepdims=True))
        tiles.append((ids // 64).astype(F32))
    place = iota((8, 128), 0)
    stack = jnp.zeros((8, 128), F32)
    for t in range(TOP):
        stack = jnp.where(place == t, tiles[t], jnp.where(place == t + 4, ranks[t], stack))
    spread = (iota((128, 512), 1) // 8 == iota((128, 512), 0)).astype(BF16)
    wide = dot(stack.astype(BF16), spread)
    col, row8 = iota((8, 512), 1), iota((8, 512), 0)
    wide = jnp.where(row8 % 4 == (col // 2) % 4, wide * jnp.where(row8 < 4, 10.0, 2.0), 0.0)
    slot = jnp.sum(wide, 0, keepdims=True) + (iota((1, 512), 1) % 2).astype(F32)
    out_ref[...] = jnp.where(slot.astype(jnp.int32) == iota((SLOTS, 512), 0), 1.0, 0.0).astype(BF16)
    scol_ref[...] = jnp.transpose(jnp.broadcast_to(slot, (128, 512)))


def receive_map_kernel(at_ref, ids_ref, take_ref, give_ref):
    own_tile = at_ref[0] * 8 + at_ref[1]
    blocks = 8
    row, lane = iota((128, 128), 0), iota((128, 128), 1)
    halves = (row // 64) == (lane // 64)
    before = jnp.concatenate([(halves & (row < lane)).astype(BF16), halves.astype(BF16)], 1)
    r, c = iota((256, 256), 0), iota((256, 256), 1)
    lower = ((r // 4 == c // 4) & (c % 4 < r % 4)).astype(BF16)
    sr, sc = iota((160, 160), 0), iota((160, 160), 1)
    pick = (((sr // 10) % 8 == (sc % 32) // 4) & ((sr % 10) // 2 == sc // 32)).astype(BF16)
    side = iota((160, NC), 0) // 80 == iota((160, NC), 1) // 64
    ids = jnp.concatenate([ids_ref[:, b * NC : (b + 1) * NC] for b in range(blocks)], 0)
    hit = ids // 64 == own_tile
    counts = dot(hit.astype(BF16), before)
    rank = counts[:, 0:NC] + dot(lower, counts[:, NC:].astype(BF16))
    value = (ids % 64 + 1).astype(F32)
    held = [jnp.where(hit & (rank == float(k)), value, 0.0) for k in range(CAP)]
    stacked = jnp.concatenate(
        [jnp.concatenate([h[b * 32 : (b + 1) * 32] for h in held], 0) for b in range(blocks)], 1
    )
    found = dot(pick, stacked.astype(BF16))
    found = jnp.concatenate(
        [jnp.where(side, found[:, b * NC : (b + 1) * NC], 0.0) for b in range(blocks)], 0
    )
    local = dot(found.astype(BF16), jnp.ones((NC, NC), BF16)).astype(jnp.int32)
    row, col = iota((SLOTS, NC), 0), iota((SLOTS, NC), 1)
    give = jnp.where((local - 1 == col % 64) & (row % 2 == col // 64), 1.0, 0.0)
    give_ref[...] = give.astype(BF16)
    for b in range(SLOTS // NC):
        take_ref[:, b * NC : (b + 1) * NC] = jnp.transpose(give[b * NC : (b + 1) * NC]).astype(BF16)


def pack_kernel(c_ref, map_ref, fold_ref, out_ref):
    del fold_ref
    out_ref[...] = dot(map_ref[...], c_ref[...].astype(BF16)).astype(BF16)


def ocean_surface_kernel(in_ref, take_ref, give_ref, m_ref, first_ref, new_ref, back_ref):
    forcing = dot(take_ref[...], in_ref[...])
    wet = 0.25 * m_ref[...].astype(F32)
    news = []
    for f in range(2):
        new = first_ref[f] + wet * forcing[f * NR : (f + 1) * NR]
        new_ref[f] = new
        news.append(new)
    sea = jnp.concatenate(news, 0).astype(BF16)
    back_ref[...] = dot(give_ref[...], sea).astype(BF16)


WB = 8


def return_kernel(in_ref, scol_ref, w_hbm, kept_ref, out_ref, w_s, e_s, p_s, sems):
    def chunk(i):
        return pltpu.make_async_copy(w_hbm.at[pl.ds(i * WB, WB)], w_s.at[i], sems.at[i])

    far = (NR - KEPT) // WB
    for i in range(far):
        chunk(i).start()
    total = jnp.zeros((512, 128), F32)
    slot = scol_ref[...].astype(jnp.int32)
    for b in range(SLOTS // 128):
        hot = jnp.where(slot == iota((512, 128), 1) + b * 128, 1.0, 0.0).astype(BF16)
        total = total + dot(hot, in_ref[b * 128 : (b + 1) * 128, :])
    term = (iota((512, 128), 0) % 8) // 2
    e_s[...] = jnp.concatenate([jnp.where(term == t, total, 0.0) for t in range(TOP)], 1)

    def apply(x, weight):
        rows = pl.ds(pl.multiple_of(x * 8, 8), 8)
        p_s[rows, :] = dot(e_s[rows, :].astype(BF16), weight.reshape(TOP * NC, NC))

    def near_step(i, carry):
        for k in range(WB):
            apply(NR - KEPT + i * WB + k, kept_ref[i * WB + k])
        return carry

    def far_step(i, carry):
        chunk(i).wait()
        for k in range(WB):
            apply(i * WB + k, w_s[i, k])
        return carry

    lax.fori_loop(0, KEPT // WB, near_step, 0)
    lax.fori_loop(0, far, far_step, 0)
    r, c = iota((128, 512), 0), iota((128, 512), 1)
    gather = jnp.where((c // 8 == r % NR) & (c % 2 == r // NR), 1.0, 0.0).astype(BF16)
    parts = p_s[...]
    high = parts.astype(BF16)
    low = (parts - high.astype(F32)).astype(BF16)
    done = dot(jnp.concatenate([gather, gather], 1), jnp.concatenate([high, low], 0))
    for f in range(2):
        out_ref[f] = done[f * NR : (f + 1) * NR]


def shape(dims, dtype=F32):
    return jax.ShapeDtypeStruct(dims, dtype)


def shifted(x, axis, by):
    count = lax.axis_size(axis)
    return lax.ppermute(x, axis, [(i, (i + by) % count) for i in range(count)])


def per_device(atm_state, ocean_state, land_mask, elem_op, column_mix, kappa, remap_weight, intersection):
    gx, gy = lax.axis_index("gx"), lax.axis_index("gy")
    at = jnp.stack([gx, gy]).astype(jnp.int32)
    smem = pl.BlockSpec(memory_space=pltpu.SMEM)
    full = whole((PAY, NC))

    vmem = pl.BlockSpec(memory_space=pltpu.VMEM)
    hbm = pl.BlockSpec(memory_space=pl.ANY)

    def pinned(x):
        return pltpu.with_memory_space_constraint(x, pltpu.HBM)

    atm_in, ocean_in, mask_in = pinned(atm_state), pinned(ocean_state), pinned(land_mask)
    mix_in, elem_in = pinned(column_mix), pinned(elem_op)
    payload = shape((PAY, NC), BF16)
    rim, send_next, send_prev, element = pl.pallas_call(
        atm_rim_kernel,
        in_specs=[hbm] * 5,
        out_specs=[vmem] * 4,
        out_shape=[shape((2, 2, LEV, 8, NC)), payload, payload, shape((512, 512), BF16)],
        scratch_shapes=[
            pltpu.VMEM((2, 2, LEV, 8, NC), F32),
            pltpu.VMEM((2, 2, LO, 8, NC), F32),
            pltpu.VMEM((NR, NC), jnp.int32),
            pltpu.VMEM((LEV, LEV), F32),
            pltpu.VMEM((16, 16), F32),
            pltpu.SemaphoreType.DMA((7,)),
        ],
        compiler_params=params(16),
        name="atm_rim",
    )(atm_in, ocean_in, mask_in, mix_in, elem_in)

    from_prev = shifted(send_next, "gx", 1)
    from_next = shifted(send_prev, "gx", -1)

    weights = remap_weight[:, 0]
    weights_in = pinned(weights)
    z, top_level, z_cols, ocean_cols, near_weights = pl.pallas_call(
        inner_kernel,
        in_specs=[hbm, hbm, hbm, vmem, vmem, vmem, hbm],
        out_specs=[hbm] + [vmem] * 4,
        out_shape=[
            pltpu.HBM(atm_state.shape, F32),
            shape((2, NR, NC)),
            shape((2, 144, NC)),
            shape((4, 128, NC)),
            pltpu.VMEM(weights.shape, BF16),
        ],
        scratch_shapes=[
            pltpu.VMEM((INNER, 2, LEV, 8, NC), F32),
            pltpu.VMEM(atm_state.shape, F32),
            pltpu.VMEM(ocean_state.shape, F32),
            pltpu.VMEM((LEV, LEV), F32),
            pltpu.SemaphoreType.DMA((2 * INNER,)),
            pltpu.SemaphoreType.DMA((5,)),
        ],
        compiler_params=params(14),
        cost_estimate=pl.CostEstimate(flops=1000000000, bytes_accessed=14000000, transcendentals=0),
        name="inner",
    )(atm_in, mix_in, ocean_in, element, land_mask, rim, weights_in)

    send_south, send_north = pl.pallas_call(
        cols_kernel,
        out_shape=[shape((PAY, NC), BF16)] * 2,
        compiler_params=params(),
        name="cols",
    )(z_cols, ocean_cols, land_mask, from_prev, from_next)

    from_south = shifted(send_north, "gy", 1)
    from_north = shifted(send_south, "gy", -1)
    gx_count, gy_count = lax.axis_size("gx"), lax.axis_size("gy")
    top = gy_count - 1
    folded = lax.ppermute(
        send_north, ("gx", "gy"), [(i * gy_count + top, (gx_count - 1 - i) * gy_count + top) for i in range(gx_count)]
    )

    ids = jnp.transpose(intersection, (1, 2, 0)).reshape(32, 1024)
    send_map, slot_col, from_north = pl.pallas_call(
        send_map_kernel,
        in_specs=[smem, vmem, hbm],
        out_specs=[vmem, vmem, hbm],
        out_shape=[shape((SLOTS, 512), BF16), shape((512, 128)), payload],
        input_output_aliases={2: 2},
        compiler_params=params(),
        cost_estimate=pl.CostEstimate(flops=4000000, bytes_accessed=4200000, transcendentals=0),
        name="send_map",
    )(at, ids, from_north)

    surface = pl.pallas_call(
        surface_kernel,
        in_specs=[vmem] * 5,
        out_shape=shape((2, NR, NC), BF16),
        compiler_params=params(),
        name="surface",
    )(top_level, from_prev, from_next, from_south, from_north)

    products = lax.dot_general(
        near_weights, surface, (((3,), (2,)), ((0,), (1,))), preferred_element_type=F32
    )
    contrib = jnp.transpose(products, (0, 1, 3, 2)).reshape(2 * ENT, NC)
    outgoing = pl.pallas_call(
        pack_kernel,
        in_specs=[vmem, vmem, hbm],
        out_shape=shape((SLOTS, NC), BF16),
        compiler_params=params(),
        name="pack",
    )(contrib, send_map, folded)
    incoming = lax.all_to_all(
        outgoing.reshape(TILES, CAP, 2, NC), ("gx", "gy"), split_axis=0, concat_axis=0, tiled=True
    ).reshape(SLOTS, NC)

    ocean_mid, first_level = pl.pallas_call(
        ocean_kernel,
        in_specs=[smem, smem, hbm] + [vmem] * 11,
        out_specs=[hbm, vmem],
        out_shape=[pltpu.HBM(ocean_state.shape, F32), shape((2, NR, NC))],
        scratch_shapes=[
            pltpu.VMEM((LO // OB, 2, OB, NR, NC), F32),
            pltpu.VMEM((4, 128, NC), F32),
            pltpu.VMEM((4, NR, NC), F32),
            pltpu.SemaphoreType.DMA((2 * (LO // OB),)),
        ],
        compiler_params=params(16),
        cost_estimate=pl.CostEstimate(flops=30000000, bytes_accessed=8000000, transcendentals=0),
        name="ocean",
    )(
        at[1:], kappa, ocean_in, land_mask, kappa, send_prev, send_next, send_south, send_north,
        from_prev, from_next, from_south, from_north, folded,
    )

    take, give = pl.pallas_call(
        receive_map_kernel,
        in_specs=[smem, vmem],
        out_shape=[shape((128, SLOTS), BF16), shape((SLOTS, 128), BF16)],
        compiler_params=params(),
        cost_estimate=pl.CostEstimate(flops=4000000, bytes_accessed=4200000, transcendentals=0),
        name="receive_map",
    )(at, ids)

    new_level, back_out = pl.pallas_call(
        ocean_surface_kernel,
        out_shape=[shape((2, NR, NC)), shape((SLOTS, NC), BF16)],
        compiler_params=params(),
        name="ocean_surface",
    )(incoming, take, give, land_mask, first_level)

    back_in = lax.all_to_all(
        back_out.reshape(TILES, CAP, 2, NC), ("gx", "gy"), split_axis=0, concat_axis=0, tiled=True
    ).reshape(SLOTS, NC)

    atm_next, ocean_next, kept_weights = pl.pallas_call(
        finish_kernel,
        in_specs=[hbm] + [vmem] * 5 + [hbm] * 2,
        out_specs=[hbm, hbm, vmem],
        out_shape=[
            pltpu.HBM(atm_state.shape, F32),
            pltpu.HBM(ocean_state.shape, F32),
            shape((KEPT, TOP, NC, NC), BF16),
        ],
        input_output_aliases={7: 1},
        scratch_shapes=[
            pltpu.VMEM((LEV // FB, 2, FB, NR, NC), F32),
            pltpu.VMEM((LEV // FB, 2, FB, NR, NC), F32),
            pltpu.VMEM((4, 144, NC), F32),
            pltpu.SemaphoreType.DMA((2 * (LEV // FB),)),
            pltpu.SemaphoreType.DMA(()),
            pltpu.SemaphoreType.DMA(()),
        ],
        compiler_params=params(16),
        cost_estimate=pl.CostEstimate(flops=20000000, bytes_accessed=9400000, transcendentals=0),
        name="finish",
    )(pinned(z), from_prev, from_next, from_south, from_north, new_level, weights_in, ocean_mid)

    returned = pl.pallas_call(
        return_kernel,
        in_specs=[vmem, vmem, hbm, vmem],
        out_specs=vmem,
        out_shape=shape((2, NR, NC)),
        scratch_shapes=[
            pltpu.VMEM(((NR - KEPT) // WB, WB, TOP, NC, NC), BF16),
            pltpu.VMEM((512, 512), F32),
            pltpu.VMEM((512, NC), F32),
            pltpu.SemaphoreType.DMA((NR // WB,)),
        ],
        compiler_params=params(16),
        name="returned",
    )(back_in, slot_col, weights_in, kept_weights)
    return atm_next, ocean_next, returned


def solution(mesh):
    placed = (
        P(None, None, "gx", "gy"),
        P(None, None, "gx", "gy"),
        P("gx", "gy"),
        P(),
        P(),
        P(),
        P("gx", "gy", None, None, None),
        P(),
    )
    return jax.shard_map(
        per_device,
        mesh=mesh,
        in_specs=placed,
        out_specs=(P(None, None, "gx", "gy"), P(None, None, "gx", "gy"), P(None, "gx", "gy")),
        check_vma=False,
    )
```
